512 devices in a mesh: wide: 128 (over y, z, core), rep: 4 (over x).
Axes of the slice: x: 4, y: 8, z: 8, core: 2. Of those that a mesh axis runs over, the one named last changes fastest.
Arguments:
- node_feats: bfloat16 [131072, 512], P('wide'), may hold values from -6 to 6
- w_self: bfloat16 [512, 512], replicated, may hold values from -0.25 to 0.25
- w_neigh: bfloat16 [512, 512], replicated, may hold values from -0.25 to 0.25
- send_rows: int32 [128, 128, 32], P('wide', None, 'rep'), may hold values from 0 to 1023
- tile_dst: int32 [128, 4, 128], P('wide', 'rep'), may hold values from 0 to 15
- tile_src: int32 [128, 4, 128], P('wide', 'rep'), may hold values from 0 to 31
- tile_bits: int32 [128, 4, 32768], P('wide', 'rep'), may hold values from 0 to 65280
- norm_count: int32 [131072], P('wide'), may hold values from 512 to 2048
- grad_out: bfloat16 [131072, 512], P(('wide', 'rep')), may hold values from -6 to 6
Outputs:
- out_feats: bfloat16 [131072, 512], P(('wide', 'rep'))
- grad_feats: bfloat16 [131072, 512], P(('wide', 'rep'))
- grad_self: bfloat16 [512, 512], replicated
- grad_neigh: bfloat16 [512, 512], replicated
The draws below stay inside these ranges and needn't reach their ends.
All inputs are finite; a program needn't handle non-finite values.
Results may differ from the reference program's by a relative error of at most 0.014.
Values may be sent and summed in bfloat16 or wider, within the bound.
No kernel may reach another device: no remote copies, remote signals or barrier semaphores. Data moves between devices by JAX's collectives and lax.ppermute only.
A program may use at most 64 MiB of HBM per device.

```python
import jax
import jax.numpy as jnp
from jax import lax

F = 512
BLOCK = 64
NODE_DEV = 1024
SLOT_DEV = 8
TILE_DEV = 128
NODES = 131072
SLOTS = 32
SRC_BLK = 32
WORDS = 32768
N_WIDE = 128
N_REP = 4


def place_ends(entries, rng, least, high):
    dims = entries.shape
    spot = [jax.random.randint(jax.random.fold_in(rng, axis), (), 0, dims[axis]) for axis in range(len(dims))]
    entries = entries.at[tuple(spot)].set(least)
    longest = dims.index(max(dims))
    spot[longest] = (spot[longest] + 1) % dims[longest]
    return entries.at[tuple(spot)].set(high)


def shard_levels(own_key, shape, shards, smallest, largest):
    def one(dim, blocks):
        steps = jax.random.uniform(jax.random.fold_in(jax.random.fold_in(own_key, 6), dim), (blocks,), jnp.float32, smallest / len(shards), largest / len(shards))
        return jnp.repeat(jnp.exp(steps), shape[dim] // blocks).reshape((-1,) + (1,) * (len(shape) - dim - 1))

    gain = one(*shards[0])
    for cut in shards[1:]:
        gain = gain * one(*cut)
    return gain


def centred(own_key, dims, scale, limit, split=(), held_as=jnp.bfloat16):
    result = jax.random.normal(own_key, dims, jnp.float32) * scale
    if len(split) > 0:
        result = shard_levels(own_key, dims, split, -0.22, 0.18) * result
    return jnp.clip(result, min=-limit, max=limit).astype(held_as)


def setup_inputs(seed: int = 0) -> dict:
    seeds = jax.random.split(jax.random.key(seed), 10)
    return {
        "node_feats": centred(seeds[0], (NODES, F), 1.0, 6.0, ((0, 128),)),
        "w_self": centred(seeds[1], (F, F), F ** -0.5, 0.25),
        "w_neigh": centred(seeds[2], (F, F), F ** -0.5, 0.25),
        "send_rows": place_ends(jax.random.randint(seeds[3], (N_WIDE, N_WIDE, SLOTS), 0, NODE_DEV), jax.random.fold_in(seeds[3], 1), 0, NODE_DEV - 1).astype(jnp.int32),
        "tile_dst": place_ends(jax.random.randint(seeds[4], (N_WIDE, N_REP, TILE_DEV), 0, NODE_DEV // BLOCK), jax.random.fold_in(seeds[4], 1), 0, (NODE_DEV // BLOCK) - 1).astype(jnp.int32),
        "tile_src": place_ends(jax.random.randint(seeds[5], (N_WIDE, N_REP, TILE_DEV), 0, SRC_BLK), jax.random.fold_in(seeds[5], 1), 0, SRC_BLK - 1).astype(jnp.int32),
        "tile_bits": place_ends(jax.random.randint(seeds[6], (N_WIDE, N_REP, WORDS), 0, 65281), jax.random.fold_in(seeds[6], 1), 0, 65280).astype(jnp.int32),
        "norm_count": place_ends(jax.random.randint(seeds[7], (NODES,), max(1, TILE_DEV * N_REP * BLOCK * BLOCK // (4 * NODE_DEV)), TILE_DEV * N_REP * BLOCK * BLOCK // NODE_DEV + 1), jax.random.fold_in(seeds[7], 1), max(1, TILE_DEV * N_REP * BLOCK * BLOCK // (4 * NODE_DEV)), (TILE_DEV * N_REP * BLOCK * BLOCK // NODE_DEV + 1) - 1).astype(jnp.int32),
        "grad_out": centred(seeds[8], (NODES, F), 1.0, 6.0, ((0, 512),)),
    }


def unpack_bits(packed, tile_count):
    shaped = packed.reshape(tile_count, BLOCK, BLOCK // 16)
    shift_list = jnp.arange(16, dtype=jnp.int32)
    bit_grid = jnp.bitwise_and(jnp.right_shift(shaped[..., None], shift_list), 1)
    return bit_grid.reshape(tile_count, BLOCK, BLOCK).astype(jnp.float32)

def build_table(per_device, send_rows, wide_index, rep_index):
    owners = jnp.arange(N_WIDE, dtype=jnp.int32)[:, None]
    column = jnp.take(send_rows, wide_index, axis=1)
    slot_rows = column[:, rep_index * SLOT_DEV:(rep_index + 1) * SLOT_DEV]
    halo_rows = per_device[owners, slot_rows]
    src_table = jnp.concatenate([per_device[wide_index], halo_rows.reshape(N_WIDE * SLOT_DEV, F)], axis=0)
    targets = (owners * NODE_DEV + slot_rows).reshape(-1)
    return (src_table, targets)

def reference(node_feats, w_self, w_neigh, send_rows, tile_dst, tile_src, tile_bits, norm_count, grad_out):
    per_device = node_feats.reshape(N_WIDE, NODE_DEV, F)
    dst_count = NODE_DEV // BLOCK

    def aggregate(wide_index):
        running = jnp.zeros((dst_count, BLOCK, F), jnp.float32)
        for rep_index in range(N_REP):
            src_table, _ = build_table(per_device, send_rows, wide_index, rep_index)
            blocks = src_table.reshape(SRC_BLK, BLOCK, F).astype(jnp.float32)
            tile_masks = unpack_bits(tile_bits[wide_index, rep_index], TILE_DEV)
            picked = blocks[tile_src[wide_index, rep_index]]
            products = jnp.einsum('tij,tjf->tif', tile_masks, picked, precision=lax.Precision.HIGHEST)
            running = running.at[tile_dst[wide_index, rep_index]].add(products)
        return running.reshape(NODE_DEV, F)
    neigh_sums = lax.map(aggregate, jnp.arange(N_WIDE, dtype=jnp.int32)).reshape(NODES, F)
    row_scale = lax.rsqrt(norm_count.astype(jnp.float32))
    agg_rows = (neigh_sums * row_scale[:, None]).astype(jnp.bfloat16)
    pre_act = jnp.dot(node_feats, w_self, preferred_element_type=jnp.float32) + jnp.dot(agg_rows, w_neigh, preferred_element_type=jnp.float32)
    sigmoid = jax.nn.sigmoid(pre_act)
    out_feats = (pre_act * sigmoid).astype(jnp.bfloat16)
    grad_pre = (grad_out.astype(jnp.float32) * sigmoid * (1.0 + pre_act * (1.0 - sigmoid))).astype(jnp.bfloat16)
    grad_self = jnp.dot(node_feats.T, grad_pre, preferred_element_type=jnp.float32).astype(jnp.bfloat16)
    grad_neigh = jnp.dot(agg_rows.T, grad_pre, preferred_element_type=jnp.float32).astype(jnp.bfloat16)
    grad_agg = (jnp.dot(grad_pre, w_neigh.T, preferred_element_type=jnp.float32) * row_scale[:, None]).astype(jnp.bfloat16)
    agg_blocks = grad_agg.reshape(N_WIDE, dst_count, BLOCK, F)

    def spread(grad_rows, wide_index):
        for rep_index in range(N_REP):
            _, targets = build_table(per_device, send_rows, wide_index, rep_index)
            tile_masks = unpack_bits(tile_bits[wide_index, rep_index], TILE_DEV)
            picked = agg_blocks[wide_index][tile_dst[wide_index, rep_index]].astype(jnp.float32)
            products = jnp.einsum('tij,tif->tjf', tile_masks, picked, precision=lax.Precision.HIGHEST)
            table_grad = jnp.zeros((SRC_BLK, BLOCK, F), jnp.float32).at[tile_src[wide_index, rep_index]].add(products)
            table_grad = table_grad.reshape(SRC_BLK * BLOCK, F)
            own_rows = lax.dynamic_slice_in_dim(grad_rows, wide_index * NODE_DEV, NODE_DEV, 0)
            grad_rows = lax.dynamic_update_slice_in_dim(grad_rows, own_rows + table_grad[:NODE_DEV], wide_index * NODE_DEV, 0)
            rounded = lax.optimization_barrier(table_grad[NODE_DEV:].astype(jnp.bfloat16))
            grad_rows = grad_rows.at[targets].add(rounded.astype(jnp.float32))
        return (grad_rows, None)
    grad_rows, _ = lax.scan(spread, jnp.zeros((NODES, F), jnp.float32), jnp.arange(N_WIDE, dtype=jnp.int32))
    grad_feats = (grad_rows + jnp.dot(grad_pre, w_self.T, preferred_element_type=jnp.float32)).astype(jnp.bfloat16)
    return (out_feats, grad_feats, grad_self, grad_neigh)
```

```python
import jax
import jax.numpy as jnp
from jax import lax
from jax.experimental import pallas as pl
from jax.experimental.pallas import tpu as pltpu
from jax.sharding import PartitionSpec as P

BLOCK = 64
LANES = 128
F32 = jnp.float32
BF16 = jnp.bfloat16


def dot(left, right, left_dim, right_dim):
    dims = (((left_dim,), (right_dim,)), ((), ()))
    return lax.dot_general(left, right, dims, preferred_element_type=F32)


def count_kernel(place_ref, words_ref, counts_ref):
    counts_ref[...] = jnp.zeros_like(counts_ref)
    row = lax.broadcasted_iota(jnp.int32, (BLOCK, LANES), 0)
    lane = lax.broadcasted_iota(jnp.int32, (BLOCK, LANES), 1)
    word_lane = (row % 32) * 4 + (lane % BLOCK) // 16
    shift = lane % 16
    half = lane // BLOCK

    def add_tile(t, carry):
        place = place_ref[t]
        dst = pl.multiple_of((place // 64) * BLOCK, BLOCK)
        src = place % 64
        upper = jnp.broadcast_to(words_ref[pl.ds(2 * t, 1), :], (32, LANES))
        lower = jnp.broadcast_to(words_ref[pl.ds(2 * t + 1, 1), :], (32, LANES))
        words = jnp.concatenate([upper, lower], axis=0)
        picked = jnp.take_along_axis(words, word_lane, axis=1)
        bits = jnp.right_shift(picked, shift) & 1
        tile = jnp.where(half == src % 2, bits, 0).astype(F32).astype(BF16)
        rows = pl.ds(dst, BLOCK)
        cols = pl.ds(pl.multiple_of((src // 2) * LANES, LANES), LANES)
        counts_ref[rows, cols] = counts_ref[rows, cols] + tile
        return carry

    lax.fori_loop(0, place_ref.shape[0], add_tile, 0, unroll=4)


def dense_counts(place, words, rows, cols):
    return pl.pallas_call(
        count_kernel,
        out_shape=jax.ShapeDtypeStruct((rows, cols), BF16),
        in_specs=[
            pl.BlockSpec(memory_space=pltpu.SMEM),
            pl.BlockSpec(memory_space=pltpu.VMEM),
        ],
        out_specs=pl.BlockSpec(memory_space=pltpu.VMEM),
        compiler_params=pltpu.CompilerParams(vmem_limit_bytes=16 << 20),
        cost_estimate=pl.CostEstimate(
            flops=20_000_000, bytes_accessed=rows * cols * 4, transcendentals=0
        ),
        name="dense_counts",
    )(place, words)


def send_to(x, step, replicas):
    return lax.ppermute(x, "rep", [(i, (i + step) % replicas) for i in range(replicas)])


def on_device(
    node_feats, w_self, w_neigh, send_rows, tile_dst, tile_src, tile_bits, norm_count, grad_out
):
    node_rows, feat_width = node_feats.shape
    peer_count = lax.axis_size("wide")
    replicas = lax.axis_size("rep")
    slot_count = send_rows.shape[2]
    tile_total = tile_dst.shape[2]
    quarter = node_rows // replicas
    rep_index = lax.axis_index("rep")
    dst_count = node_rows // BLOCK
    halo_rows = peer_count * slot_count
    first_row = rep_index * quarter
    first_block = rep_index * (quarter // BLOCK)

    def turned(x, axis=0):
        twice = jnp.concatenate([x, x], axis=axis)
        return lax.dynamic_slice_in_dim(twice, first_row, node_rows, axis)

    slot_rows = send_rows[0].reshape(-1)
    every_row = lax.broadcasted_iota(jnp.int32, (node_rows, halo_rows), 0)
    send_pick = (every_row == slot_rows[None, :]).astype(BF16)
    outgoing = dot(send_pick, node_feats, 0, 0).astype(BF16)
    incoming = lax.all_to_all(
        outgoing.reshape(peer_count, slot_count, feat_width), "wide", 0, 0, tiled=True
    ).reshape(halo_rows, feat_width)

    feats = turned(node_feats)
    scale = turned(lax.rsqrt(norm_count.astype(F32)))[:, None]
    grad_out_parts = [grad_out] + [send_to(grad_out, replicas - k, replicas) for k in range(1, replicas)]
    grad_out_all = jnp.concatenate(grad_out_parts, axis=0)
    dst = (tile_dst[0, 0] - first_block) % dst_count
    src = tile_src[0, 0]
    src = jnp.where(src < dst_count, (src - first_block) % dst_count, src)
    counts = dense_counts(
        dst * 64 + src, tile_bits.reshape(tile_total * 2, LANES), node_rows, node_rows + halo_rows
    )
    counts_local = counts[:, :node_rows]
    counts_halo = counts[:, node_rows:]
    sums_local = dot(counts_local, feats, 1, 0)
    pre_self = dot(feats, w_self, 1, 0)

    sums = sums_local + dot(counts_halo, incoming, 1, 0)
    own_sums = sums[:quarter]
    for k in range(1, replicas):
        own_sums = own_sums + send_to(
            sums[k * quarter : (k + 1) * quarter].astype(BF16), k, replicas
        ).astype(F32)
    own_agg = (own_sums * scale[:quarter]).astype(BF16)
    agg = jnp.concatenate(
        [own_agg] + [send_to(own_agg, replicas - k, replicas) for k in range(1, replicas)], axis=0
    )
    pre = pre_self + dot(agg, w_neigh, 1, 0)
    sigmoid = jax.nn.sigmoid(pre)
    out_feats = (pre[:quarter] * sigmoid[:quarter]).astype(BF16)
    grad_pre = (grad_out_all.astype(F32) * sigmoid * (1.0 + pre * (1.0 - sigmoid))).astype(BF16)
    grad_agg = (dot(grad_pre, w_neigh, 1, 1) * scale).astype(BF16)

    halo_grad = dot(counts_halo, grad_agg, 0, 0).astype(BF16)
    returned = lax.all_to_all(
        halo_grad.reshape(peer_count, slot_count, feat_width), "wide", 0, 0, tiled=True
    ).reshape(halo_rows, feat_width)

    share = feat_width // replicas
    share_of = lambda x: lax.dynamic_slice_in_dim(x, rep_index * share, share, 1)
    weight_part = jnp.concatenate(
        [dot(share_of(feats), grad_pre, 0, 0), dot(share_of(agg), grad_pre, 0, 0)], axis=0
    )
    weight_share = lax.psum(weight_part, "wide").astype(BF16)
    weight_all = lax.all_gather(weight_share, "rep", axis=0)
    grad_self = weight_all[:, :share].reshape(feat_width, feat_width)
    grad_neigh = weight_all[:, share:].reshape(feat_width, feat_width)

    grad_local = dot(counts_local, grad_agg, 0, 0)
    turned_slots = (slot_rows - first_row) % node_rows
    return_pick = (every_row == turned_slots[None, :]).astype(BF16)
    block_grad = grad_local + dot(return_pick, returned, 1, 0)
    own_grad = block_grad[:quarter] + dot(grad_pre[:quarter], w_self, 1, 1)
    for k in range(1, replicas):
        own_grad = own_grad + send_to(
            block_grad[k * quarter : (k + 1) * quarter].astype(BF16), k, replicas
        ).astype(F32)
    return out_feats, own_grad.astype(BF16), grad_self, grad_neigh


def solution(mesh):
    in_specs = (
        P("wide", None),
        P(),
        P(),
        P("wide", None, "rep"),
        P("wide", "rep", None),
        P("wide", "rep", None),
        P("wide", "rep", None),
        P("wide"),
        P(("wide", "rep"), None),
    )
    out_specs = (P(("wide", "rep"), None), P(("wide", "rep"), None), P(), P())
    return jax.shard_map(
        on_device, mesh=mesh, in_specs=in_specs, out_specs=out_specs, check_vma=False
    )
```

```python
import jax
import jax.numpy as jnp
from jax import lax
from jax.experimental import pallas as pl
from jax.experimental.pallas import tpu as pltpu
from jax.sharding import Mesh
from jax.sharding import PartitionSpec as P

BLOCK = 64
LANES = 128
WIDE = ("y", "z", "core")
F32 = jnp.float32
BF16 = jnp.bfloat16


def dot(left, right, left_dim, right_dim):
    dims = (((left_dim,), (right_dim,)), ((), ()))
    return lax.dot_general(left, right, dims, preferred_element_type=F32)


def count_kernel(place_ref, words_ref, counts_ref):
    counts_ref[...] = jnp.zeros_like(counts_ref)
    row = lax.broadcasted_iota(jnp.int32, (BLOCK, LANES), 0)
    lane = lax.broadcasted_iota(jnp.int32, (BLOCK, LANES), 1)
    word_lane = (row % 32) * 4 + (lane % BLOCK) // 16
    shift = lane % 16
    half = lane // BLOCK

    def add_tile(t, carry):
        place = place_ref[t]
        dst = pl.multiple_of((place // 64) * BLOCK, BLOCK)
        src = place % 64
        upper = jnp.broadcast_to(words_ref[pl.ds(2 * t, 1), :], (32, LANES))
        lower = jnp.broadcast_to(words_ref[pl.ds(2 * t + 1, 1), :], (32, LANES))
        words = jnp.concatenate([upper, lower], axis=0)
        picked = jnp.take_along_axis(words, word_lane, axis=1)
        bits = jnp.right_shift(picked, shift) & 1
        tile = jnp.where(half == src % 2, bits, 0).astype(F32).astype(BF16)
        rows = pl.ds(dst, BLOCK)
        cols = pl.ds(pl.multiple_of((src // 2) * LANES, LANES), LANES)
        counts_ref[rows, cols] = counts_ref[rows, cols] + tile
        return carry

    lax.fori_loop(0, place_ref.shape[0], add_tile, 0, unroll=4)


def dense_counts(place, words, rows, cols):
    return pl.pallas_call(
        count_kernel,
        out_shape=jax.ShapeDtypeStruct((rows, cols), BF16),
        in_specs=[
            pl.BlockSpec(memory_space=pltpu.SMEM),
            pl.BlockSpec(memory_space=pltpu.VMEM),
        ],
        out_specs=pl.BlockSpec(memory_space=pltpu.VMEM),
        compiler_params=pltpu.CompilerParams(vmem_limit_bytes=16 << 20),
        cost_estimate=pl.CostEstimate(
            flops=20_000_000, bytes_accessed=rows * cols * 4, transcendentals=0
        ),
        name="dense_counts",
    )(place, words)


def send_to(x, step, replicas):
    return lax.ppermute(x, "rep", [(i, (i + step) % replicas) for i in range(replicas)])


def gather_wide(tile, peer_count):
    copies = jnp.broadcast_to(tile, (peer_count,) + tile.shape)
    return lax.all_to_all(copies, WIDE, 0, 0, tiled=True)


def on_device(
    node_feats, w_self, w_neigh, send_rows, tile_dst, tile_src, tile_bits, norm_count, grad_out
):
    node_rows, feat_width = node_feats.shape
    peer_count = lax.axis_size(WIDE)
    replicas = lax.axis_size("rep")
    slot_count = send_rows.shape[2]
    tile_total = tile_dst.shape[2]
    quarter = node_rows // replicas
    rep_index = lax.axis_index("rep")
    dst_count = node_rows // BLOCK
    halo_rows = peer_count * slot_count
    first_row = rep_index * quarter
    first_block = rep_index * (quarter // BLOCK)

    def turned(x, axis=0):
        twice = jnp.concatenate([x, x], axis=axis)
        return lax.dynamic_slice_in_dim(twice, first_row, node_rows, axis)

    slot_rows = send_rows[0].reshape(-1)
    every_row = lax.broadcasted_iota(jnp.int32, (node_rows, halo_rows), 0)
    send_pick = (every_row == slot_rows[None, :]).astype(BF16)
    outgoing = dot(send_pick, node_feats, 0, 0).astype(BF16)
    incoming = lax.all_to_all(
        outgoing.reshape(peer_count, slot_count, feat_width), WIDE, 0, 0, tiled=True
    ).reshape(halo_rows, feat_width)

    feats = turned(node_feats)
    scale = turned(lax.rsqrt(norm_count.astype(F32)))[:, None]
    grad_out_all = turned(lax.all_gather(grad_out, "rep", axis=0, tiled=True))
    dst = (tile_dst[0, 0] - first_block) % dst_count
    src = tile_src[0, 0]
    src = jnp.where(src < dst_count, (src - first_block) % dst_count, src)
    counts = dense_counts(
        dst * 64 + src, tile_bits.reshape(tile_total * 2, LANES), node_rows, node_rows + halo_rows
    )
    counts_local = counts[:, :node_rows]
    counts_halo = counts[:, node_rows:]
    sums_local = dot(counts_local, feats, 1, 0)
    pre_self = dot(feats, w_self, 1, 0)

    sums = sums_local + dot(counts_halo, incoming, 1, 0)
    own_sums = sums[:quarter]
    for k in range(1, replicas):
        own_sums = own_sums + send_to(
            sums[k * quarter : (k + 1) * quarter].astype(BF16), k, replicas
        ).astype(F32)
    own_agg = (own_sums * scale[:quarter]).astype(BF16)
    agg = jnp.concatenate(
        [own_agg] + [send_to(own_agg, replicas - k, replicas) for k in range(1, replicas)], axis=0
    )
    pre = pre_self + dot(agg, w_neigh, 1, 0)
    sigmoid = jax.nn.sigmoid(pre)
    out_feats = (pre[:quarter] * sigmoid[:quarter]).astype(BF16)
    grad_pre = (grad_out_all.astype(F32) * sigmoid * (1.0 + pre * (1.0 - sigmoid))).astype(BF16)
    grad_agg = (dot(grad_pre, w_neigh, 1, 1) * scale).astype(BF16)

    share = feat_width // replicas
    share_of = lambda x: lax.dynamic_slice_in_dim(x, rep_index * share, share, 1)
    weight_part = jnp.concatenate(
        [dot(share_of(feats), grad_pre, 0, 0), dot(share_of(agg), grad_pre, 0, 0)], axis=0
    ).astype(BF16)
    lane_tiles = feat_width // LANES
    weight_tiles = (
        weight_part.reshape(-1, slot_count, lane_tiles, LANES)
        .transpose(0, 2, 1, 3)
        .reshape(peer_count, -1, slot_count, LANES)
        .transpose(0, 2, 1, 3)
        .reshape(peer_count, slot_count, -1)
    )
    halo_grad = dot(counts_halo, grad_agg, 0, 0).astype(BF16)
    returned = lax.all_to_all(
        jnp.concatenate(
            [halo_grad.reshape(peer_count, slot_count, feat_width), weight_tiles], axis=2
        ),
        WIDE,
        0,
        0,
        tiled=True,
    )
    own_tile = returned[:, :, feat_width:].astype(F32).sum(axis=0).astype(BF16)
    returned = returned[:, :, :feat_width].reshape(halo_rows, feat_width)
    all_tiles = gather_wide(own_tile, peer_count)
    weight_share = (
        all_tiles.reshape(peer_count, slot_count, -1, LANES)
        .transpose(0, 2, 1, 3)
        .reshape(-1, lane_tiles, slot_count, LANES)
        .transpose(0, 2, 1, 3)
        .reshape(2 * share, feat_width)
    )
    weight_all = lax.all_gather(weight_share, "rep", axis=0)
    grad_self = weight_all[:, :share].reshape(feat_width, feat_width)
    grad_neigh = weight_all[:, share:].reshape(feat_width, feat_width)

    grad_local = dot(counts_local, grad_agg, 0, 0)
    turned_slots = (slot_rows - first_row) % node_rows
    return_pick = (every_row == turned_slots[None, :]).astype(BF16)
    block_grad = grad_local + dot(return_pick, returned, 1, 0)
    own_grad = block_grad[:quarter] + dot(grad_pre[:quarter], w_self, 1, 1)
    for k in range(1, replicas):
        own_grad = own_grad + send_to(
            block_grad[k * quarter : (k + 1) * quarter].astype(BF16), k, replicas
        ).astype(F32)
    return out_feats, own_grad.astype(BF16), grad_self, grad_neigh


def solution(mesh):
    fine = Mesh(
        mesh.devices.reshape(8, mesh.shape["wide"] // 16, 2, mesh.shape["rep"]), WIDE + ("rep",)
    )
    in_specs = (
        P(WIDE, None),
        P(),
        P(),
        P(WIDE, None, "rep"),
        P(WIDE, "rep", None),
        P(WIDE, "rep", None),
        P(WIDE, "rep", None),
        P(WIDE),
        P(WIDE + ("rep",), None),
    )
    out_specs = (P(WIDE + ("rep",), None), P(WIDE + ("rep",), None), P(), P())
    return jax.shard_map(
        on_device, mesh=fine, in_specs=in_specs, out_specs=out_specs, check_vma=False
    )
```

```python
import jax
import jax.numpy as jnp
from jax import lax
from jax.experimental import pallas as pl
from jax.experimental.pallas import tpu as pltpu
from jax.sharding import Mesh
from jax.sharding import PartitionSpec as P

BLOCK = 64
LANES = 128
WIDE = ("y", "z", "core")
F32 = jnp.float32
BF16 = jnp.bfloat16
VMEM = pl.BlockSpec(memory_space=pltpu.VMEM)
SMEM = pl.BlockSpec(memory_space=pltpu.SMEM)


def dot(left, right, left_dim, right_dim):
    dims = (((left_dim,), (right_dim,)), ((), ()))
    return lax.dot_general(left, right, dims, preferred_element_type=F32)


def call(kernel, name, outs, in_specs, args, flops, scratch=(), vmem=24):
    moved = sum(a.size * a.dtype.itemsize for a in args) + sum(
        o.size * o.dtype.itemsize for o in outs
    )
    return pl.pallas_call(
        kernel,
        out_shape=outs,
        in_specs=in_specs,
        out_specs=[VMEM] * len(outs),
        scratch_shapes=scratch,
        compiler_params=pltpu.CompilerParams(vmem_limit_bytes=vmem << 20),
        cost_estimate=pl.CostEstimate(flops=flops, bytes_accessed=moved, transcendentals=0),
        name=name,
    )(*args)


def shape(rows, cols, dtype):
    return jax.ShapeDtypeStruct((rows, cols), dtype)


def count_kernel(place_ref, words_ref, local_ref, halo_ref, counts_ref):
    counts_ref[...] = jnp.zeros_like(counts_ref)
    row = lax.broadcasted_iota(jnp.int32, (BLOCK, LANES), 0)
    lane = lax.broadcasted_iota(jnp.int32, (BLOCK, LANES), 1)
    word_lane = (row % 32) * 4 + (lane % BLOCK) // 16
    shift = lane % 16
    half = lane // BLOCK

    def add_tile(t, carry):
        place = place_ref[t]
        dst = pl.multiple_of((place // 64) * BLOCK, BLOCK)
        src = place % 64
        upper = jnp.broadcast_to(words_ref[pl.ds(2 * t, 1), :], (32, LANES))
        lower = jnp.broadcast_to(words_ref[pl.ds(2 * t + 1, 1), :], (32, LANES))
        words = jnp.concatenate([upper, lower], axis=0)
        picked = jnp.take_along_axis(words, word_lane, axis=1)
        bits = jnp.right_shift(picked, shift) & 1
        tile = jnp.where(half == src % 2, bits, 0).astype(F32).astype(BF16)
        rows = pl.ds(dst, BLOCK)
        cols = pl.ds(pl.multiple_of((src // 2) * LANES, LANES), LANES)
        counts_ref[rows, cols] = counts_ref[rows, cols] + tile
        return carry

    lax.fori_loop(0, place_ref.shape[0], add_tile, 0, unroll=4)
    split = local_ref.shape[1]
    local_ref[...] = counts_ref[:, :split]
    halo_ref[...] = counts_ref[:, split:]


def sum_kernel(counts_ref, incoming_ref, local_ref, own_ref, *send_refs):
    quarter = own_ref.shape[0]
    for k in (*range(1, 1 + len(send_refs)), 0):
        rows = pl.ds(k * quarter, quarter)
        total = dot(counts_ref[rows, :], incoming_ref[...], 1, 0) + local_ref[rows, :]
        if k:
            send_refs[k - 1][...] = total.astype(BF16)
        else:
            own_ref[...] = total


def dense_kernel(
    rep_ref, agg0, agg1, agg2, agg3, pre_ref, grad_ref, w_self_ref, w_neigh_ref, scale_ref,
    share_ref, halo_t_ref, out_ref, own_ref, grad_agg_ref, joint_ref,
):
    aggs = (agg0, agg1, agg2, agg3)
    quarter, feat_width = agg0.shape
    share = feat_width // len(aggs)
    share_cols = pl.ds(pl.multiple_of(rep_ref[0] * share, LANES), share)
    w_neigh = w_neigh_ref[...]
    grad_self = jnp.zeros((share, feat_width), F32)
    grad_neigh = jnp.zeros((share, feat_width), F32)
    for k, agg_ref in enumerate(aggs):
        rows = pl.ds(k * quarter, quarter)
        pre = pre_ref[rows, :] + dot(agg_ref[...], w_neigh, 1, 0)
        sigmoid = jax.nn.sigmoid(pre)
        grad_pre = (
            grad_ref[rows, :].astype(F32) * sigmoid * (1.0 + pre * (1.0 - sigmoid))
        ).astype(BF16)
        if k == 0:
            out_ref[...] = (pre * sigmoid).astype(BF16)
            own_ref[...] = dot(grad_pre, w_self_ref[...], 1, 1)
        grad_agg_ref[rows, :] = (dot(grad_pre, w_neigh, 1, 1) * scale_ref[rows, :]).astype(BF16)
        grad_self = grad_self + dot(share_ref[rows, :], grad_pre, 0, 0)
        grad_neigh = grad_neigh + dot(agg_ref[:, share_cols], grad_pre, 0, 0)
    tile = 0
    peers = joint_ref.shape[0] // 8
    lanes = joint_ref.shape[1] - feat_width
    per_peer = lanes // LANES
    for part in (grad_self, grad_neigh):
        for g in range(0, share, 8):
            for c in range(0, feat_width, LANES):
                peer, slot = tile // per_peer, tile % per_peer
                joint_ref[peer * 8 : peer * 8 + 8, feat_width + slot * LANES : feat_width + (slot + 1) * LANES] = (
                    part[g : g + 8, c : c + LANES].astype(BF16)
                )
                tile += 1
    halo_rows = halo_t_ref.shape[0]
    step = min(256, halo_rows)
    for at in range(0, halo_rows, step):
        rows = pl.ds(at, step)
        joint_ref[rows, :feat_width] = dot(halo_t_ref[rows, :], grad_agg_ref[...], 1, 0).astype(BF16)


def return_kernel(slots_ref, joint_ref, local_ref, base_ref, tile_ref, own_ref, *send_refs):
    quarter, feat_width = own_ref.shape
    halo_rows = joint_ref.shape[0]
    slots = jnp.broadcast_to(slots_ref[...], (quarter, halo_rows))
    row = lax.broadcasted_iota(jnp.int32, (quarter, halo_rows), 0)
    for k in (*range(1, 1 + len(send_refs)), 0):
        rows = pl.ds(k * quarter, quarter)
        pick = jnp.where(row + k * quarter == slots, 1.0, 0.0).astype(BF16)
        total = dot(pick, joint_ref[:, :feat_width], 1, 0) + local_ref[rows, :]
        if k:
            send_refs[k - 1][...] = total.astype(BF16)
        else:
            own_ref[...] = total + base_ref[...]
    tiles = joint_ref[:, feat_width:].astype(F32)
    tile_ref[...] = tiles.reshape(halo_rows // 8, 8, tiles.shape[1]).sum(axis=0).astype(BF16)


def place_kernel(rep_ref, part0, part1, part2, part3, self_ref, neigh_ref):
    parts = (part0, part1, part2, part3)
    share = part0.shape[0] // 2
    for k, part in enumerate(parts):
        at = pl.ds(pl.multiple_of(((rep_ref[0] + k) % len(parts)) * share, share), share)
        self_ref[at, :] = part[:share, :]
        neigh_ref[at, :] = part[share:, :]


def send_to(x, step, replicas):
    return lax.ppermute(x, "rep", [(i, (i + step) % replicas) for i in range(replicas)])


def from_ahead(x, replicas):
    return [send_to(x, replicas - k, replicas) for k in range(1, replicas)]


def on_device(
    node_feats, w_self, w_neigh, send_rows, tile_dst, tile_src, tile_bits, norm_count, grad_out
):
    node_rows, feat_width = node_feats.shape
    peer_count = lax.axis_size(WIDE)
    replicas = lax.axis_size("rep")
    slot_count = send_rows.shape[2]
    tile_total = tile_dst.shape[2]
    quarter = node_rows // replicas
    share = feat_width // replicas
    rep_index = lax.axis_index("rep")
    rep_ref = rep_index.reshape(1).astype(jnp.int32)
    dst_count = node_rows // BLOCK
    halo_rows = peer_count * slot_count
    first_row = rep_index * quarter
    first_block = rep_index * (quarter // BLOCK)
    send_outs = [shape(quarter, feat_width, BF16)] * (replicas - 1)

    def turned(x, axis=0):
        twice = jnp.concatenate([x, x], axis=axis)
        return lax.dynamic_slice_in_dim(twice, first_row, node_rows, axis)

    slot_rows = send_rows[0].reshape(-1)
    every_row = lax.broadcasted_iota(jnp.int32, (node_rows, halo_rows), 0)
    send_pick = (every_row == slot_rows[None, :]).astype(BF16)
    outgoing = dot(send_pick, node_feats, 0, 0).astype(BF16)
    incoming = lax.all_to_all(outgoing, WIDE, 0, 0, tiled=True)

    feats = turned(node_feats)
    scale = turned(lax.rsqrt(norm_count.astype(F32)))[:, None]
    grad_out_all = jnp.concatenate([grad_out] + from_ahead(grad_out, replicas), axis=0)
    dst = (tile_dst[0, 0] - first_block) % dst_count
    src = tile_src[0, 0]
    src = jnp.where(src < dst_count, (src - first_block) % dst_count, src)
    counts_local, counts_halo = call(
        count_kernel,
        "tile_counts",
        [shape(node_rows, node_rows, BF16), shape(node_rows, halo_rows, BF16)],
        [SMEM, VMEM],
        (dst * 64 + src, tile_bits.reshape(tile_total * 2, LANES)),
        tile_total * BLOCK * LANES * 20,
        scratch=[pltpu.VMEM((node_rows, node_rows + halo_rows), BF16)],
    )
    sums_local = dot(counts_local, feats, 1, 0)
    pre_self = dot(feats, w_self, 1, 0)
    feats_share = lax.dynamic_slice_in_dim(feats, rep_index * share, share, 1)
    turned_slots = ((slot_rows - first_row) % node_rows)[None, :]
    halo_t = counts_halo.T
    (
        incoming, sums_local, pre_self, feats_share, halo_t, counts_local, counts_halo, grad_out_all, scale,
        turned_slots,
    ) = lax.optimization_barrier(
        (
            incoming, sums_local, pre_self, feats_share, halo_t, counts_local, counts_halo, grad_out_all, scale,
            turned_slots,
        )
    )

    block_flops = 2 * node_rows * halo_rows * feat_width
    own_sums, *sends = call(
        sum_kernel,
        "neighbour_sums",
        [shape(quarter, feat_width, F32)] + send_outs,
        [VMEM] * 3,
        (counts_halo, incoming, sums_local),
        block_flops,
    )
    for k in range(1, replicas):
        own_sums = own_sums + send_to(sends[k - 1], k, replicas).astype(F32)
    own_agg = (own_sums * scale[:quarter]).astype(BF16)
    aggs = [own_agg] + from_ahead(own_agg, replicas)
    out_feats, own_base, grad_agg, joint = call(
        dense_kernel,
        "dense",
        [
            shape(quarter, feat_width, BF16),
            shape(quarter, feat_width, F32),
            shape(node_rows, feat_width, BF16),
            shape(halo_rows, feat_width + 2 * share * feat_width // halo_rows, BF16),
        ],
        [SMEM] + [VMEM] * 11,
        (rep_ref, *aggs, pre_self, grad_out_all, w_self, w_neigh, scale, feats_share, halo_t),
        2 * block_flops,
    )
    returned = lax.all_to_all(joint, WIDE, 0, 0, tiled=True)
    grad_local = dot(counts_local, grad_agg, 0, 0)
    returned, grad_local = lax.optimization_barrier((returned, grad_local))

    tile, own_grad, *sends = call(
        return_kernel,
        "returned_rows",
        [shape(slot_count, joint.shape[1] - feat_width, BF16), shape(quarter, feat_width, F32)]
        + send_outs,
        [VMEM] * 4,
        (turned_slots, returned, grad_local, own_base),
        block_flops,
    )
    for k in range(1, replicas):
        own_grad = own_grad + send_to(sends[k - 1], k, replicas).astype(F32)

    copies = jnp.broadcast_to(tile, (peer_count,) + tile.shape)
    tiles = lax.all_to_all(copies, WIDE, 0, 0, tiled=True)
    lane_tiles = feat_width // LANES
    own_share = (
        tiles.reshape(peer_count, slot_count, -1, LANES)
        .transpose(0, 2, 1, 3)
        .reshape(-1, lane_tiles, slot_count, LANES)
        .transpose(0, 2, 1, 3)
        .reshape(2 * share, feat_width)
    )
    grad_self, grad_neigh = call(
        place_kernel,
        "place",
        [shape(feat_width, feat_width, BF16)] * 2,
        [SMEM] + [VMEM] * replicas,
        (rep_ref, own_share, *from_ahead(own_share, replicas)),
        0,
    )
    return out_feats, own_grad.astype(BF16), grad_self, grad_neigh


def solution(mesh):
    fine = Mesh(
        mesh.devices.reshape(8, mesh.shape["wide"] // 16, 2, mesh.shape["rep"]), WIDE + ("rep",)
    )
    in_specs = (
        P(WIDE, None),
        P(),
        P(),
        P(WIDE, None, "rep"),
        P(WIDE, "rep", None),
        P(WIDE, "rep", None),
        P(WIDE, "rep", None),
        P(WIDE),
        P(WIDE + ("rep",), None),
    )
    out_specs = (P(WIDE + ("rep",), None), P(WIDE + ("rep",), None), P(), P())
    return jax.shard_map(
        on_device, mesh=fine, in_specs=in_specs, out_specs=out_specs, check_vma=False
    )
```

```python
import functools

import jax
import jax.numpy as jnp
from jax import lax
from jax.experimental import pallas as pl
from jax.experimental.pallas import tpu as pltpu
from jax.sharding import Mesh
from jax.sharding import PartitionSpec as P

BLOCK = 64
LANES = 128
WIDE = ("y", "z", "core")
F32 = jnp.float32
BF16 = jnp.bfloat16
VMEM = pl.BlockSpec(memory_space=pltpu.VMEM)
HBM = pl.BlockSpec(memory_space=pltpu.HBM)
SMEM = pl.BlockSpec(memory_space=pltpu.SMEM)


def dot(left, right, left_dim, right_dim):
    dims = (((left_dim,), (right_dim,)), ((), ()))
    return lax.dot_general(left, right, dims, preferred_element_type=F32)


def call(kernel, name, outs, in_specs, args, flops, out_specs=None, scratch=(), vmem=24):
    moved = sum(a.size * a.dtype.itemsize for a in args) + sum(
        o.size * o.dtype.itemsize for o in outs
    )
    args = [
        pltpu.with_memory_space_constraint(a, pltpu.HBM) if spec is HBM else a
        for a, spec in zip(args, in_specs, strict=True)
    ]
    out_specs = out_specs or [VMEM] * len(outs)
    outs = [
        pltpu.HBM(o.shape, o.dtype) if spec is HBM else o
        for o, spec in zip(outs, out_specs, strict=True)
    ]
    return pl.pallas_call(
        kernel,
        out_shape=outs,
        in_specs=in_specs,
        out_specs=out_specs,
        scratch_shapes=scratch,
        compiler_params=pltpu.CompilerParams(vmem_limit_bytes=vmem << 20),
        cost_estimate=pl.CostEstimate(flops=flops, bytes_accessed=moved, transcendentals=0),
        name=name,
    )(*args)


def shape(rows, cols, dtype):
    return jax.ShapeDtypeStruct((rows, cols), dtype)


def started(source, target, sem):
    copy = pltpu.make_async_copy(source, target, sem)
    copy.start()
    return copy


def turned_quarters(rep_ref, feats_hbm, feats_ref, sems, replicas):
    quarter = feats_ref.shape[0] // replicas
    copies = []
    for k in range(replicas):
        at = pl.multiple_of(((rep_ref[0] + k) % replicas) * quarter, quarter)
        copies.append(
            started(
                feats_hbm.at[pl.ds(at, quarter), :],
                feats_ref.at[pl.ds(k * quarter, quarter), :],
                sems.at[k],
            )
        )
    return copies


def count_kernel(
    replicas, rep_ref, place_ref, words_ref, feats_hbm, local_hbm, halo_ref, halo_t_hbm, sums_hbm,
    counts_ref, halo_t_ref, feats_ref, sums_ref, sems,
):
    feats_copies = turned_quarters(rep_ref, feats_hbm, feats_ref, sems, replicas)
    counts_ref[...] = jnp.zeros_like(counts_ref)
    row = lax.broadcasted_iota(jnp.int32, (BLOCK, LANES), 0)
    lane = lax.broadcasted_iota(jnp.int32, (BLOCK, LANES), 1)
    word_lane = (row % 32) * 4 + (lane % BLOCK) // 16
    shift = lane % 16
    half = lane // BLOCK

    def add_tile(t, carry):
        place = place_ref[t]
        dst = pl.multiple_of((place // 64) * BLOCK, BLOCK)
        src = place % 64
        upper = jnp.broadcast_to(words_ref[pl.ds(2 * t, 1), :], (32, LANES))
        lower = jnp.broadcast_to(words_ref[pl.ds(2 * t + 1, 1), :], (32, LANES))
        words = jnp.concatenate([upper, lower], axis=0)
        picked = jnp.take_along_axis(words, word_lane, axis=1)
        bits = jnp.right_shift(picked, shift) & 1
        tile = jnp.where(half == src % 2, bits, 0).astype(F32).astype(BF16)
        rows = pl.ds(dst, BLOCK)
        cols = pl.ds(pl.multiple_of((src // 2) * LANES, LANES), LANES)
        counts_ref[rows, cols] = counts_ref[rows, cols] + tile
        return carry

    lax.fori_loop(0, place_ref.shape[0], add_tile, 0, unroll=4)
    split = local_hbm.shape[1]
    local_copy = started(counts_ref.at[:, pl.ds(0, split)], local_hbm, sems.at[replicas])
    halo_ref[...] = counts_ref[:, split:]
    halo_t_ref[...] = counts_ref[:, split:].T
    halo_t_copy = started(halo_t_ref, halo_t_hbm, sems.at[replicas + 1])
    for copy in feats_copies:
        copy.wait()
    rows_done = 256
    for at in range(0, counts_ref.shape[0], rows_done):
        rows = pl.ds(at, rows_done)
        sums_ref[rows, :] = dot(counts_ref[rows, :split], feats_ref[...], 1, 0)
    sums_copy = started(sums_ref, sums_hbm, sems.at[replicas + 2])
    local_copy.wait()
    halo_t_copy.wait()
    sums_copy.wait()


def sum_kernel(counts_ref, incoming_ref, local_hbm, own_ref, send1, send2, send3, local_ref, sems):
    quarter = own_ref.shape[0]
    order = (2, 1, 3, 0)
    quarters = {k: pl.ds(k * quarter, quarter) for k in order}
    copies = {
        k: started(local_hbm.at[rows, :], local_ref.at[rows, :], sems.at[k])
        for k, rows in quarters.items()
    }
    for k, rows in quarters.items():
        total = dot(counts_ref[rows, :], incoming_ref[...], 1, 0)
        copies[k].wait()
        total = total + local_ref[rows, :]
        if k:
            (send1, send2, send3)[k - 1][...] = total.astype(BF16)
        else:
            own_ref[...] = total


def dense_kernel(
    replicas, rep_ref, agg0, agg1, agg2, agg3, grad0, grad1, grad2, grad3, feats_hbm, w_self_hbm,
    w_neigh_hbm, scale_ref, halo_t_hbm, out_ref, grad_pre_ref, grad_agg_hbm, joint_hbm,
    grad_ref, feats_ref, w_self_ref, w_neigh_ref, halo_t_ref, grad_agg_ref, joint_ref, sems,
):
    aggs = (agg0, agg1, agg2, agg3)
    quarter, feat_width = agg0.shape
    share = feat_width // replicas
    halo_rows = halo_t_ref.shape[0]
    step = min(256, halo_rows)
    starts = range(0, halo_rows, step)
    neigh_copy = started(w_neigh_hbm, w_neigh_ref, sems.at[0])
    self_copy = started(w_self_hbm, w_self_ref, sems.at[1])
    feats_copies = turned_quarters(rep_ref, feats_hbm, feats_ref, sems.at[pl.ds(2, replicas)], replicas)
    grad_copies = [
        started(grad, grad_ref.at[pl.ds(k * quarter, quarter), :], sems.at[2 + replicas + k])
        for k, grad in enumerate((grad0, grad1, grad2, grad3))
    ]
    at = 2 + 2 * replicas
    halo_copies = [
        started(halo_t_hbm.at[pl.ds(i, step), :], halo_t_ref.at[pl.ds(i, step), :], sems.at[at + n])
        for n, i in enumerate(starts)
    ]
    at += len(starts)
    share_cols = pl.ds(pl.multiple_of(rep_ref[0] * share, LANES), share)
    grad_self = jnp.zeros((share, feat_width), F32)
    grad_neigh = jnp.zeros((share, feat_width), F32)
    neigh_copy.wait()
    self_copy.wait()
    w_neigh = w_neigh_ref[...]
    for k, agg_ref in enumerate(aggs):
        rows = pl.ds(k * quarter, quarter)
        feats_copies[k].wait()
        pre = dot(agg_ref[...], w_neigh, 1, 0) + dot(feats_ref[rows, :], w_self_ref[...], 1, 0)
        sigmoid = jax.nn.sigmoid(pre)
        grad_copies[k].wait()
        grad_pre = (
            grad_ref[rows, :].astype(F32) * sigmoid * (1.0 + pre * (1.0 - sigmoid))
        ).astype(BF16)
        if k == 0:
            out_ref[...] = (pre * sigmoid).astype(BF16)
            grad_pre_ref[...] = grad_pre
        grad_agg_ref[rows, :] = (dot(grad_pre, w_neigh, 1, 1) * scale_ref[rows, :]).astype(BF16)
        grad_self = grad_self + dot(feats_ref[rows, share_cols], grad_pre, 0, 0)
        grad_neigh = grad_neigh + dot(agg_ref[:, share_cols], grad_pre, 0, 0)
    grad_agg_copy = started(grad_agg_ref, grad_agg_hbm, sems.at[at])
    tile = 0
    per_peer = (joint_ref.shape[1] - feat_width) // LANES
    for part in (grad_self, grad_neigh):
        for g in range(0, share, 8):
            for c in range(0, feat_width, LANES):
                peer, slot = tile // per_peer, tile % per_peer
                lane = feat_width + slot * LANES
                joint_ref[peer * 8 : peer * 8 + 8, lane : lane + LANES] = part[
                    g : g + 8, c : c + LANES
                ].astype(BF16)
                tile += 1
    joint_copies = []
    for n, i in enumerate(starts):
        rows = pl.ds(i, step)
        halo_copies[n].wait()
        joint_ref[rows, :feat_width] = dot(halo_t_ref[rows, :], grad_agg_ref[...], 1, 0).astype(BF16)
        joint_copies.append(started(joint_ref.at[rows, :], joint_hbm.at[rows, :], sems.at[at + 1 + n]))
    grad_agg_copy.wait()
    for copy in joint_copies:
        copy.wait()


def return_kernel(
    replicas, slots_ref, joint_ref, local_hbm, base_hbm, copies_hbm, own_ref, send1, send2, send3,
    tiles_ref, local_ref, base_ref, sems,
):
    quarter, feat_width = own_ref.shape
    halo_rows = joint_ref.shape[0]
    order = (2, 1, 3, 0)
    local_copies = {
        k: started(
            local_hbm.at[pl.ds(k * quarter, quarter), :],
            local_ref.at[pl.ds(k * quarter, quarter), :],
            sems.at[k],
        )
        for k in order
    }
    base_copy = started(base_hbm, base_ref, sems.at[replicas])
    lanes = joint_ref.shape[1] - feat_width
    tiles = joint_ref[:, feat_width:].astype(F32).reshape(halo_rows // 8, 8, lanes)
    tile = tiles.sum(axis=0, keepdims=True)
    tiles_ref[...] = (
        jnp.broadcast_to(tile, tiles.shape).reshape(halo_rows, lanes).astype(BF16)
    )
    copies_copy = started(tiles_ref, copies_hbm, sems.at[replicas + 1])
    slots = jnp.broadcast_to(slots_ref[...], (quarter, halo_rows))
    row = lax.broadcasted_iota(jnp.int32, (quarter, halo_rows), 0)
    for k in order:
        pick = jnp.where(row + k * quarter == slots, 1.0, 0.0).astype(BF16)
        total = dot(pick, joint_ref[:, :feat_width], 1, 0)
        local_copies[k].wait()
        total = total + local_ref[pl.ds(k * quarter, quarter), :]
        if k:
            (send1, send2, send3)[k - 1][...] = total.astype(BF16)
        else:
            base_copy.wait()
            own_ref[...] = total + base_ref[...]
    copies_copy.wait()


def place_kernel(rep_ref, part0, part1, part2, part3, self_ref, neigh_ref):
    parts = (part0, part1, part2, part3)
    share = part0.shape[0] // 2
    for k, part in enumerate(parts):
        at = pl.ds(pl.multiple_of(((rep_ref[0] + k) % len(parts)) * share, share), share)
        self_ref[at, :] = part[:share, :]
        neigh_ref[at, :] = part[share:, :]


def send_to(x, step, replicas):
    return lax.ppermute(x, "rep", [(i, (i + step) % replicas) for i in range(replicas)])


def from_ahead(x, replicas):
    return [send_to(x, replicas - k, replicas) for k in range(1, replicas)]


def on_device(
    node_feats, w_self, w_neigh, send_rows, tile_dst, tile_src, tile_bits, norm_count, grad_out
):
    node_rows, feat_width = node_feats.shape
    peer_count = lax.axis_size(WIDE)
    replicas = lax.axis_size("rep")
    slot_count = send_rows.shape[2]
    tile_total = tile_dst.shape[2]
    quarter = node_rows // replicas
    share = feat_width // replicas
    rep_index = lax.axis_index("rep")
    rep_ref = rep_index.reshape(1).astype(jnp.int32)
    dst_count = node_rows // BLOCK
    halo_rows = peer_count * slot_count
    first_row = rep_index * quarter
    first_block = rep_index * (quarter // BLOCK)
    send_outs = [shape(quarter, feat_width, BF16)] * (replicas - 1)

    slot_rows = send_rows[0].reshape(-1)
    every_row = lax.broadcasted_iota(jnp.int32, (node_rows, halo_rows), 0)
    send_pick = (every_row == slot_rows[None, :]).astype(BF16)
    outgoing = dot(send_pick, node_feats, 0, 0).astype(BF16)
    incoming = lax.all_to_all(outgoing, WIDE, 0, 0, tiled=True)

    scale = lax.rsqrt(norm_count.astype(F32))
    scale = lax.dynamic_slice_in_dim(jnp.concatenate([scale, scale]), first_row, node_rows, 0)
    scale = scale[:, None]
    grad_outs = [grad_out] + from_ahead(grad_out, replicas)
    dst = (tile_dst[0, 0] - first_block) % dst_count
    src = tile_src[0, 0]
    src = jnp.where(src < dst_count, (src - first_block) % dst_count, src)
    block_flops = 2 * node_rows * halo_rows * feat_width
    counts_local, counts_halo, halo_t, sums_local = call(
        functools.partial(count_kernel, replicas),
        "tile_counts",
        [
            shape(node_rows, node_rows, BF16),
            shape(node_rows, halo_rows, BF16),
            shape(halo_rows, node_rows, BF16),
            shape(node_rows, feat_width, F32),
        ],
        [SMEM, SMEM, VMEM, HBM],
        (rep_ref, dst * 64 + src, tile_bits.reshape(tile_total * 2, LANES), node_feats),
        tile_total * BLOCK * LANES * 20 + block_flops,
        out_specs=[HBM, VMEM, HBM, HBM],
        scratch=[
            pltpu.VMEM((node_rows, node_rows + halo_rows), BF16),
            pltpu.VMEM((halo_rows, node_rows), BF16),
            pltpu.VMEM((node_rows, feat_width), BF16),
            pltpu.VMEM((node_rows, feat_width), F32),
            pltpu.SemaphoreType.DMA((replicas + 3,)),
        ],
    )
    turned_slots = ((slot_rows - first_row) % node_rows)[None, :]
    incoming, counts_halo, sums_local, scale, turned_slots, *grad_outs = lax.optimization_barrier(
        (incoming, counts_halo, sums_local, scale, turned_slots, *grad_outs)
    )

    own_sums, *sends = call(
        sum_kernel,
        "neighbour_sums",
        [shape(quarter, feat_width, F32)] + send_outs,
        [VMEM, VMEM, HBM],
        (counts_halo, incoming, sums_local),
        block_flops,
        scratch=[
            pltpu.VMEM((node_rows, feat_width), F32),
            pltpu.SemaphoreType.DMA((replicas,)),
        ],
    )
    for k in range(1, replicas):
        own_sums = own_sums + send_to(sends[k - 1], k, replicas).astype(F32)
    own_agg = (own_sums * scale[:quarter]).astype(BF16)
    aggs = [own_agg] + from_ahead(own_agg, replicas)
    joint_width = feat_width + 2 * share * feat_width // halo_rows
    halo_steps = max(1, halo_rows // 256)
    out_feats, grad_pre, grad_agg, joint = call(
        functools.partial(dense_kernel, replicas),
        "dense",
        [
            shape(quarter, feat_width, BF16),
            shape(quarter, feat_width, BF16),
            shape(node_rows, feat_width, BF16),
            shape(halo_rows, joint_width, BF16),
        ],
        [SMEM] + [VMEM] * 4 + [HBM] * 7 + [VMEM, HBM],
        (rep_ref, *aggs, *grad_outs, node_feats, w_self, w_neigh, scale, halo_t),
        2 * block_flops,
        out_specs=[VMEM, VMEM, HBM, HBM],
        scratch=[
            pltpu.VMEM((node_rows, feat_width), BF16),
            pltpu.VMEM((node_rows, feat_width), BF16),
            pltpu.VMEM((feat_width, feat_width), BF16),
            pltpu.VMEM((feat_width, feat_width), BF16),
            pltpu.VMEM((halo_rows, node_rows), BF16),
            pltpu.VMEM((node_rows, feat_width), BF16),
            pltpu.VMEM((halo_rows, joint_width), BF16),
            pltpu.SemaphoreType.DMA((3 + 2 * replicas + 2 * halo_steps,)),
        ],
    )
    returned = lax.all_to_all(joint, WIDE, 0, 0, tiled=True)
    grad_local = dot(counts_local, grad_agg, 0, 0)
    own_base = dot(grad_pre, w_self, 1, 1)
    returned, grad_local, own_base = lax.optimization_barrier((returned, grad_local, own_base))

    copies, own_grad, *sends = call(
        functools.partial(return_kernel, replicas),
        "returned_rows",
        [shape(halo_rows, joint_width - feat_width, BF16), shape(quarter, feat_width, F32)]
        + send_outs,
        [VMEM, VMEM, HBM, HBM],
        (turned_slots, returned, grad_local, own_base),
        block_flops,
        out_specs=[HBM] + [VMEM] * replicas,
        scratch=[
            pltpu.VMEM((halo_rows, joint_width - feat_width), BF16),
            pltpu.VMEM((node_rows, feat_width), F32),
            pltpu.VMEM((quarter, feat_width), F32),
            pltpu.SemaphoreType.DMA((replicas + 2,)),
        ],
    )
    for k in range(1, replicas):
        own_grad = own_grad + send_to(sends[k - 1], k, replicas).astype(F32)

    tiles = lax.all_to_all(copies, WIDE, 0, 0, tiled=True)
    lane_tiles = feat_width // LANES
    own_share = (
        tiles.reshape(peer_count, slot_count, -1, LANES)
        .transpose(0, 2, 1, 3)
        .reshape(-1, lane_tiles, slot_count, LANES)
        .transpose(0, 2, 1, 3)
        .reshape(2 * share, feat_width)
    )
    grad_self, grad_neigh = call(
        place_kernel,
        "place",
        [shape(feat_width, feat_width, BF16)] * 2,
        [SMEM] + [VMEM] * replicas,
        (rep_ref, own_share, *from_ahead(own_share, replicas)),
        0,
    )
    return out_feats, own_grad.astype(BF16), grad_self, grad_neigh


def solution(mesh):
    fine = Mesh(
        mesh.devices.reshape(8, mesh.shape["wide"] // 16, 2, mesh.shape["rep"]), WIDE + ("rep",)
    )
    in_specs = (
        P(WIDE, None),
        P(),
        P(),
        P(WIDE, None, "rep"),
        P(WIDE, "rep", None),
        P(WIDE, "rep", None),
        P(WIDE, "rep", None),
        P(WIDE),
        P(WIDE + ("rep",), None),
    )
    out_specs = (P(WIDE + ("rep",), None), P(WIDE + ("rep",), None), P(), P())
    return jax.shard_map(
        on_device, mesh=fine, in_specs=in_specs, out_specs=out_specs, check_vma=False
    )
```

```python
import functools

import jax
import jax.numpy as jnp
from jax import lax
from jax.experimental import pallas as pl
from jax.experimental.pallas import tpu as pltpu
from jax.sharding import Mesh
from jax.sharding import PartitionSpec as P

BLOCK = 64
LANES = 128
WIDE = ("y", "z", "core")
F32 = jnp.float32
BF16 = jnp.bfloat16
VMEM = pl.BlockSpec(memory_space=pltpu.VMEM)
HBM = pl.BlockSpec(memory_space=pltpu.HBM)
SMEM = pl.BlockSpec(memory_space=pltpu.SMEM)


def dot(left, right, left_dim, right_dim):
    dims = (((left_dim,), (right_dim,)), ((), ()))
    return lax.dot_general(left, right, dims, preferred_element_type=F32)


def call(kernel, name, outs, in_specs, args, flops, out_specs=None, scratch=(), vmem=24):
    moved = sum(a.size * a.dtype.itemsize for a in args) + sum(
        o.size * o.dtype.itemsize for o in outs
    )
    args = [
        pltpu.with_memory_space_constraint(a, pltpu.HBM) if spec is HBM else a
        for a, spec in zip(args, in_specs, strict=True)
    ]
    out_specs = out_specs or [VMEM] * len(outs)
    outs = [
        pltpu.HBM(o.shape, o.dtype) if spec is HBM else o
        for o, spec in zip(outs, out_specs, strict=True)
    ]
    return pl.pallas_call(
        kernel,
        out_shape=outs,
        in_specs=in_specs,
        out_specs=out_specs,
        scratch_shapes=scratch,
        compiler_params=pltpu.CompilerParams(vmem_limit_bytes=vmem << 20),
        cost_estimate=pl.CostEstimate(flops=flops, bytes_accessed=moved, transcendentals=0),
        name=name,
    )(*args)


def shape(rows, cols, dtype):
    return jax.ShapeDtypeStruct((rows, cols), dtype)


def started(source, target, sem):
    copy = pltpu.make_async_copy(source, target, sem)
    copy.start()
    return copy


def turned_quarters(rep_ref, feats_hbm, feats_ref, sems, replicas):
    quarter = feats_ref.shape[0] // replicas
    copies = []
    for k in range(replicas):
        at = pl.multiple_of(((rep_ref[0] + k) % replicas) * quarter, quarter)
        copies.append(
            started(
                feats_hbm.at[pl.ds(at, quarter), :],
                feats_ref.at[pl.ds(k * quarter, quarter), :],
                sems.at[k],
            )
        )
    return copies


def count_kernel(
    replicas, rep_ref, place_ref, words_ref, feats_hbm, local_t_hbm, halo_ref, halo_t_hbm, sums_hbm,
    counts_ref, turned_ref, feats_ref, sums_ref, sems,
):
    feats_copies = turned_quarters(rep_ref, feats_hbm, feats_ref, sems, replicas)
    counts_ref[...] = jnp.zeros_like(counts_ref)
    row = lax.broadcasted_iota(jnp.int32, (BLOCK, LANES), 0)
    lane = lax.broadcasted_iota(jnp.int32, (BLOCK, LANES), 1)
    word_lane = (row % 32) * 4 + (lane % BLOCK) // 16
    shift = lane % 16
    half = lane // BLOCK

    def add_tile(t, carry):
        place = place_ref[t]
        dst = pl.multiple_of((place // 64) * BLOCK, BLOCK)
        src = place % 64
        upper = jnp.broadcast_to(words_ref[pl.ds(2 * t, 1), :], (32, LANES))
        lower = jnp.broadcast_to(words_ref[pl.ds(2 * t + 1, 1), :], (32, LANES))
        words = jnp.concatenate([upper, lower], axis=0)
        picked = jnp.take_along_axis(words, word_lane, axis=1)
        bits = jnp.right_shift(picked, shift) & 1
        tile = jnp.where(half == src % 2, bits, 0).astype(F32).astype(BF16)
        rows = pl.ds(dst, BLOCK)
        cols = pl.ds(pl.multiple_of((src // 2) * LANES, LANES), LANES)
        counts_ref[rows, cols] = counts_ref[rows, cols] + tile
        return carry

    lax.fori_loop(0, place_ref.shape[0], add_tile, 0, unroll=4)
    split = local_t_hbm.shape[0]
    turned_ref[...] = counts_ref[...].T
    local_copy = started(turned_ref.at[pl.ds(0, split), :], local_t_hbm, sems.at[replicas])
    halo_copy = started(
        turned_ref.at[pl.ds(split, turned_ref.shape[0] - split), :], halo_t_hbm, sems.at[replicas + 1]
    )
    halo_ref[...] = counts_ref[:, split:]
    for copy in feats_copies:
        copy.wait()
    rows_done = 256
    for at in range(0, counts_ref.shape[0], rows_done):
        rows = pl.ds(at, rows_done)
        sums_ref[rows, :] = dot(counts_ref[rows, :split], feats_ref[...], 1, 0)
    sums_copy = started(sums_ref, sums_hbm, sems.at[replicas + 2])
    local_copy.wait()
    halo_copy.wait()
    sums_copy.wait()


def quarter_copies(local_hbm, local_ref, sems, order):
    quarter = local_ref.shape[0] // len(order)
    rows = {k: pl.ds(k * quarter, quarter) for k in order}
    return rows, {
        k: started(local_hbm.at[rows[k], :], local_ref.at[rows[k], :], sems.at[k]) for k in order
    }


def sum_kernel(
    counts_ref, incoming_ref, local_hbm, own_ref, send1, send2, send3, local_ref, total_ref, sems
):
    order = (2, 1, 3, 0)
    quarters, copies = quarter_copies(local_hbm, local_ref, sems, order)
    for rows in quarters.values():
        total_ref[rows, :] = dot(counts_ref[rows, :], incoming_ref[...], 1, 0)
    for k, rows in quarters.items():
        copies[k].wait()
        total = total_ref[rows, :] + local_ref[rows, :]
        if k:
            (send1, send2, send3)[k - 1][...] = total.astype(BF16)
        else:
            own_ref[...] = total


def dense_quarter(agg, feats, grad_out, scale, w_self, w_neigh):
    pre = dot(agg, w_neigh, 1, 0) + dot(feats, w_self, 1, 0)
    sigmoid = jax.nn.sigmoid(pre)
    grad_pre = (grad_out.astype(F32) * sigmoid * (1.0 + pre * (1.0 - sigmoid))).astype(BF16)
    grad_agg = (dot(grad_pre, w_neigh, 1, 1) * scale).astype(BF16)
    return pre * sigmoid, grad_pre, grad_agg


def own_kernel(
    replicas, rep_ref, agg_ref, grad_ref, feats_hbm, w_self_ref, w_neigh_ref, scale_ref,
    out_ref, base_hbm, grad_agg_ref, weights_ref, feats_ref, base_ref, sems,
):
    quarter, feat_width = agg_ref.shape
    share = feat_width // replicas
    own_rows = pl.ds(pl.multiple_of(rep_ref[0] * quarter, quarter), quarter)
    feats_copy = started(feats_hbm.at[own_rows, :], feats_ref, sems.at[0])
    feats_copy.wait()
    out, grad_pre, grad_agg = dense_quarter(
        agg_ref[...], feats_ref[...], grad_ref[...], scale_ref[:quarter, :], w_self_ref[...],
        w_neigh_ref[...],
    )
    out_ref[...] = out.astype(BF16)
    grad_agg_ref[...] = grad_agg
    base_ref[...] = dot(grad_pre, w_self_ref[...], 1, 1)
    base_copy = started(base_ref, base_hbm, sems.at[1])
    share_cols = pl.ds(pl.multiple_of(rep_ref[0] * share, LANES), share)
    weights_ref[:share, :] = dot(feats_ref[:, share_cols], grad_pre, 0, 0)
    weights_ref[share:, :] = dot(agg_ref[:, share_cols], grad_pre, 0, 0)
    base_copy.wait()


def dense_kernel(
    replicas, rep_ref, agg1, agg2, agg3, grad1, grad2, grad3, feats_hbm, w_self_ref, w_neigh_ref,
    scale_ref, halo_t_hbm, own_grad_ref, own_weights_ref, grad_agg_hbm, joint_hbm,
    grad_ref, feats_ref, halo_t_ref, grad_agg_ref, joint_ref, sems,
):
    aggs = {1: agg1, 2: agg2, 3: agg3}
    quarter, feat_width = agg1.shape
    share = feat_width // replicas
    halo_rows = halo_t_ref.shape[0]
    step = min(256, halo_rows)
    starts = range(0, halo_rows, step)
    feats_copies, grad_copies = {}, {}
    for k, grad in zip(aggs, (grad1, grad2, grad3), strict=True):
        at = pl.multiple_of(((rep_ref[0] + k) % replicas) * quarter, quarter)
        feats_copies[k] = started(feats_hbm.at[pl.ds(at, quarter), :], feats_ref.at[k - 1], sems.at[k - 1])
        grad_copies[k] = started(grad, grad_ref.at[k - 1], sems.at[replicas + k - 1])
    at = 2 * replicas
    halo_copies = [
        started(halo_t_hbm.at[pl.ds(i, step), :], halo_t_ref.at[pl.ds(i, step), :], sems.at[at + n])
        for n, i in enumerate(starts)
    ]
    at += len(starts)
    share_cols = pl.ds(pl.multiple_of(rep_ref[0] * share, LANES), share)
    grad_self = own_weights_ref[:share, :]
    grad_neigh = own_weights_ref[share:, :]
    grad_agg_ref[:quarter, :] = own_grad_ref[...]
    for k, agg_ref in aggs.items():
        rows = pl.ds(k * quarter, quarter)
        feats_copies[k].wait()
        grad_copies[k].wait()
        _, grad_pre, grad_agg = dense_quarter(
            agg_ref[...], feats_ref[k - 1], grad_ref[k - 1], scale_ref[rows, :], w_self_ref[...],
            w_neigh_ref[...],
        )
        grad_agg_ref[rows, :] = grad_agg
        grad_self = grad_self + dot(feats_ref[k - 1, :, share_cols], grad_pre, 0, 0)
        grad_neigh = grad_neigh + dot(agg_ref[:, share_cols], grad_pre, 0, 0)
    grad_agg_copy = started(grad_agg_ref, grad_agg_hbm, sems.at[at])
    per_peer = (joint_ref.shape[1] - feat_width) // LANES
    half = feat_width // LANES // 2
    weights = jnp.concatenate([grad_self, grad_neigh], axis=0)
    for core in range(2):
        for n in range(half):
            for g in range(2 * share // 8):
                tile = n * (2 * share // 8) + g
                row = (tile // per_peer * 2 + core) * 8
                lane = feat_width + tile % per_peer * LANES
                col = (core * half + n) * LANES
                joint_ref[row : row + 8, lane : lane + LANES] = weights[
                    g * 8 : g * 8 + 8, col : col + LANES
                ].astype(BF16)
    joint_copies = []
    for n, i in enumerate(starts):
        rows = pl.ds(i, step)
        halo_copies[n].wait()
        joint_ref[rows, :feat_width] = dot(halo_t_ref[rows, :], grad_agg_ref[...], 1, 0).astype(BF16)
        joint_copies.append(started(joint_ref.at[rows, :], joint_hbm.at[rows, :], sems.at[at + 1 + n]))
    grad_agg_copy.wait()
    for copy in joint_copies:
        copy.wait()


def local_kernel(
    replicas, counts_hbm, grad_hbm, base_hbm, local_hbm, counts_ref, grad_ref, base_ref, local_ref, sems
):
    copies = [
        started(*pair, sems.at[n])
        for n, pair in enumerate(
            ((counts_hbm, counts_ref), (grad_hbm, grad_ref), (base_hbm, base_ref))
        )
    ]
    for copy in copies:
        copy.wait()
    quarter = base_ref.shape[0]
    for k in range(replicas):
        rows = pl.ds(k * quarter, quarter)
        total = dot(counts_ref[rows, :], grad_ref[...], 1, 0)
        local_ref[rows, :] = total if k else total + base_ref[...]
    copy = started(local_ref, local_hbm, sems.at[3])
    copy.wait()


def return_kernel(
    replicas, slots_ref, joint_ref, local_hbm, tile_ref, own_ref, send1, send2, send3,
    local_ref, total_ref, sems,
):
    quarter, feat_width = own_ref.shape
    halo_rows = joint_ref.shape[0]
    order = (2, 1, 3, 0)
    quarters, copies = quarter_copies(local_hbm, local_ref, sems, order)
    lanes = joint_ref.shape[1] - feat_width
    tiles = joint_ref[:, feat_width:].astype(F32).reshape(halo_rows // 8, 8, lanes)
    tile = tiles.sum(axis=0, keepdims=True)
    many = tile_ref.shape[0]
    tile_ref[...] = (
        jnp.broadcast_to(tile, (many // 8, 8, lanes)).reshape(many, lanes).astype(BF16)
    )
    slots = jnp.broadcast_to(slots_ref[...], (quarter, halo_rows))
    row = lax.broadcasted_iota(jnp.int32, (quarter, halo_rows), 0)
    for k, rows in quarters.items():
        pick = jnp.where(row + k * quarter == slots, 1.0, 0.0).astype(BF16)
        total_ref[rows, :] = dot(pick, joint_ref[:, :feat_width], 1, 0)
    for k, rows in quarters.items():
        copies[k].wait()
        total = total_ref[rows, :] + local_ref[rows, :]
        if k:
            (send1, send2, send3)[k - 1][...] = total.astype(BF16)
        else:
            own_ref[...] = total


def place_kernel(replicas, parts_ref, self_ref, neigh_ref):
    share = self_ref.shape[0] // replicas
    cores = 2
    block = parts_ref.shape[0] // (cores * replicas)
    for core in range(cores):
        for rep in range(replicas):
            for n in range(block // (2 * share)):
                at = (core * replicas + rep) * block + n * 2 * share
                lane = (core * (block // (2 * share)) + n) * LANES
                rows = slice(rep * share, (rep + 1) * share)
                self_ref[rows, lane : lane + LANES] = parts_ref[at : at + share, :]
                neigh_ref[rows, lane : lane + LANES] = parts_ref[at + share : at + 2 * share, :]


def send_to(x, step, replicas):
    return lax.ppermute(x, "rep", [(i, (i + step) % replicas) for i in range(replicas)])


def from_ahead(x, replicas):
    return [send_to(x, replicas - k, replicas) for k in range(1, replicas)]


def on_device(
    node_feats, w_self, w_neigh, send_rows, tile_dst, tile_src, tile_bits, norm_count, grad_out
):
    node_rows, feat_width = node_feats.shape
    peer_count = lax.axis_size(WIDE)
    replicas = lax.axis_size("rep")
    slot_count = send_rows.shape[2]
    tile_total = tile_dst.shape[2]
    quarter = node_rows // replicas
    share = feat_width // replicas
    rep_index = lax.axis_index("rep")
    rep_ref = rep_index.reshape(1).astype(jnp.int32)
    dst_count = node_rows // BLOCK
    halo_rows = peer_count * slot_count
    first_row = rep_index * quarter
    first_block = rep_index * (quarter // BLOCK)
    send_outs = [shape(quarter, feat_width, BF16)] * (replicas - 1)

    slot_rows = send_rows[0].reshape(-1)
    every_row = lax.broadcasted_iota(jnp.int32, (node_rows, halo_rows), 0)
    send_pick = (every_row == slot_rows[None, :]).astype(BF16)
    outgoing = dot(send_pick, node_feats, 0, 0).astype(BF16)
    incoming = lax.all_to_all(outgoing, WIDE, 0, 0, tiled=True)

    scale = lax.rsqrt(norm_count.astype(F32))
    scale = lax.dynamic_slice_in_dim(jnp.concatenate([scale, scale]), first_row, node_rows, 0)
    scale = scale[:, None]
    grad_outs = [grad_out] + from_ahead(grad_out, replicas)
    dst = (tile_dst[0, 0] - first_block) % dst_count
    src = tile_src[0, 0]
    src = jnp.where(src < dst_count, (src - first_block) % dst_count, src)
    block_flops = 2 * node_rows * halo_rows * feat_width
    local_t, counts_halo, halo_t, sums_local = call(
        functools.partial(count_kernel, replicas),
        "tile_counts",
        [
            shape(node_rows, node_rows, BF16),
            shape(node_rows, halo_rows, BF16),
            shape(halo_rows, node_rows, BF16),
            shape(node_rows, feat_width, F32),
        ],
        [SMEM, SMEM, VMEM, HBM],
        (rep_ref, dst * 64 + src, tile_bits.reshape(tile_total * 2, LANES), node_feats),
        tile_total * BLOCK * LANES * 20 + block_flops,
        out_specs=[HBM, VMEM, HBM, HBM],
        scratch=[
            pltpu.VMEM((node_rows, node_rows + halo_rows), BF16),
            pltpu.VMEM((node_rows + halo_rows, node_rows), BF16),
            pltpu.VMEM((node_rows, feat_width), BF16),
            pltpu.VMEM((node_rows, feat_width), F32),
            pltpu.SemaphoreType.DMA((replicas + 3,)),
        ],
    )
    turned_slots = ((slot_rows - first_row) % node_rows)[None, :]
    incoming, counts_halo, sums_local, scale, turned_slots, *grad_outs = lax.optimization_barrier(
        (incoming, counts_halo, sums_local, scale, turned_slots, *grad_outs)
    )

    own_sums, *sends = call(
        sum_kernel,
        "neighbour_sums",
        [shape(quarter, feat_width, F32)] + send_outs,
        [VMEM, VMEM, HBM],
        (counts_halo, incoming, sums_local),
        block_flops,
        scratch=[pltpu.VMEM((node_rows, feat_width), F32)] * 2
        + [pltpu.SemaphoreType.DMA((replicas,))],
    )
    for k in range(1, replicas):
        own_sums = own_sums + send_to(sends[k - 1], k, replicas).astype(F32)
    own_agg = (own_sums * scale[:quarter]).astype(BF16)
    aggs = from_ahead(own_agg, replicas)
    joint_width = feat_width + 2 * share * feat_width // halo_rows
    halo_steps = max(1, halo_rows // 256)
    out_feats, own_base, own_grad_agg, own_weights = call(
        functools.partial(own_kernel, replicas),
        "dense_own",
        [
            shape(quarter, feat_width, BF16),
            shape(quarter, feat_width, F32),
            shape(quarter, feat_width, BF16),
            shape(2 * share, feat_width, F32),
        ],
        [SMEM, VMEM, VMEM, HBM, VMEM, VMEM, VMEM],
        (rep_ref, own_agg, grad_outs[0], node_feats, w_self, w_neigh, scale),
        block_flops // 2,
        out_specs=[VMEM, HBM, VMEM, VMEM],
        scratch=[
            pltpu.VMEM((quarter, feat_width), BF16),
            pltpu.VMEM((quarter, feat_width), F32),
            pltpu.SemaphoreType.DMA((2,)),
        ],
    )
    grad_agg, joint = call(
        functools.partial(dense_kernel, replicas),
        "dense_rest",
        [shape(node_rows, feat_width, BF16), shape(halo_rows, joint_width, BF16)],
        [SMEM] + [VMEM] * 3 + [HBM] * 4 + [VMEM] * 3 + [HBM, VMEM, VMEM],
        (
            rep_ref, *aggs, *grad_outs[1:], node_feats, w_self, w_neigh, scale, halo_t, own_grad_agg,
            own_weights,
        ),
        2 * block_flops,
        out_specs=[HBM, HBM],
        scratch=[
            pltpu.VMEM((replicas - 1, quarter, feat_width), BF16),
            pltpu.VMEM((replicas - 1, quarter, feat_width), BF16),
            pltpu.VMEM((halo_rows, node_rows), BF16),
            pltpu.VMEM((node_rows, feat_width), BF16),
            pltpu.VMEM((halo_rows, joint_width), BF16),
            pltpu.SemaphoreType.DMA((1 + 2 * replicas + 2 * halo_steps,)),
        ],
    )
    returned = lax.all_to_all(joint, WIDE, 0, 0, tiled=True)
    (local_grad,) = call(
        functools.partial(local_kernel, replicas),
        "local_rows",
        [shape(node_rows, feat_width, F32)],
        [HBM] * 3,
        (local_t, grad_agg, own_base),
        block_flops,
        out_specs=[HBM],
        scratch=[
            pltpu.VMEM((node_rows, node_rows), BF16),
            pltpu.VMEM((node_rows, feat_width), BF16),
            pltpu.VMEM((quarter, feat_width), F32),
            pltpu.VMEM((node_rows, feat_width), F32),
            pltpu.SemaphoreType.DMA((4,)),
        ],
    )

    lanes = joint_width - feat_width
    chips = peer_count // 2
    copies, own_grad, *sends = call(
        functools.partial(return_kernel, replicas),
        "returned_rows",
        [shape(chips * slot_count, lanes, BF16), shape(quarter, feat_width, F32)] + send_outs,
        [VMEM, VMEM, HBM],
        (turned_slots, returned, local_grad),
        block_flops,
        scratch=[pltpu.VMEM((node_rows, feat_width), F32)] * 2
        + [pltpu.SemaphoreType.DMA((replicas,))],
    )
    for k in range(1, replicas):
        own_grad = own_grad + send_to(sends[k - 1], k, replicas).astype(F32)

    tiles = lax.all_to_all(copies, ("y", "z"), 0, 0, tiled=True)
    halves = 2 * replicas
    parts = lax.all_to_all(
        jnp.broadcast_to(tiles, (halves,) + tiles.shape).reshape(-1, lanes), ("core", "rep"), 0, 0, tiled=True
    )
    parts = (
        parts.reshape(halves * chips, slot_count, -1, LANES)
        .transpose(0, 2, 1, 3)
        .reshape(-1, LANES)
    )
    grad_self, grad_neigh = call(
        functools.partial(place_kernel, replicas),
        "place",
        [shape(feat_width, feat_width, BF16)] * 2,
        [VMEM],
        (parts,),
        0,
    )
    return out_feats, own_grad.astype(BF16), grad_self, grad_neigh


def solution(mesh):
    fine = Mesh(
        mesh.devices.reshape(8, mesh.shape["wide"] // 16, 2, mesh.shape["rep"]), WIDE + ("rep",)
    )
    in_specs = (
        P(WIDE, None),
        P(),
        P(),
        P(WIDE, None, "rep"),
        P(WIDE, "rep", None),
        P(WIDE, "rep", None),
        P(WIDE, "rep", None),
        P(WIDE),
        P(WIDE + ("rep",), None),
    )
    out_specs = (P(WIDE + ("rep",), None), P(WIDE + ("rep",), None), P(), P())
    return jax.shard_map(
        on_device, mesh=fine, in_specs=in_specs, out_specs=out_specs, check_vma=False
    )
```

```python
import functools

import jax
import jax.numpy as jnp
from jax import lax
from jax.experimental import pallas as pl
from jax.experimental.pallas import tpu as pltpu
from jax.sharding import Mesh
from jax.sharding import PartitionSpec as P

BLOCK = 64
LANES = 128
WIDE = ("y", "z", "core")
FAR_FIRST = (2, 1, 3)
F32 = jnp.float32
BF16 = jnp.bfloat16
VMEM = pl.BlockSpec(memory_space=pltpu.VMEM)
HBM = pl.BlockSpec(memory_space=pltpu.HBM)
SMEM = pl.BlockSpec(memory_space=pltpu.SMEM)


def dot(left, right, left_dim, right_dim):
    dims = (((left_dim,), (right_dim,)), ((), ()))
    return lax.dot_general(left, right, dims, preferred_element_type=F32)


def call(kernel, name, outs, in_specs, args, flops, out_specs=None, scratch=(), vmem=24):
    moved = sum(a.size * a.dtype.itemsize for a in args) + sum(
        o.size * o.dtype.itemsize for o in outs
    )
    args = [
        pltpu.with_memory_space_constraint(a, pltpu.HBM) if spec is HBM else a
        for a, spec in zip(args, in_specs, strict=True)
    ]
    out_specs = out_specs or [VMEM] * len(outs)
    outs = [
        pltpu.HBM(o.shape, o.dtype) if spec is HBM else o
        for o, spec in zip(outs, out_specs, strict=True)
    ]
    return pl.pallas_call(
        kernel,
        out_shape=outs,
        in_specs=in_specs,
        out_specs=out_specs,
        scratch_shapes=scratch,
        compiler_params=pltpu.CompilerParams(vmem_limit_bytes=vmem << 20),
        cost_estimate=pl.CostEstimate(flops=flops, bytes_accessed=moved, transcendentals=0),
        name=name,
    )(*args)


def shape(rows, cols, dtype):
    return jax.ShapeDtypeStruct((rows, cols), dtype)


def started(source, target, sem):
    copy = pltpu.make_async_copy(source, target, sem)
    copy.start()
    return copy


def turned_quarters(rep_ref, feats_hbm, feats_ref, sems, replicas):
    quarter = feats_ref.shape[0] // replicas
    copies = []
    for k in range(replicas):
        at = pl.multiple_of(((rep_ref[0] + k) % replicas) * quarter, quarter)
        copies.append(
            started(
                feats_hbm.at[pl.ds(at, quarter), :],
                feats_ref.at[pl.ds(k * quarter, quarter), :],
                sems.at[k],
            )
        )
    return copies


def count_kernel(
    replicas, rep_ref, place_ref, words_ref, feats_hbm, local_t_hbm, halo_ref, halo_t_hbm, sums_hbm,
    counts_ref, turned_ref, feats_ref, sums_ref, sems,
):
    feats_copies = turned_quarters(rep_ref, feats_hbm, feats_ref, sems, replicas)
    counts_ref[...] = jnp.zeros_like(counts_ref)
    row = lax.broadcasted_iota(jnp.int32, (BLOCK, LANES), 0)
    lane = lax.broadcasted_iota(jnp.int32, (BLOCK, LANES), 1)
    word_lane = (row % 32) * 4 + (lane % BLOCK) // 16
    shift = lane % 16
    half = lane // BLOCK

    def add_tile(t, carry):
        place = place_ref[t]
        dst = pl.multiple_of((place // 64) * BLOCK, BLOCK)
        src = place % 64
        upper = jnp.broadcast_to(words_ref[pl.ds(2 * t, 1), :], (32, LANES))
        lower = jnp.broadcast_to(words_ref[pl.ds(2 * t + 1, 1), :], (32, LANES))
        words = jnp.concatenate([upper, lower], axis=0)
        picked = jnp.take_along_axis(words, word_lane, axis=1)
        bits = jnp.right_shift(picked, shift) & 1
        tile = jnp.where(half == src % 2, bits, 0).astype(F32).astype(BF16)
        rows = pl.ds(dst, BLOCK)
        cols = pl.ds(pl.multiple_of((src // 2) * LANES, LANES), LANES)
        counts_ref[rows, cols] = counts_ref[rows, cols] + tile
        return carry

    lax.fori_loop(0, place_ref.shape[0], add_tile, 0, unroll=4)
    split = local_t_hbm.shape[0]
    turned_ref[...] = counts_ref[...].T
    local_copy = started(turned_ref.at[pl.ds(0, split), :], local_t_hbm, sems.at[replicas])
    halo_copy = started(
        turned_ref.at[pl.ds(split, turned_ref.shape[0] - split), :], halo_t_hbm, sems.at[replicas + 1]
    )
    halo_ref[...] = counts_ref[:, split:]
    for copy in feats_copies:
        copy.wait()
    rows_done = 256
    for at in range(0, counts_ref.shape[0], rows_done):
        rows = pl.ds(at, rows_done)
        sums_ref[rows, :] = dot(counts_ref[rows, :split], feats_ref[...], 1, 0)
    sums_copy = started(sums_ref, sums_hbm, sems.at[replicas + 2])
    local_copy.wait()
    halo_copy.wait()
    sums_copy.wait()


def quarter_copies(local_hbm, local_ref, sems, order):
    quarter = local_ref.shape[0] // len(order)
    rows = {k: pl.ds(k * quarter, quarter) for k in order}
    return rows, {
        k: started(local_hbm.at[rows[k], :], local_ref.at[rows[k], :], sems.at[k]) for k in order
    }


def gather_kernel(slots_hbm, feats_hbm, rows_hbm, slots_ref, feats_ref, rows_ref, sems):
    slots_copy = started(slots_hbm, slots_ref, sems.at[0])
    feats_copy = started(feats_hbm, feats_ref, sems.at[1])
    slots_copy.wait()
    slot_count, peers = slots_ref.shape
    node_rows = feats_ref.shape[0]
    lane = lax.broadcasted_iota(jnp.int32, (slot_count, node_rows), 1)
    slots = slots_ref[...]
    step = min(32, peers)
    copies = []
    for at in range(0, peers, step):
        pick = jnp.concatenate(
            [
                jnp.where(lane == slots[:, s : s + 1], 1.0, 0.0).astype(F32)
                for s in range(at, at + step)
            ],
            axis=0,
        ).astype(BF16)
        if at == 0:
            feats_copy.wait()
        rows = pl.ds(at * slot_count, step * slot_count)
        rows_ref[rows, :] = dot(pick, feats_ref[...], 1, 0).astype(BF16)
        copies.append(
            started(rows_ref.at[rows, :], rows_hbm.at[rows, :], sems.at[2 + at // step])
        )
    for copy in copies:
        copy.wait()


def sum_kernel(
    counts_ref, incoming_ref, local_hbm, own_ref, send1, send2, send3, local_ref, total_ref, sems
):
    order = (2, 1, 3, 0)
    quarters, copies = quarter_copies(local_hbm, local_ref, sems, order)
    for rows in quarters.values():
        total_ref[rows, :] = dot(counts_ref[rows, :], incoming_ref[...], 1, 0)
    for k, rows in quarters.items():
        copies[k].wait()
        total = total_ref[rows, :] + local_ref[rows, :]
        if k:
            (send1, send2, send3)[k - 1][...] = total.astype(BF16)
        else:
            own_ref[...] = total


def dense_quarter(agg, feats, grad_out, scale, w_self, w_neigh):
    pre = dot(agg, w_neigh, 1, 0) + dot(feats, w_self, 1, 0)
    sigmoid = jax.nn.sigmoid(pre)
    grad_pre = (grad_out.astype(F32) * sigmoid * (1.0 + pre * (1.0 - sigmoid))).astype(BF16)
    grad_agg = (dot(grad_pre, w_neigh, 1, 1) * scale).astype(BF16)
    return pre * sigmoid, grad_pre, grad_agg


def own_kernel(
    replicas, rep_ref, agg_ref, grad_ref, feats_hbm, w_self_ref, w_neigh_ref, scale_ref,
    out_ref, base_hbm, grad_agg_ref, weights_ref, feats_ref, base_ref, sems,
):
    quarter, feat_width = agg_ref.shape
    share = feat_width // replicas
    own_rows = pl.ds(pl.multiple_of(rep_ref[0] * quarter, quarter), quarter)
    feats_copy = started(feats_hbm.at[own_rows, :], feats_ref, sems.at[0])
    feats_copy.wait()
    out, grad_pre, grad_agg = dense_quarter(
        agg_ref[...], feats_ref[...], grad_ref[...], scale_ref[:quarter, :], w_self_ref[...],
        w_neigh_ref[...],
    )
    out_ref[...] = out.astype(BF16)
    grad_agg_ref[...] = grad_agg
    base_ref[...] = dot(grad_pre, w_self_ref[...], 1, 1)
    base_copy = started(base_ref, base_hbm, sems.at[1])
    share_cols = pl.ds(pl.multiple_of(rep_ref[0] * share, LANES), share)
    weights_ref[:share, :] = dot(feats_ref[:, share_cols], grad_pre, 0, 0)
    weights_ref[share:, :] = dot(agg_ref[:, share_cols], grad_pre, 0, 0)
    base_copy.wait()


def dense_kernel(
    replicas, rep_ref, agg1, agg3, agg2, grad1, grad2, grad3, feats_hbm, w_self_ref, w_neigh_ref,
    scale_ref, halo_t_hbm, own_grad_ref, own_weights_ref, grad_agg_hbm, joint_hbm,
    grad_ref, feats_ref, halo_t_ref, grad_agg_ref, joint_ref, sems,
):
    aggs = {1: agg1, 2: agg2, 3: agg3}
    quarter, feat_width = agg1.shape
    share = feat_width // replicas
    halo_rows = halo_t_ref.shape[0]
    step = min(256, halo_rows)
    starts = range(0, halo_rows, step)
    feats_copies, grad_copies = {}, {}
    for k, grad in zip(aggs, (grad1, grad2, grad3), strict=True):
        at = pl.multiple_of(((rep_ref[0] + k) % replicas) * quarter, quarter)
        feats_copies[k] = started(feats_hbm.at[pl.ds(at, quarter), :], feats_ref.at[k - 1], sems.at[k - 1])
        grad_copies[k] = started(grad, grad_ref.at[k - 1], sems.at[replicas + k - 1])
    at = 2 * replicas
    halo_copies = [
        started(halo_t_hbm.at[pl.ds(i, step), :], halo_t_ref.at[pl.ds(i, step), :], sems.at[at + n])
        for n, i in enumerate(starts)
    ]
    at += len(starts)
    share_cols = pl.ds(pl.multiple_of(rep_ref[0] * share, LANES), share)
    grad_self = own_weights_ref[:share, :]
    grad_neigh = own_weights_ref[share:, :]
    grad_agg_ref[:quarter, :] = own_grad_ref[...]
    for k, agg_ref in aggs.items():
        rows = pl.ds(k * quarter, quarter)
        feats_copies[k].wait()
        grad_copies[k].wait()
        _, grad_pre, grad_agg = dense_quarter(
            agg_ref[...], feats_ref[k - 1], grad_ref[k - 1], scale_ref[rows, :], w_self_ref[...],
            w_neigh_ref[...],
        )
        grad_agg_ref[rows, :] = grad_agg
        grad_self = grad_self + dot(feats_ref[k - 1, :, share_cols], grad_pre, 0, 0)
        grad_neigh = grad_neigh + dot(agg_ref[:, share_cols], grad_pre, 0, 0)
    grad_agg_copy = started(grad_agg_ref, grad_agg_hbm, sems.at[at])
    tile = 0
    per_peer = (joint_ref.shape[1] - feat_width) // LANES
    for part in (grad_self, grad_neigh):
        for g in range(0, share, 8):
            for c in range(0, feat_width, LANES):
                peer, slot = tile // per_peer, tile % per_peer
                lane = feat_width + slot * LANES
                joint_ref[peer * 8 : peer * 8 + 8, lane : lane + LANES] = part[
                    g : g + 8, c : c + LANES
                ].astype(BF16)
                tile += 1
    joint_copies = []
    for n, i in enumerate(starts):
        rows = pl.ds(i, step)
        halo_copies[n].wait()
        joint_ref[rows, :feat_width] = dot(halo_t_ref[rows, :], grad_agg_ref[...], 1, 0).astype(BF16)
        joint_copies.append(started(joint_ref.at[rows, :], joint_hbm.at[rows, :], sems.at[at + 1 + n]))
    grad_agg_copy.wait()
    for copy in joint_copies:
        copy.wait()


def local_kernel(
    replicas, counts_hbm, grad_hbm, base_hbm, local_hbm, counts_ref, grad_ref, base_ref, local_ref, sems
):
    copies = [
        started(*pair, sems.at[n])
        for n, pair in enumerate(
            ((counts_hbm, counts_ref), (grad_hbm, grad_ref), (base_hbm, base_ref))
        )
    ]
    for copy in copies:
        copy.wait()
    quarter = base_ref.shape[0]
    for k in range(replicas):
        rows = pl.ds(k * quarter, quarter)
        total = dot(counts_ref[rows, :], grad_ref[...], 1, 0)
        local_ref[rows, :] = total if k else total + base_ref[...]
    copy = started(local_ref, local_hbm, sems.at[3])
    copy.wait()


def return_kernel(
    replicas, slots_ref, joint_ref, local_hbm, copies_hbm, own_ref, send1, send2, send3,
    tiles_ref, local_ref, total_ref, sems,
):
    quarter, feat_width = own_ref.shape
    halo_rows = joint_ref.shape[0]
    order = (2, 1, 3, 0)
    quarters, copies = quarter_copies(local_hbm, local_ref, sems, order)
    lanes = joint_ref.shape[1] - feat_width
    tiles = joint_ref[:, feat_width:].astype(F32).reshape(halo_rows // 8, 8, lanes)
    tile = tiles.sum(axis=0, keepdims=True)
    tiles_ref[...] = jnp.broadcast_to(tile, tiles.shape).reshape(halo_rows, lanes).astype(BF16)
    copies_copy = started(tiles_ref, copies_hbm, sems.at[replicas])
    slots = jnp.broadcast_to(slots_ref[...], (quarter, halo_rows))
    row = lax.broadcasted_iota(jnp.int32, (quarter, halo_rows), 0)
    for k, rows in quarters.items():
        pick = jnp.where(row + k * quarter == slots, 1.0, 0.0).astype(BF16)
        total_ref[rows, :] = dot(pick, joint_ref[:, :feat_width], 1, 0)
    for k, rows in quarters.items():
        copies[k].wait()
        total = total_ref[rows, :] + local_ref[rows, :]
        if k:
            (send1, send2, send3)[k - 1][...] = total.astype(BF16)
        else:
            own_ref[...] = total
    copies_copy.wait()


def place_kernel(rep_ref, part0, part1, part3, part2, self_ref, neigh_ref):
    parts = (part0, part1, part2, part3)
    share = part0.shape[0] // 2
    for k, part in enumerate(parts):
        at = pl.ds(pl.multiple_of(((rep_ref[0] + k) % len(parts)) * share, share), share)
        self_ref[at, :] = part[:share, :]
        neigh_ref[at, :] = part[share:, :]


def send_to(x, step, replicas):
    return lax.ppermute(x, "rep", [(i, (i + step) % replicas) for i in range(replicas)])


def from_ahead(x, replicas):
    ahead = {k: send_to(x, replicas - k, replicas) for k in reversed(FAR_FIRST)}
    return [ahead[k] for k in range(1, replicas)]


def on_device(
    node_feats, w_self, w_neigh, send_rows, tile_dst, tile_src, tile_bits, norm_count, grad_out
):
    node_rows, feat_width = node_feats.shape
    peer_count = lax.axis_size(WIDE)
    replicas = lax.axis_size("rep")
    slot_count = send_rows.shape[2]
    tile_total = tile_dst.shape[2]
    quarter = node_rows // replicas
    share = feat_width // replicas
    rep_index = lax.axis_index("rep")
    rep_ref = rep_index.reshape(1).astype(jnp.int32)
    dst_count = node_rows // BLOCK
    halo_rows = peer_count * slot_count
    first_row = rep_index * quarter
    first_block = rep_index * (quarter // BLOCK)
    send_outs = [shape(quarter, feat_width, BF16)] * (replicas - 1)

    slot_rows = send_rows[0].reshape(-1)
    (outgoing,) = call(
        gather_kernel,
        "gather_rows",
        [shape(halo_rows, feat_width, BF16)],
        [HBM, HBM],
        (send_rows[0].T, node_feats),
        2 * node_rows * halo_rows * feat_width,
        out_specs=[HBM],
        scratch=[
            pltpu.VMEM((slot_count, peer_count), jnp.int32),
            pltpu.VMEM((node_rows, feat_width), BF16),
            pltpu.VMEM((halo_rows, feat_width), BF16),
            pltpu.SemaphoreType.DMA((2 + max(1, peer_count // 32),)),
        ],
    )
    incoming = lax.all_to_all(outgoing, WIDE, 0, 0, tiled=True)

    scale = lax.rsqrt(norm_count.astype(F32))
    scale = lax.dynamic_slice_in_dim(jnp.concatenate([scale, scale]), first_row, node_rows, 0)
    scale = scale[:, None]
    grad_outs = [grad_out] + from_ahead(grad_out, replicas)
    dst = (tile_dst[0, 0] - first_block) % dst_count
    src = tile_src[0, 0]
    src = jnp.where(src < dst_count, (src - first_block) % dst_count, src)
    block_flops = 2 * node_rows * halo_rows * feat_width
    local_t, counts_halo, halo_t, sums_local = call(
        functools.partial(count_kernel, replicas),
        "tile_counts",
        [
            shape(node_rows, node_rows, BF16),
            shape(node_rows, halo_rows, BF16),
            shape(halo_rows, node_rows, BF16),
            shape(node_rows, feat_width, F32),
        ],
        [SMEM, SMEM, VMEM, HBM],
        (rep_ref, dst * 64 + src, tile_bits.reshape(tile_total * 2, LANES), node_feats),
        tile_total * BLOCK * LANES * 20 + block_flops,
        out_specs=[HBM, VMEM, HBM, HBM],
        scratch=[
            pltpu.VMEM((node_rows, node_rows + halo_rows), BF16),
            pltpu.VMEM((node_rows + halo_rows, node_rows), BF16),
            pltpu.VMEM((node_rows, feat_width), BF16),
            pltpu.VMEM((node_rows, feat_width), F32),
            pltpu.SemaphoreType.DMA((replicas + 3,)),
        ],
    )
    turned_slots = ((slot_rows - first_row) % node_rows)[None, :]
    incoming, counts_halo, sums_local, scale, turned_slots, *grad_outs = lax.optimization_barrier(
        (incoming, counts_halo, sums_local, scale, turned_slots, *grad_outs)
    )

    own_sums, *sends = call(
        sum_kernel,
        "neighbour_sums",
        [shape(quarter, feat_width, F32)] + send_outs,
        [VMEM, VMEM, HBM],
        (counts_halo, incoming, sums_local),
        block_flops,
        scratch=[pltpu.VMEM((node_rows, feat_width), F32)] * 2
        + [pltpu.SemaphoreType.DMA((replicas,))],
    )
    for k in FAR_FIRST:
        own_sums = own_sums + send_to(sends[k - 1], k, replicas).astype(F32)
    own_agg = (own_sums * scale[:quarter]).astype(BF16)
    aggs = from_ahead(own_agg, replicas)
    joint_width = feat_width + 2 * share * feat_width // halo_rows
    halo_steps = max(1, halo_rows // 256)
    out_feats, own_base, own_grad_agg, own_weights = call(
        functools.partial(own_kernel, replicas),
        "dense_own",
        [
            shape(quarter, feat_width, BF16),
            shape(quarter, feat_width, F32),
            shape(quarter, feat_width, BF16),
            shape(2 * share, feat_width, F32),
        ],
        [SMEM, VMEM, VMEM, HBM, VMEM, VMEM, VMEM],
        (rep_ref, own_agg, grad_outs[0], node_feats, w_self, w_neigh, scale),
        block_flops // 2,
        out_specs=[VMEM, HBM, VMEM, VMEM],
        scratch=[
            pltpu.VMEM((quarter, feat_width), BF16),
            pltpu.VMEM((quarter, feat_width), F32),
            pltpu.SemaphoreType.DMA((2,)),
        ],
    )
    grad_agg, joint = call(
        functools.partial(dense_kernel, replicas),
        "dense_rest",
        [shape(node_rows, feat_width, BF16), shape(halo_rows, joint_width, BF16)],
        [SMEM] + [VMEM] * 3 + [HBM] * 4 + [VMEM] * 3 + [HBM, VMEM, VMEM],
        (
            rep_ref, aggs[0], aggs[2], aggs[1], *grad_outs[1:], node_feats, w_self, w_neigh, scale, halo_t, own_grad_agg,
            own_weights,
        ),
        2 * block_flops,
        out_specs=[HBM, HBM],
        scratch=[
            pltpu.VMEM((replicas - 1, quarter, feat_width), BF16),
            pltpu.VMEM((replicas - 1, quarter, feat_width), BF16),
            pltpu.VMEM((halo_rows, node_rows), BF16),
            pltpu.VMEM((node_rows, feat_width), BF16),
            pltpu.VMEM((halo_rows, joint_width), BF16),
            pltpu.SemaphoreType.DMA((1 + 2 * replicas + 2 * halo_steps,)),
        ],
    )
    returned = lax.all_to_all(joint, WIDE, 0, 0, tiled=True)
    (local_grad,) = call(
        functools.partial(local_kernel, replicas),
        "local_rows",
        [shape(node_rows, feat_width, F32)],
        [HBM] * 3,
        (local_t, grad_agg, own_base),
        block_flops,
        out_specs=[HBM],
        scratch=[
            pltpu.VMEM((node_rows, node_rows), BF16),
            pltpu.VMEM((node_rows, feat_width), BF16),
            pltpu.VMEM((quarter, feat_width), F32),
            pltpu.VMEM((node_rows, feat_width), F32),
            pltpu.SemaphoreType.DMA((4,)),
        ],
    )

    lanes = joint_width - feat_width
    copies, own_grad, *sends = call(
        functools.partial(return_kernel, replicas),
        "returned_rows",
        [shape(halo_rows, lanes, BF16), shape(quarter, feat_width, F32)] + send_outs,
        [VMEM, VMEM, HBM],
        (turned_slots, returned, local_grad),
        block_flops,
        out_specs=[HBM] + [VMEM] * replicas,
        scratch=[pltpu.VMEM((halo_rows, lanes), BF16)]
        + [pltpu.VMEM((node_rows, feat_width), F32)] * 2
        + [pltpu.SemaphoreType.DMA((replicas + 1,))],
    )
    for k in FAR_FIRST:
        own_grad = own_grad + send_to(sends[k - 1], k, replicas).astype(F32)

    tiles = lax.all_to_all(copies, WIDE, 0, 0, tiled=True)
    lane_tiles = feat_width // LANES
    own_share = (
        tiles.reshape(peer_count, slot_count, -1, LANES)
        .transpose(0, 2, 1, 3)
        .reshape(-1, lane_tiles, slot_count, LANES)
        .transpose(0, 2, 1, 3)
        .reshape(2 * share, feat_width)
    )
    shares = from_ahead(own_share, replicas)
    grad_self, grad_neigh = call(
        place_kernel,
        "place",
        [shape(feat_width, feat_width, BF16)] * 2,
        [SMEM] + [VMEM] * replicas,
        (rep_ref, own_share, shares[0], shares[2], shares[1]),
        0,
    )
    return out_feats, own_grad.astype(BF16), grad_self, grad_neigh


def solution(mesh):
    fine = Mesh(
        mesh.devices.reshape(8, mesh.shape["wide"] // 16, 2, mesh.shape["rep"]), WIDE + ("rep",)
    )
    in_specs = (
        P(WIDE, None),
        P(),
        P(),
        P(WIDE, None, "rep"),
        P(WIDE, "rep", None),
        P(WIDE, "rep", None),
        P(WIDE, "rep", None),
        P(WIDE),
        P(WIDE + ("rep",), None),
    )
    out_specs = (P(WIDE + ("rep",), None), P(WIDE + ("rep",), None), P(), P())
    return jax.shard_map(
        on_device, mesh=fine, in_specs=in_specs, out_specs=out_specs, check_vma=False
    )
```

```python
import functools

import jax
import jax.numpy as jnp
from jax import lax
from jax.experimental import pallas as pl
from jax.experimental.pallas import tpu as pltpu
from jax.sharding import Mesh
from jax.sharding import PartitionSpec as P

BLOCK = 64
LANES = 128
WIDE = ("y", "z", "core")
FAR_FIRST = (2, 1, 3)
F32 = jnp.float32
BF16 = jnp.bfloat16
VMEM = pl.BlockSpec(memory_space=pltpu.VMEM)
HBM = pl.BlockSpec(memory_space=pltpu.HBM)
SMEM = pl.BlockSpec(memory_space=pltpu.SMEM)


def dot(left, right, left_dim, right_dim):
    dims = (((left_dim,), (right_dim,)), ((), ()))
    return lax.dot_general(left, right, dims, preferred_element_type=F32)


def call(kernel, name, outs, in_specs, args, flops, out_specs=None, scratch=(), vmem=24):
    moved = sum(a.size * a.dtype.itemsize for a in args) + sum(
        o.size * o.dtype.itemsize for o in outs
    )
    args = [
        pltpu.with_memory_space_constraint(a, pltpu.HBM) if spec is HBM else a
        for a, spec in zip(args, in_specs, strict=True)
    ]
    out_specs = out_specs or [VMEM] * len(outs)
    outs = [
        pltpu.HBM(o.shape, o.dtype) if spec is HBM else o
        for o, spec in zip(outs, out_specs, strict=True)
    ]
    return pl.pallas_call(
        kernel,
        out_shape=outs,
        in_specs=in_specs,
        out_specs=out_specs,
        scratch_shapes=scratch,
        compiler_params=pltpu.CompilerParams(vmem_limit_bytes=vmem << 20),
        cost_estimate=pl.CostEstimate(flops=flops, bytes_accessed=moved, transcendentals=0),
        name=name,
    )(*args)


def shape(rows, cols, dtype):
    return jax.ShapeDtypeStruct((rows, cols), dtype)


def started(source, target, sem):
    copy = pltpu.make_async_copy(source, target, sem)
    copy.start()
    return copy


def turned_quarters(rep_ref, feats_hbm, feats_ref, sems, replicas):
    quarter = feats_ref.shape[0] // replicas
    copies = []
    for k in range(replicas):
        at = pl.multiple_of(((rep_ref[0] + k) % replicas) * quarter, quarter)
        copies.append(
            started(
                feats_hbm.at[pl.ds(at, quarter), :],
                feats_ref.at[pl.ds(k * quarter, quarter), :],
                sems.at[k],
            )
        )
    return copies


def count_kernel(
    replicas, rep_ref, place_ref, words_ref, feats_hbm, local_t_hbm, halo_ref, halo_t_hbm, sums_hbm,
    counts_ref, turned_ref, feats_ref, sums_ref, sems,
):
    feats_copies = turned_quarters(rep_ref, feats_hbm, feats_ref, sems, replicas)
    counts_ref[...] = jnp.zeros_like(counts_ref)
    row = lax.broadcasted_iota(jnp.int32, (BLOCK, LANES), 0)
    lane = lax.broadcasted_iota(jnp.int32, (BLOCK, LANES), 1)
    word_lane = (row % 32) * 4 + (lane % BLOCK) // 16
    shift = lane % 16
    half = lane // BLOCK

    def add_tile(t, carry):
        place = place_ref[t]
        dst = pl.multiple_of((place // 64) * BLOCK, BLOCK)
        src = place % 64
        upper = jnp.broadcast_to(words_ref[pl.ds(2 * t, 1), :], (32, LANES))
        lower = jnp.broadcast_to(words_ref[pl.ds(2 * t + 1, 1), :], (32, LANES))
        words = jnp.concatenate([upper, lower], axis=0)
        picked = jnp.take_along_axis(words, word_lane, axis=1)
        bits = jnp.right_shift(picked, shift) & 1
        tile = jnp.where(half == src % 2, bits, 0).astype(F32).astype(BF16)
        rows = pl.ds(dst, BLOCK)
        cols = pl.ds(pl.multiple_of((src // 2) * LANES, LANES), LANES)
        counts_ref[rows, cols] = counts_ref[rows, cols] + tile
        return carry

    lax.fori_loop(0, place_ref.shape[0], add_tile, 0, unroll=4)
    split = local_t_hbm.shape[0]
    turned_ref[...] = counts_ref[...].T
    local_copy = started(turned_ref.at[pl.ds(0, split), :], local_t_hbm, sems.at[replicas])
    halo_copy = started(
        turned_ref.at[pl.ds(split, turned_ref.shape[0] - split), :], halo_t_hbm, sems.at[replicas + 1]
    )
    halo_ref[...] = counts_ref[:, split:]
    for copy in feats_copies:
        copy.wait()
    rows_done = 256
    for at in range(0, counts_ref.shape[0], rows_done):
        rows = pl.ds(at, rows_done)
        sums_ref[rows, :] = dot(counts_ref[rows, :split], feats_ref[...], 1, 0)
    sums_copy = started(sums_ref, sums_hbm, sems.at[replicas + 2])
    local_copy.wait()
    halo_copy.wait()
    sums_copy.wait()


def quarter_copies(local_hbm, local_ref, sems, order):
    quarter = local_ref.shape[0] // len(order)
    rows = {k: pl.ds(k * quarter, quarter) for k in order}
    return rows, {
        k: started(local_hbm.at[rows[k], :], local_ref.at[rows[k], :], sems.at[k]) for k in order
    }


def gather_kernel(slots_hbm, feats_hbm, rows_hbm, slots_ref, feats_ref, rows_ref, sems):
    slots_copy = started(slots_hbm, slots_ref, sems.at[0])
    feats_copy = started(feats_hbm, feats_ref, sems.at[1])
    slots_copy.wait()
    slot_count, peers = slots_ref.shape
    node_rows = feats_ref.shape[0]
    lane = lax.broadcasted_iota(jnp.int32, (slot_count, node_rows), 1)
    slots = slots_ref[...]
    step = min(32, peers)
    copies = []
    for at in range(0, peers, step):
        pick = jnp.concatenate(
            [
                jnp.where(lane == slots[:, s : s + 1], 1.0, 0.0).astype(F32)
                for s in range(at, at + step)
            ],
            axis=0,
        ).astype(BF16)
        if at == 0:
            feats_copy.wait()
        rows = pl.ds(at * slot_count, step * slot_count)
        rows_ref[rows, :] = dot(pick, feats_ref[...], 1, 0).astype(BF16)
        copies.append(
            started(rows_ref.at[rows, :], rows_hbm.at[rows, :], sems.at[2 + at // step])
        )
    for copy in copies:
        copy.wait()


def sum_kernel(
    counts_ref, incoming_ref, local_hbm, own_ref, send1, send2, send3, local_ref, total_ref, sems
):
    order = (2, 1, 3, 0)
    quarters, copies = quarter_copies(local_hbm, local_ref, sems, order)
    for rows in quarters.values():
        total_ref[rows, :] = dot(counts_ref[rows, :], incoming_ref[...], 1, 0)
    for k, rows in quarters.items():
        copies[k].wait()
        total = total_ref[rows, :] + local_ref[rows, :]
        if k:
            (send1, send2, send3)[k - 1][...] = total.astype(BF16)
        else:
            own_ref[...] = total


def dense_quarter(agg, feats, grad_out, scale, w_self, w_neigh):
    pre = dot(agg, w_neigh, 1, 0) + dot(feats, w_self, 1, 0)
    sigmoid = jax.nn.sigmoid(pre)
    grad_pre = (grad_out.astype(F32) * sigmoid * (1.0 + pre * (1.0 - sigmoid))).astype(BF16)
    grad_agg = (dot(grad_pre, w_neigh, 1, 1) * scale).astype(BF16)
    return pre * sigmoid, grad_pre, grad_agg


def own_kernel(
    replicas, rep_ref, agg_ref, grad_ref, feats_hbm, w_self_ref, w_neigh_ref, scale_ref,
    out_ref, base_hbm, grad_agg_ref, weights_ref, feats_ref, base_ref, sems,
):
    quarter, feat_width = agg_ref.shape
    share = feat_width // replicas
    own_rows = pl.ds(pl.multiple_of(rep_ref[0] * quarter, quarter), quarter)
    feats_copy = started(feats_hbm.at[own_rows, :], feats_ref, sems.at[0])
    feats_copy.wait()
    out, grad_pre, grad_agg = dense_quarter(
        agg_ref[...], feats_ref[...], grad_ref[...], scale_ref[:quarter, :], w_self_ref[...],
        w_neigh_ref[...],
    )
    out_ref[...] = out.astype(BF16)
    grad_agg_ref[...] = grad_agg
    base_ref[...] = dot(grad_pre, w_self_ref[...], 1, 1)
    base_copy = started(base_ref, base_hbm, sems.at[1])
    share_cols = pl.ds(pl.multiple_of(rep_ref[0] * share, LANES), share)
    weights_ref[:share, :] = dot(feats_ref[:, share_cols], grad_pre, 0, 0)
    weights_ref[share:, :] = dot(agg_ref[:, share_cols], grad_pre, 0, 0)
    base_copy.wait()


def far_kernel(
    replicas, step, rep_ref, agg_ref, grad_hbm, feats_hbm, w_self_ref, w_neigh_ref, scale_ref, before_ref,
    grad_agg_ref, weights_ref, grad_ref, feats_ref, sems,
):
    quarter, feat_width = agg_ref.shape
    share = feat_width // replicas
    at = pl.multiple_of(((rep_ref[0] + step) % replicas) * quarter, quarter)
    feats_copy = started(feats_hbm.at[pl.ds(at, quarter), :], feats_ref, sems.at[0])
    grad_copy = started(grad_hbm, grad_ref, sems.at[1])
    feats_copy.wait()
    grad_copy.wait()
    _, grad_pre, grad_agg = dense_quarter(
        agg_ref[...], feats_ref[...], grad_ref[...], scale_ref[pl.ds(step * quarter, quarter), :],
        w_self_ref[...], w_neigh_ref[...],
    )
    grad_agg_ref[...] = grad_agg
    share_cols = pl.ds(pl.multiple_of(rep_ref[0] * share, LANES), share)
    weights_ref[:share, :] = before_ref[:share, :] + dot(feats_ref[:, share_cols], grad_pre, 0, 0)
    weights_ref[share:, :] = before_ref[share:, :] + dot(agg_ref[:, share_cols], grad_pre, 0, 0)


def dense_kernel(
    replicas, rep_ref, agg1, agg3, grad1, grad3, feats_hbm, w_self_ref, w_neigh_ref, scale_ref,
    halo_t_hbm, grad_agg0_ref, grad_agg2_ref, weights_ref, grad_agg_hbm, joint_hbm,
    grad_ref, feats_ref, halo_t_ref, grad_agg_ref, joint_ref, sems,
):
    aggs = {1: agg1, 3: agg3}
    quarter, feat_width = agg1.shape
    share = feat_width // replicas
    halo_rows = halo_t_ref.shape[0]
    step = min(256, halo_rows)
    starts = range(0, halo_rows, step)
    feats_copies, grad_copies = [], []
    for n, (k, grad) in enumerate(zip(aggs, (grad1, grad3), strict=True)):
        at = pl.multiple_of(((rep_ref[0] + k) % replicas) * quarter, quarter)
        feats_copies.append(started(feats_hbm.at[pl.ds(at, quarter), :], feats_ref.at[n], sems.at[n]))
        grad_copies.append(started(grad, grad_ref.at[n], sems.at[2 + n]))
    at = 4
    halo_copies = [
        started(halo_t_hbm.at[pl.ds(i, step), :], halo_t_ref.at[pl.ds(i, step), :], sems.at[at + n])
        for n, i in enumerate(starts)
    ]
    at += len(starts)
    share_cols = pl.ds(pl.multiple_of(rep_ref[0] * share, LANES), share)
    grad_self = weights_ref[:share, :]
    grad_neigh = weights_ref[share:, :]
    grad_agg_ref[:quarter, :] = grad_agg0_ref[...]
    grad_agg_ref[pl.ds(2 * quarter, quarter), :] = grad_agg2_ref[...]
    for n, (k, agg_ref) in enumerate(aggs.items()):
        rows = pl.ds(k * quarter, quarter)
        feats_copies[n].wait()
        grad_copies[n].wait()
        _, grad_pre, grad_agg = dense_quarter(
            agg_ref[...], feats_ref[n], grad_ref[n], scale_ref[rows, :], w_self_ref[...],
            w_neigh_ref[...],
        )
        grad_agg_ref[rows, :] = grad_agg
        grad_self = grad_self + dot(feats_ref[n, :, share_cols], grad_pre, 0, 0)
        grad_neigh = grad_neigh + dot(agg_ref[:, share_cols], grad_pre, 0, 0)
    grad_agg_copy = started(grad_agg_ref, grad_agg_hbm, sems.at[at])
    tile = 0
    per_peer = (joint_ref.shape[1] - feat_width) // LANES
    for part in (grad_self, grad_neigh):
        for g in range(0, share, 8):
            for c in range(0, feat_width, LANES):
                peer, slot = tile // per_peer, tile % per_peer
                lane = feat_width + slot * LANES
                joint_ref[peer * 8 : peer * 8 + 8, lane : lane + LANES] = part[
                    g : g + 8, c : c + LANES
                ].astype(BF16)
                tile += 1
    joint_copies = []
    for n, i in enumerate(starts):
        rows = pl.ds(i, step)
        halo_copies[n].wait()
        joint_ref[rows, :feat_width] = dot(halo_t_ref[rows, :], grad_agg_ref[...], 1, 0).astype(BF16)
        joint_copies.append(started(joint_ref.at[rows, :], joint_hbm.at[rows, :], sems.at[at + 1 + n]))
    grad_agg_copy.wait()
    for copy in joint_copies:
        copy.wait()


def local_kernel(
    replicas, counts_hbm, grad_hbm, base_hbm, local_hbm, counts_ref, grad_ref, base_ref, local_ref, sems
):
    copies = [
        started(*pair, sems.at[n])
        for n, pair in enumerate(
            ((counts_hbm, counts_ref), (grad_hbm, grad_ref), (base_hbm, base_ref))
        )
    ]
    for copy in copies:
        copy.wait()
    quarter = base_ref.shape[0]
    for k in range(replicas):
        rows = pl.ds(k * quarter, quarter)
        total = dot(counts_ref[rows, :], grad_ref[...], 1, 0)
        local_ref[rows, :] = total if k else total + base_ref[...]
    copy = started(local_ref, local_hbm, sems.at[3])
    copy.wait()


def tile_kernel(joint_ref, copies_hbm, tiles_ref, sems):
    halo_rows, lanes = tiles_ref.shape
    feat_width = joint_ref.shape[1] - lanes
    tiles = joint_ref[:, feat_width:].astype(F32).reshape(halo_rows // 8, 8, lanes)
    tile = tiles.sum(axis=0, keepdims=True)
    tiles_ref[...] = jnp.broadcast_to(tile, tiles.shape).reshape(halo_rows, lanes).astype(BF16)
    copy = started(tiles_ref, copies_hbm, sems.at[0])
    copy.wait()


def return_kernel(
    replicas, rep_ref, slots_ref, joint_ref, local_hbm, own_ref, send1, send2, send3, local_ref,
    total_ref, sems,
):
    quarter, feat_width = own_ref.shape
    halo_rows = joint_ref.shape[0]
    order = (2, 1, 3, 0)
    quarters, copies = quarter_copies(local_hbm, local_ref, sems, order)
    slots = slots_ref[...]
    slot = lax.broadcasted_iota(jnp.int32, slots.shape, 0)
    lane = lax.broadcasted_iota(jnp.int32, slots.shape, 1)
    pieces = []
    for at in range(0, halo_rows, LANES):
        picked = jnp.take_along_axis(slots, at // 8 + lane // 8, axis=1)
        pieces.append(jnp.where(slot == lane % 8, picked, 0).sum(axis=0, keepdims=True))
    turned = jnp.concatenate(pieces, axis=1) - rep_ref[0] * quarter
    turned = jnp.where(turned < 0, turned + quarter * replicas, turned)
    turned = jnp.broadcast_to(turned, (quarter, halo_rows))
    row = lax.broadcasted_iota(jnp.int32, (quarter, halo_rows), 0)
    for k, rows in quarters.items():
        pick = jnp.where(row + k * quarter == turned, 1.0, 0.0).astype(BF16)
        total_ref[rows, :] = dot(pick, joint_ref[:, :feat_width], 1, 0)
    for k, rows in quarters.items():
        copies[k].wait()
        total = total_ref[rows, :] + local_ref[rows, :]
        if k:
            (send1, send2, send3)[k - 1][...] = total.astype(BF16)
        else:
            own_ref[...] = total


def place_kernel(rep_ref, part0, part1, part3, part2, self_ref, neigh_ref):
    parts = (part0, part1, part2, part3)
    share = part0.shape[0] // 2
    for k, part in enumerate(parts):
        at = pl.ds(pl.multiple_of(((rep_ref[0] + k) % len(parts)) * share, share), share)
        self_ref[at, :] = part[:share, :]
        neigh_ref[at, :] = part[share:, :]


def send_to(x, step, replicas):
    return lax.ppermute(x, "rep", [(i, (i + step) % replicas) for i in range(replicas)])


def from_ahead(x, replicas):
    ahead = {k: send_to(x, replicas - k, replicas) for k in reversed(FAR_FIRST)}
    return [ahead[k] for k in range(1, replicas)]


def on_device(
    node_feats, w_self, w_neigh, send_rows, tile_dst, tile_src, tile_bits, norm_count, grad_out
):
    node_rows, feat_width = node_feats.shape
    peer_count = lax.axis_size(WIDE)
    replicas = lax.axis_size("rep")
    slot_count = send_rows.shape[2]
    tile_total = tile_dst.shape[2]
    quarter = node_rows // replicas
    share = feat_width // replicas
    rep_index = lax.axis_index("rep")
    rep_ref = rep_index.reshape(1).astype(jnp.int32)
    dst_count = node_rows // BLOCK
    halo_rows = peer_count * slot_count
    first_row = rep_index * quarter
    first_block = rep_index * (quarter // BLOCK)
    send_outs = [shape(quarter, feat_width, BF16)] * (replicas - 1)

    slots = send_rows[0].T
    (outgoing,) = call(
        gather_kernel,
        "gather_rows",
        [shape(halo_rows, feat_width, BF16)],
        [HBM, HBM],
        (slots, node_feats),
        2 * node_rows * halo_rows * feat_width,
        out_specs=[HBM],
        scratch=[
            pltpu.VMEM((slot_count, peer_count), jnp.int32),
            pltpu.VMEM((node_rows, feat_width), BF16),
            pltpu.VMEM((halo_rows, feat_width), BF16),
            pltpu.SemaphoreType.DMA((2 + max(1, peer_count // 32),)),
        ],
    )
    incoming = lax.all_to_all(outgoing, WIDE, 0, 0, tiled=True)

    scale = lax.rsqrt(norm_count.astype(F32))
    scale = lax.dynamic_slice_in_dim(jnp.concatenate([scale, scale]), first_row, node_rows, 0)
    scale = scale[:, None]
    grad_outs = [grad_out] + from_ahead(grad_out, replicas)
    dst = (tile_dst[0, 0] - first_block) % dst_count
    src = tile_src[0, 0]
    src = jnp.where(src < dst_count, (src - first_block) % dst_count, src)
    block_flops = 2 * node_rows * halo_rows * feat_width
    local_t, counts_halo, halo_t, sums_local = call(
        functools.partial(count_kernel, replicas),
        "tile_counts",
        [
            shape(node_rows, node_rows, BF16),
            shape(node_rows, halo_rows, BF16),
            shape(halo_rows, node_rows, BF16),
            shape(node_rows, feat_width, F32),
        ],
        [SMEM, SMEM, VMEM, HBM],
        (rep_ref, dst * 64 + src, tile_bits.reshape(tile_total * 2, LANES), node_feats),
        tile_total * BLOCK * LANES * 20 + block_flops,
        out_specs=[HBM, VMEM, HBM, HBM],
        scratch=[
            pltpu.VMEM((node_rows, node_rows + halo_rows), BF16),
            pltpu.VMEM((node_rows + halo_rows, node_rows), BF16),
            pltpu.VMEM((node_rows, feat_width), BF16),
            pltpu.VMEM((node_rows, feat_width), F32),
            pltpu.SemaphoreType.DMA((replicas + 3,)),
        ],
    )
    incoming, counts_halo, sums_local, scale, *grad_outs = lax.optimization_barrier(
        (incoming, counts_halo, sums_local, scale, *grad_outs)
    )

    own_sums, *sends = call(
        sum_kernel,
        "neighbour_sums",
        [shape(quarter, feat_width, F32)] + send_outs,
        [VMEM, VMEM, HBM],
        (counts_halo, incoming, sums_local),
        block_flops,
        scratch=[pltpu.VMEM((node_rows, feat_width), F32)] * 2
        + [pltpu.SemaphoreType.DMA((replicas,))],
    )
    for k in FAR_FIRST:
        own_sums = own_sums + send_to(sends[k - 1], k, replicas).astype(F32)
    own_agg = (own_sums * scale[:quarter]).astype(BF16)
    aggs = from_ahead(own_agg, replicas)
    joint_width = feat_width + 2 * share * feat_width // halo_rows
    halo_steps = max(1, halo_rows // 256)
    out_feats, own_base, own_grad_agg, own_weights = call(
        functools.partial(own_kernel, replicas),
        "dense_own",
        [
            shape(quarter, feat_width, BF16),
            shape(quarter, feat_width, F32),
            shape(quarter, feat_width, BF16),
            shape(2 * share, feat_width, F32),
        ],
        [SMEM, VMEM, VMEM, HBM, VMEM, VMEM, VMEM],
        (rep_ref, own_agg, grad_outs[0], node_feats, w_self, w_neigh, scale),
        block_flops // 2,
        out_specs=[VMEM, HBM, VMEM, VMEM],
        scratch=[
            pltpu.VMEM((quarter, feat_width), BF16),
            pltpu.VMEM((quarter, feat_width), F32),
            pltpu.SemaphoreType.DMA((2,)),
        ],
    )
    far_grad_agg, far_weights = call(
        functools.partial(far_kernel, replicas, 2),
        "dense_far",
        [shape(quarter, feat_width, BF16), shape(2 * share, feat_width, F32)],
        [SMEM, VMEM, HBM, HBM, VMEM, VMEM, VMEM, VMEM],
        (rep_ref, aggs[1], grad_outs[2], node_feats, w_self, w_neigh, scale, own_weights),
        block_flops // 2,
        scratch=[pltpu.VMEM((quarter, feat_width), BF16)] * 2 + [pltpu.SemaphoreType.DMA((2,))],
    )
    grad_agg, joint = call(
        functools.partial(dense_kernel, replicas),
        "dense_rest",
        [shape(node_rows, feat_width, BF16), shape(halo_rows, joint_width, BF16)],
        [SMEM] + [VMEM] * 2 + [HBM] * 3 + [VMEM] * 3 + [HBM] + [VMEM] * 3,
        (
            rep_ref, aggs[0], aggs[2], grad_outs[1], grad_outs[3], node_feats, w_self, w_neigh, scale, halo_t,
            own_grad_agg, far_grad_agg, far_weights,
        ),
        2 * block_flops,
        out_specs=[HBM, HBM],
        scratch=[
            pltpu.VMEM((2, quarter, feat_width), BF16),
            pltpu.VMEM((2, quarter, feat_width), BF16),
            pltpu.VMEM((halo_rows, node_rows), BF16),
            pltpu.VMEM((node_rows, feat_width), BF16),
            pltpu.VMEM((halo_rows, joint_width), BF16),
            pltpu.SemaphoreType.DMA((5 + 2 * halo_steps,)),
        ],
    )
    returned = lax.all_to_all(joint, WIDE, 0, 0, tiled=True)
    (local_grad,) = call(
        functools.partial(local_kernel, replicas),
        "local_rows",
        [shape(node_rows, feat_width, F32)],
        [HBM] * 3,
        (local_t, grad_agg, own_base),
        block_flops,
        out_specs=[HBM],
        scratch=[
            pltpu.VMEM((node_rows, node_rows), BF16),
            pltpu.VMEM((node_rows, feat_width), BF16),
            pltpu.VMEM((quarter, feat_width), F32),
            pltpu.VMEM((node_rows, feat_width), F32),
            pltpu.SemaphoreType.DMA((4,)),
        ],
    )

    lanes = joint_width - feat_width
    (copies,) = call(
        tile_kernel,
        "weight_tile",
        [shape(halo_rows, lanes, BF16)],
        [VMEM],
        (returned,),
        halo_rows * lanes,
        out_specs=[HBM],
        scratch=[pltpu.VMEM((halo_rows, lanes), BF16), pltpu.SemaphoreType.DMA((1,))],
    )
    own_grad, *sends = call(
        functools.partial(return_kernel, replicas),
        "returned_rows",
        [shape(quarter, feat_width, F32)] + send_outs,
        [SMEM, VMEM, VMEM, HBM],
        (rep_ref, jnp.pad(slots, ((0, 0), (0, -peer_count % LANES))), returned, local_grad),
        block_flops,
        scratch=[pltpu.VMEM((node_rows, feat_width), F32)] * 2
        + [pltpu.SemaphoreType.DMA((replicas,))],
    )
    for k in FAR_FIRST:
        own_grad = own_grad + send_to(sends[k - 1], k, replicas).astype(F32)

    tiles = lax.all_to_all(copies, WIDE, 0, 0, tiled=True)
    lane_tiles = feat_width // LANES
    own_share = (
        tiles.reshape(peer_count, slot_count, -1, LANES)
        .transpose(0, 2, 1, 3)
        .reshape(-1, lane_tiles, slot_count, LANES)
        .transpose(0, 2, 1, 3)
        .reshape(2 * share, feat_width)
    )
    shares = from_ahead(own_share, replicas)
    grad_self, grad_neigh = call(
        place_kernel,
        "place",
        [shape(feat_width, feat_width, BF16)] * 2,
        [SMEM] + [VMEM] * replicas,
        (rep_ref, own_share, shares[0], shares[2], shares[1]),
        0,
    )
    return out_feats, own_grad.astype(BF16), grad_self, grad_neigh


def solution(mesh):
    fine = Mesh(
        mesh.devices.reshape(8, mesh.shape["wide"] // 16, 2, mesh.shape["rep"]), WIDE + ("rep",)
    )
    in_specs = (
        P(WIDE, None),
        P(),
        P(),
        P(WIDE, None, "rep"),
        P(WIDE, "rep", None),
        P(WIDE, "rep", None),
        P(WIDE, "rep", None),
        P(WIDE),
        P(WIDE + ("rep",), None),
    )
    out_specs = (P(WIDE + ("rep",), None), P(WIDE + ("rep",), None), P(), P())
    return jax.shard_map(
        on_device, mesh=fine, in_specs=in_specs, out_specs=out_specs, check_vma=False
    )
```

```python
import functools

import jax
import jax.numpy as jnp
from jax import lax
from jax.experimental import pallas as pl
from jax.experimental.pallas import tpu as pltpu
from jax.sharding import Mesh
from jax.sharding import PartitionSpec as P

BLOCK = 64
LANES = 128
WIDE = ("y", "z", "core")
FAR_FIRST = (2, 1, 3)
F32 = jnp.float32
BF16 = jnp.bfloat16
VMEM = pl.BlockSpec(memory_space=pltpu.VMEM)
HBM = pl.BlockSpec(memory_space=pltpu.HBM)
SMEM = pl.BlockSpec(memory_space=pltpu.SMEM)


def dot(left, right, left_dim, right_dim):
    dims = (((left_dim,), (right_dim,)), ((), ()))
    return lax.dot_general(left, right, dims, preferred_element_type=F32)


def call(kernel, name, outs, in_specs, args, flops, out_specs=None, scratch=(), vmem=24):
    moved = sum(a.size * a.dtype.itemsize for a in args) + sum(
        o.size * o.dtype.itemsize for o in outs
    )
    args = [
        pltpu.with_memory_space_constraint(a, pltpu.HBM) if spec is HBM else a
        for a, spec in zip(args, in_specs, strict=True)
    ]
    out_specs = out_specs or [VMEM] * len(outs)
    outs = [
        pltpu.HBM(o.shape, o.dtype) if spec is HBM else o
        for o, spec in zip(outs, out_specs, strict=True)
    ]
    return pl.pallas_call(
        kernel,
        out_shape=outs,
        in_specs=in_specs,
        out_specs=out_specs,
        scratch_shapes=scratch,
        compiler_params=pltpu.CompilerParams(vmem_limit_bytes=vmem << 20),
        cost_estimate=pl.CostEstimate(flops=flops, bytes_accessed=moved, transcendentals=0),
        name=name,
    )(*args)


def shape(rows, cols, dtype):
    return jax.ShapeDtypeStruct((rows, cols), dtype)


def started(source, target, sem):
    copy = pltpu.make_async_copy(source, target, sem)
    copy.start()
    return copy


def turned_quarters(rep_ref, feats_hbm, feats_ref, sems, replicas):
    quarter = feats_ref.shape[0] // replicas
    copies = []
    for k in range(replicas):
        at = pl.multiple_of(((rep_ref[0] + k) % replicas) * quarter, quarter)
        copies.append(
            started(
                feats_hbm.at[pl.ds(at, quarter), :],
                feats_ref.at[pl.ds(k * quarter, quarter), :],
                sems.at[k],
            )
        )
    return copies


def count_kernel(
    replicas, rep_ref, place_ref, words_ref, feats_hbm, local_t_hbm, halo_ref, halo_t_hbm, sums_hbm,
    counts_ref, turned_ref, feats_ref, sums_ref, sems,
):
    feats_copies = turned_quarters(rep_ref, feats_hbm, feats_ref, sems, replicas)
    counts_ref[...] = jnp.zeros_like(counts_ref)
    row = lax.broadcasted_iota(jnp.int32, (BLOCK, LANES), 0)
    lane = lax.broadcasted_iota(jnp.int32, (BLOCK, LANES), 1)
    word_lane = (row % 32) * 4 + (lane % BLOCK) // 16
    shift = lane % 16
    half = lane // BLOCK

    def add_tile(t, carry):
        place = place_ref[t]
        dst = pl.multiple_of((place // 64) * BLOCK, BLOCK)
        src = place % 64
        upper = jnp.broadcast_to(words_ref[pl.ds(2 * t, 1), :], (32, LANES))
        lower = jnp.broadcast_to(words_ref[pl.ds(2 * t + 1, 1), :], (32, LANES))
        words = jnp.concatenate([upper, lower], axis=0)
        picked = jnp.take_along_axis(words, word_lane, axis=1)
        bits = jnp.right_shift(picked, shift) & 1
        tile = jnp.where(half == src % 2, bits, 0).astype(F32).astype(BF16)
        rows = pl.ds(dst, BLOCK)
        cols = pl.ds(pl.multiple_of((src // 2) * LANES, LANES), LANES)
        counts_ref[rows, cols] = counts_ref[rows, cols] + tile
        return carry

    lax.fori_loop(0, place_ref.shape[0], add_tile, 0, unroll=4)
    split = local_t_hbm.shape[0]
    turned_ref[...] = counts_ref[...].T
    local_copy = started(turned_ref.at[pl.ds(0, split), :], local_t_hbm, sems.at[replicas])
    halo_copy = started(
        turned_ref.at[pl.ds(split, turned_ref.shape[0] - split), :], halo_t_hbm, sems.at[replicas + 1]
    )
    halo_ref[...] = counts_ref[:, split:]
    for copy in feats_copies:
        copy.wait()
    rows_done = 256
    for at in range(0, counts_ref.shape[0], rows_done):
        rows = pl.ds(at, rows_done)
        sums_ref[rows, :] = dot(counts_ref[rows, :split], feats_ref[...], 1, 0)
    sums_copy = started(sums_ref, sums_hbm, sems.at[replicas + 2])
    local_copy.wait()
    halo_copy.wait()
    sums_copy.wait()


def quarter_copies(local_hbm, local_ref, sems, order):
    quarter = local_ref.shape[0] // len(order)
    rows = {k: pl.ds(k * quarter, quarter) for k in order}
    return rows, {
        k: started(local_hbm.at[rows[k], :], local_ref.at[rows[k], :], sems.at[k]) for k in order
    }


def gather_kernel(slots_hbm, feats_hbm, rows_hbm, slots_ref, feats_ref, rows_ref, sems):
    slots_copy = started(slots_hbm, slots_ref, sems.at[0])
    feats_copy = started(feats_hbm, feats_ref, sems.at[1])
    slots_copy.wait()
    slot_count, peers = slots_ref.shape
    node_rows = feats_ref.shape[0]
    lane = lax.broadcasted_iota(jnp.int32, (slot_count, node_rows), 1)
    slots = slots_ref[...]
    step = min(32, peers)
    copies = []
    for at in range(0, peers, step):
        pick = jnp.concatenate(
            [
                jnp.where(lane == slots[:, s : s + 1], 1.0, 0.0).astype(F32)
                for s in range(at, at + step)
            ],
            axis=0,
        ).astype(BF16)
        if at == 0:
            feats_copy.wait()
        rows = pl.ds(at * slot_count, step * slot_count)
        rows_ref[rows, :] = dot(pick, feats_ref[...], 1, 0).astype(BF16)
        copies.append(
            started(rows_ref.at[rows, :], rows_hbm.at[rows, :], sems.at[2 + at // step])
        )
    for copy in copies:
        copy.wait()


def sum_kernel(
    counts_ref, incoming_ref, local_hbm, own_ref, send1, send2, send3, local_ref, total_ref, sems
):
    order = (2, 1, 3, 0)
    quarters, copies = quarter_copies(local_hbm, local_ref, sems, order)
    for rows in quarters.values():
        total_ref[rows, :] = dot(counts_ref[rows, :], incoming_ref[...], 1, 0)
    for k, rows in quarters.items():
        copies[k].wait()
        total = total_ref[rows, :] + local_ref[rows, :]
        if k:
            (send1, send2, send3)[k - 1][...] = total.astype(BF16)
        else:
            own_ref[...] = total


def dense_quarter(agg, feats, grad_out, scale, w_self, w_neigh):
    pre = dot(agg, w_neigh, 1, 0) + dot(feats, w_self, 1, 0)
    sigmoid = jax.nn.sigmoid(pre)
    grad_pre = (grad_out.astype(F32) * sigmoid * (1.0 + pre * (1.0 - sigmoid))).astype(BF16)
    grad_agg = (dot(grad_pre, w_neigh, 1, 1) * scale).astype(BF16)
    return pre * sigmoid, grad_pre, grad_agg


def own_kernel(
    replicas, rep_ref, agg_ref, grad_ref, feats_hbm, w_self_ref, w_neigh_ref, scale_ref,
    out_ref, base_hbm, grad_agg_ref, weights_ref, feats_ref, base_ref, sems,
):
    quarter, feat_width = agg_ref.shape
    share = feat_width // replicas
    own_rows = pl.ds(pl.multiple_of(rep_ref[0] * quarter, quarter), quarter)
    feats_copy = started(feats_hbm.at[own_rows, :], feats_ref, sems.at[0])
    feats_copy.wait()
    out, grad_pre, grad_agg = dense_quarter(
        agg_ref[...], feats_ref[...], grad_ref[...], scale_ref[:quarter, :], w_self_ref[...],
        w_neigh_ref[...],
    )
    out_ref[...] = out.astype(BF16)
    grad_agg_ref[...] = grad_agg
    base_ref[...] = dot(grad_pre, w_self_ref[...], 1, 1)
    base_copy = started(base_ref, base_hbm, sems.at[1])
    share_cols = pl.ds(pl.multiple_of(rep_ref[0] * share, LANES), share)
    weights_ref[:share, :] = dot(feats_ref[:, share_cols], grad_pre, 0, 0)
    weights_ref[share:, :] = dot(agg_ref[:, share_cols], grad_pre, 0, 0)
    base_copy.wait()


def far_kernel(
    replicas, step, rep_ref, agg_ref, grad_hbm, feats_hbm, w_self_ref, w_neigh_ref, scale_ref, before_ref,
    grad_agg_ref, weights_ref, grad_ref, feats_ref, sems,
):
    quarter, feat_width = agg_ref.shape
    share = feat_width // replicas
    at = pl.multiple_of(((rep_ref[0] + step) % replicas) * quarter, quarter)
    feats_copy = started(feats_hbm.at[pl.ds(at, quarter), :], feats_ref, sems.at[0])
    grad_copy = started(grad_hbm, grad_ref, sems.at[1])
    feats_copy.wait()
    grad_copy.wait()
    _, grad_pre, grad_agg = dense_quarter(
        agg_ref[...], feats_ref[...], grad_ref[...], scale_ref[pl.ds(step * quarter, quarter), :],
        w_self_ref[...], w_neigh_ref[...],
    )
    grad_agg_ref[...] = grad_agg
    share_cols = pl.ds(pl.multiple_of(rep_ref[0] * share, LANES), share)
    weights_ref[:share, :] = before_ref[:share, :] + dot(feats_ref[:, share_cols], grad_pre, 0, 0)
    weights_ref[share:, :] = before_ref[share:, :] + dot(agg_ref[:, share_cols], grad_pre, 0, 0)


def dense_kernel(
    replicas, rep_ref, agg1, agg3, grad1, grad3, feats_hbm, w_self_ref, w_neigh_ref, scale_ref,
    halo_t_hbm, grad_agg0_ref, grad_agg2_ref, weights_ref, grad_agg_hbm, joint_hbm,
    grad_ref, feats_ref, halo_t_ref, grad_agg_ref, joint_ref, sems,
):
    aggs = {1: agg1, 3: agg3}
    quarter, feat_width = agg1.shape
    share = feat_width // replicas
    halo_rows = halo_t_ref.shape[0]
    step = min(256, halo_rows)
    starts = range(0, halo_rows, step)
    feats_copies, grad_copies = [], []
    for n, (k, grad) in enumerate(zip(aggs, (grad1, grad3), strict=True)):
        at = pl.multiple_of(((rep_ref[0] + k) % replicas) * quarter, quarter)
        feats_copies.append(started(feats_hbm.at[pl.ds(at, quarter), :], feats_ref.at[n], sems.at[n]))
        grad_copies.append(started(grad, grad_ref.at[n], sems.at[2 + n]))
    at = 4
    halo_copies = [
        started(halo_t_hbm.at[pl.ds(i, step), :], halo_t_ref.at[pl.ds(i, step), :], sems.at[at + n])
        for n, i in enumerate(starts)
    ]
    at += len(starts)
    share_cols = pl.ds(pl.multiple_of(rep_ref[0] * share, LANES), share)
    grad_self = weights_ref[:share, :]
    grad_neigh = weights_ref[share:, :]
    grad_agg_ref[:quarter, :] = grad_agg0_ref[...]
    grad_agg_ref[pl.ds(2 * quarter, quarter), :] = grad_agg2_ref[...]
    for n, (k, agg_ref) in enumerate(aggs.items()):
        rows = pl.ds(k * quarter, quarter)
        feats_copies[n].wait()
        grad_copies[n].wait()
        _, grad_pre, grad_agg = dense_quarter(
            agg_ref[...], feats_ref[n], grad_ref[n], scale_ref[rows, :], w_self_ref[...],
            w_neigh_ref[...],
        )
        grad_agg_ref[rows, :] = grad_agg
        grad_self = grad_self + dot(feats_ref[n, :, share_cols], grad_pre, 0, 0)
        grad_neigh = grad_neigh + dot(agg_ref[:, share_cols], grad_pre, 0, 0)
    grad_agg_copy = started(grad_agg_ref, grad_agg_hbm, sems.at[at])
    tile = 0
    per_peer = (joint_ref.shape[1] - feat_width) // LANES
    for part in (grad_self, grad_neigh):
        for g in range(0, share, 8):
            for c in range(0, feat_width, LANES):
                peer, slot = tile // per_peer, tile % per_peer
                lane = feat_width + slot * LANES
                joint_ref[peer * 8 : peer * 8 + 8, lane : lane + LANES] = part[
                    g : g + 8, c : c + LANES
                ].astype(BF16)
                tile += 1
    joint_copies = []
    for n, i in enumerate(starts):
        rows = pl.ds(i, step)
        halo_copies[n].wait()
        joint_ref[rows, :feat_width] = dot(halo_t_ref[rows, :], grad_agg_ref[...], 1, 0).astype(BF16)
        joint_copies.append(started(joint_ref.at[rows, :], joint_hbm.at[rows, :], sems.at[at + 1 + n]))
    grad_agg_copy.wait()
    for copy in joint_copies:
        copy.wait()


def local_kernel(
    replicas, counts_hbm, grad_hbm, base_hbm, local_hbm, counts_ref, grad_ref, base_ref, local_ref, sems
):
    copies = [
        started(*pair, sems.at[n])
        for n, pair in enumerate(
            ((counts_hbm, counts_ref), (grad_hbm, grad_ref), (base_hbm, base_ref))
        )
    ]
    for copy in copies:
        copy.wait()
    quarter = base_ref.shape[0]
    for k in range(replicas):
        rows = pl.ds(k * quarter, quarter)
        total = dot(counts_ref[rows, :], grad_ref[...], 1, 0)
        local_ref[rows, :] = total if k else total + base_ref[...]
    copy = started(local_ref, local_hbm, sems.at[3])
    copy.wait()


def tile_kernel(joint_ref, copies_hbm, tiles_ref, sems):
    halo_rows, lanes = tiles_ref.shape
    feat_width = joint_ref.shape[1] - lanes
    tiles = joint_ref[:, feat_width:].astype(F32).reshape(halo_rows // 8, 8, lanes)
    tile = tiles.sum(axis=0, keepdims=True)
    tiles_ref[...] = jnp.broadcast_to(tile, tiles.shape).reshape(halo_rows, lanes).astype(BF16)
    copy = started(tiles_ref, copies_hbm, sems.at[0])
    copy.wait()


def return_kernel(
    replicas, rep_ref, slots_ref, joint_ref, local_hbm, own_ref, send1, send2, send3, local_ref,
    total_ref, sems,
):
    quarter, feat_width = own_ref.shape
    halo_rows = joint_ref.shape[0]
    order = (2, 1, 3, 0)
    quarters, copies = quarter_copies(local_hbm, local_ref, sems, order)
    slots = slots_ref[...]
    slot = lax.broadcasted_iota(jnp.int32, slots.shape, 0)
    lane = lax.broadcasted_iota(jnp.int32, slots.shape, 1)
    pieces = []
    for at in range(0, halo_rows, LANES):
        picked = jnp.take_along_axis(slots, at // 8 + lane // 8, axis=1)
        pieces.append(jnp.where(slot == lane % 8, picked, 0).sum(axis=0, keepdims=True))
    turned = jnp.concatenate(pieces, axis=1) - rep_ref[0] * quarter
    turned = jnp.where(turned < 0, turned + quarter * replicas, turned)
    turned = jnp.broadcast_to(turned, (quarter, halo_rows))
    row = lax.broadcasted_iota(jnp.int32, (quarter, halo_rows), 0)
    for k, rows in quarters.items():
        pick = jnp.where(row + k * quarter == turned, 1.0, 0.0).astype(BF16)
        total_ref[rows, :] = dot(pick, joint_ref[:, :feat_width], 1, 0)
    for k, rows in quarters.items():
        copies[k].wait()
        total = total_ref[rows, :] + local_ref[rows, :]
        if k:
            (send1, send2, send3)[k - 1][...] = total.astype(BF16)
        else:
            own_ref[...] = total


def place_kernel(rep_ref, part0, part1, part3, part2, self_ref, neigh_ref):
    parts = (part0, part1, part2, part3)
    share = part0.shape[0] // 2
    for k, part in enumerate(parts):
        at = pl.ds(pl.multiple_of(((rep_ref[0] + k) % len(parts)) * share, share), share)
        self_ref[at, :] = part[:share, :]
        neigh_ref[at, :] = part[share:, :]


def send_to(x, step, replicas):
    return lax.ppermute(x, "rep", [(i, (i + step) % replicas) for i in range(replicas)])


def from_ahead(x, replicas):
    ahead = {k: send_to(x, replicas - k, replicas) for k in reversed(FAR_FIRST)}
    return [ahead[k] for k in range(1, replicas)]


def on_device(
    node_feats, w_self, w_neigh, send_rows, tile_dst, tile_src, tile_bits, norm_count, grad_out
):
    node_rows, feat_width = node_feats.shape
    peer_count = lax.axis_size(WIDE)
    replicas = lax.axis_size("rep")
    slot_count = send_rows.shape[2]
    tile_total = tile_dst.shape[2]
    quarter = node_rows // replicas
    share = feat_width // replicas
    rep_index = lax.axis_index("rep")
    rep_ref = rep_index.reshape(1).astype(jnp.int32)
    dst_count = node_rows // BLOCK
    halo_rows = peer_count * slot_count
    first_row = rep_index * quarter
    first_block = rep_index * (quarter // BLOCK)
    send_outs = [shape(quarter, feat_width, BF16)] * (replicas - 1)

    slots = send_rows[0].T
    (outgoing,) = call(
        gather_kernel,
        "gather_rows",
        [shape(halo_rows, feat_width, BF16)],
        [HBM, HBM],
        (slots, node_feats),
        2 * node_rows * halo_rows * feat_width,
        out_specs=[HBM],
        scratch=[
            pltpu.VMEM((slot_count, peer_count), jnp.int32),
            pltpu.VMEM((node_rows, feat_width), BF16),
            pltpu.VMEM((halo_rows, feat_width), BF16),
            pltpu.SemaphoreType.DMA((2 + max(1, peer_count // 32),)),
        ],
    )
    incoming = lax.all_to_all(outgoing, WIDE, 0, 0, tiled=True)

    scale = lax.rsqrt(norm_count.astype(F32))
    scale = lax.dynamic_slice_in_dim(jnp.concatenate([scale, scale]), first_row, node_rows, 0)
    scale = scale[:, None]
    grad_outs = [grad_out] + from_ahead(grad_out, replicas)
    dst = (tile_dst[0, 0] - first_block) % dst_count
    src = tile_src[0, 0]
    src = jnp.where(src < dst_count, (src - first_block) % dst_count, src)
    block_flops = 2 * node_rows * halo_rows * feat_width
    local_t, counts_halo, halo_t, sums_local = call(
        functools.partial(count_kernel, replicas),
        "tile_counts",
        [
            shape(node_rows, node_rows, BF16),
            shape(node_rows, halo_rows, BF16),
            shape(halo_rows, node_rows, BF16),
            shape(node_rows, feat_width, F32),
        ],
        [SMEM, SMEM, VMEM, HBM],
        (rep_ref, dst * 64 + src, tile_bits.reshape(tile_total * 2, LANES), node_feats),
        tile_total * BLOCK * LANES * 20 + block_flops,
        out_specs=[HBM, VMEM, HBM, HBM],
        scratch=[
            pltpu.VMEM((node_rows, node_rows + halo_rows), BF16),
            pltpu.VMEM((node_rows + halo_rows, node_rows), BF16),
            pltpu.VMEM((node_rows, feat_width), BF16),
            pltpu.VMEM((node_rows, feat_width), F32),
            pltpu.SemaphoreType.DMA((replicas + 3,)),
        ],
    )
    incoming, counts_halo, sums_local, scale, *grad_outs = lax.optimization_barrier(
        (incoming, counts_halo, sums_local, scale, *grad_outs)
    )

    own_sums, *sends = call(
        sum_kernel,
        "neighbour_sums",
        [shape(quarter, feat_width, F32)] + send_outs,
        [VMEM, VMEM, HBM],
        (counts_halo, incoming, sums_local),
        block_flops,
        scratch=[pltpu.VMEM((node_rows, feat_width), F32)] * 2
        + [pltpu.SemaphoreType.DMA((replicas,))],
    )
    for k in FAR_FIRST:
        own_sums = own_sums + send_to(sends[k - 1], k, replicas).astype(F32)
    own_agg = (own_sums * scale[:quarter]).astype(BF16)
    aggs = from_ahead(own_agg, replicas)
    joint_width = feat_width + 2 * share * feat_width // halo_rows
    halo_steps = max(1, halo_rows // 256)
    out_feats, own_base, own_grad_agg, own_weights = call(
        functools.partial(own_kernel, replicas),
        "dense_own",
        [
            shape(quarter, feat_width, BF16),
            shape(quarter, feat_width, F32),
            shape(quarter, feat_width, BF16),
            shape(2 * share, feat_width, F32),
        ],
        [SMEM, VMEM, VMEM, HBM, VMEM, VMEM, VMEM],
        (rep_ref, own_agg, grad_outs[0], node_feats, w_self, w_neigh, scale),
        block_flops // 2,
        out_specs=[VMEM, HBM, VMEM, VMEM],
        scratch=[
            pltpu.VMEM((quarter, feat_width), BF16),
            pltpu.VMEM((quarter, feat_width), F32),
            pltpu.SemaphoreType.DMA((2,)),
        ],
    )
    far_grad_agg, far_weights = call(
        functools.partial(far_kernel, replicas, 2),
        "dense_far",
        [shape(quarter, feat_width, BF16), shape(2 * share, feat_width, F32)],
        [SMEM, VMEM, HBM, HBM, VMEM, VMEM, VMEM, VMEM],
        (rep_ref, aggs[1], grad_outs[2], node_feats, w_self, w_neigh, scale, own_weights),
        block_flops // 2,
        scratch=[pltpu.VMEM((quarter, feat_width), BF16)] * 2 + [pltpu.SemaphoreType.DMA((2,))],
    )
    grad_agg, joint = call(
        functools.partial(dense_kernel, replicas),
        "dense_rest",
        [shape(node_rows, feat_width, BF16), shape(halo_rows, joint_width, BF16)],
        [SMEM] + [VMEM] * 2 + [HBM] * 3 + [VMEM] * 3 + [HBM] + [VMEM] * 3,
        (
            rep_ref, aggs[0], aggs[2], grad_outs[1], grad_outs[3], node_feats, w_self, w_neigh, scale, halo_t,
            own_grad_agg, far_grad_agg, far_weights,
        ),
        2 * block_flops,
        out_specs=[HBM, HBM],
        scratch=[
            pltpu.VMEM((2, quarter, feat_width), BF16),
            pltpu.VMEM((2, quarter, feat_width), BF16),
            pltpu.VMEM((halo_rows, node_rows), BF16),
            pltpu.VMEM((node_rows, feat_width), BF16),
            pltpu.VMEM((halo_rows, joint_width), BF16),
            pltpu.SemaphoreType.DMA((5 + 2 * halo_steps,)),
        ],
    )
    returned = lax.all_to_all(joint, WIDE, 0, 0, tiled=True)
    (local_grad,) = call(
        functools.partial(local_kernel, replicas),
        "local_rows",
        [shape(node_rows, feat_width, F32)],
        [HBM] * 3,
        (local_t, grad_agg, own_base),
        block_flops,
        out_specs=[HBM],
        scratch=[
            pltpu.VMEM((node_rows, node_rows), BF16),
            pltpu.VMEM((node_rows, feat_width), BF16),
            pltpu.VMEM((quarter, feat_width), F32),
            pltpu.VMEM((node_rows, feat_width), F32),
            pltpu.SemaphoreType.DMA((4,)),
        ],
    )

    returned, local_grad = lax.optimization_barrier((returned, local_grad))
    lanes = joint_width - feat_width
    (copies,) = call(
        tile_kernel,
        "weight_tile",
        [shape(halo_rows, lanes, BF16)],
        [VMEM],
        (returned,),
        halo_rows * lanes,
        out_specs=[HBM],
        scratch=[pltpu.VMEM((halo_rows, lanes), BF16), pltpu.SemaphoreType.DMA((1,))],
    )
    own_grad, *sends = call(
        functools.partial(return_kernel, replicas),
        "returned_rows",
        [shape(quarter, feat_width, F32)] + send_outs,
        [SMEM, VMEM, VMEM, HBM],
        (rep_ref, jnp.pad(slots, ((0, 0), (0, -peer_count % LANES))), returned, local_grad),
        block_flops,
        scratch=[pltpu.VMEM((node_rows, feat_width), F32)] * 2
        + [pltpu.SemaphoreType.DMA((replicas,))],
    )
    for k in FAR_FIRST:
        own_grad = own_grad + send_to(sends[k - 1], k, replicas).astype(F32)

    tiles = lax.all_to_all(copies, WIDE, 0, 0, tiled=True)
    lane_tiles = feat_width // LANES
    own_share = (
        tiles.reshape(peer_count, slot_count, -1, LANES)
        .transpose(0, 2, 1, 3)
        .reshape(-1, lane_tiles, slot_count, LANES)
        .transpose(0, 2, 1, 3)
        .reshape(2 * share, feat_width)
    )
    shares = from_ahead(own_share, replicas)
    grad_self, grad_neigh = call(
        place_kernel,
        "place",
        [shape(feat_width, feat_width, BF16)] * 2,
        [SMEM] + [VMEM] * replicas,
        (rep_ref, own_share, shares[0], shares[2], shares[1]),
        0,
    )
    return out_feats, own_grad.astype(BF16), grad_self, grad_neigh


def solution(mesh):
    fine = Mesh(
        mesh.devices.reshape(8, mesh.shape["wide"] // 16, 2, mesh.shape["rep"]), WIDE + ("rep",)
    )
    in_specs = (
        P(WIDE, None),
        P(),
        P(),
        P(WIDE, None, "rep"),
        P(WIDE, "rep", None),
        P(WIDE, "rep", None),
        P(WIDE, "rep", None),
        P(WIDE),
        P(WIDE + ("rep",), None),
    )
    out_specs = (P(WIDE + ("rep",), None), P(WIDE + ("rep",), None), P(), P())
    return jax.shard_map(
        on_device, mesh=fine, in_specs=in_specs, out_specs=out_specs, check_vma=False
    )
```

```python
import functools

import jax
import jax.numpy as jnp
from jax import lax
from jax.experimental import pallas as pl
from jax.experimental.pallas import tpu as pltpu
from jax.sharding import Mesh
from jax.sharding import PartitionSpec as P

BLOCK = 64
LANES = 128
WIDE = ("y", "z", "core")
FAR_FIRST = (2, 1, 3)
F32 = jnp.float32
BF16 = jnp.bfloat16
VMEM = pl.BlockSpec(memory_space=pltpu.VMEM)
HBM = pl.BlockSpec(memory_space=pltpu.HBM)
SMEM = pl.BlockSpec(memory_space=pltpu.SMEM)


def dot(left, right, left_dim, right_dim):
    dims = (((left_dim,), (right_dim,)), ((), ()))
    return lax.dot_general(left, right, dims, preferred_element_type=F32)


def call(kernel, name, outs, in_specs, args, flops, out_specs=None, scratch=(), vmem=24):
    moved = sum(a.size * a.dtype.itemsize for a in args) + sum(
        o.size * o.dtype.itemsize for o in outs
    )
    args = [
        pltpu.with_memory_space_constraint(a, pltpu.HBM) if spec is HBM else a
        for a, spec in zip(args, in_specs, strict=True)
    ]
    out_specs = out_specs or [VMEM] * len(outs)
    outs = [
        pltpu.HBM(o.shape, o.dtype) if spec is HBM else o
        for o, spec in zip(outs, out_specs, strict=True)
    ]
    return pl.pallas_call(
        kernel,
        out_shape=outs,
        in_specs=in_specs,
        out_specs=out_specs,
        scratch_shapes=scratch,
        compiler_params=pltpu.CompilerParams(vmem_limit_bytes=vmem << 20),
        cost_estimate=pl.CostEstimate(flops=flops, bytes_accessed=moved, transcendentals=0),
        name=name,
    )(*args)


def shape(rows, cols, dtype):
    return jax.ShapeDtypeStruct((rows, cols), dtype)


def started(source, target, sem):
    copy = pltpu.make_async_copy(source, target, sem)
    copy.start()
    return copy


def turned_quarters(rep_ref, feats_hbm, feats_ref, sems, replicas):
    quarter = feats_ref.shape[0] // replicas
    copies = []
    for k in range(replicas):
        at = pl.multiple_of(((rep_ref[0] + k) % replicas) * quarter, quarter)
        copies.append(
            started(
                feats_hbm.at[pl.ds(at, quarter), :],
                feats_ref.at[pl.ds(k * quarter, quarter), :],
                sems.at[k],
            )
        )
    return copies


def count_kernel(
    replicas, rep_ref, place_ref, words_ref, feats_hbm, local_t_hbm, halo_ref, halo_t_hbm, sums_hbm,
    counts_ref, turned_ref, feats_ref, sums_ref, sems,
):
    feats_copies = turned_quarters(rep_ref, feats_hbm, feats_ref, sems, replicas)
    counts_ref[...] = jnp.zeros_like(counts_ref)
    row = lax.broadcasted_iota(jnp.int32, (BLOCK, LANES), 0)
    lane = lax.broadcasted_iota(jnp.int32, (BLOCK, LANES), 1)
    word_lane = (row % 32) * 4 + (lane % BLOCK) // 16
    shift = lane % 16
    half = lane // BLOCK

    def add_tile(t, carry):
        place = place_ref[t]
        dst = pl.multiple_of((place // 64) * BLOCK, BLOCK)
        src = place % 64
        upper = jnp.broadcast_to(words_ref[pl.ds(2 * t, 1), :], (32, LANES))
        lower = jnp.broadcast_to(words_ref[pl.ds(2 * t + 1, 1), :], (32, LANES))
        words = jnp.concatenate([upper, lower], axis=0)
        picked = jnp.take_along_axis(words, word_lane, axis=1)
        bits = jnp.right_shift(picked, shift) & 1
        tile = jnp.where(half == src % 2, bits, 0).astype(F32).astype(BF16)
        rows = pl.ds(dst, BLOCK)
        cols = pl.ds(pl.multiple_of((src // 2) * LANES, LANES), LANES)
        counts_ref[rows, cols] = counts_ref[rows, cols] + tile
        return carry

    lax.fori_loop(0, place_ref.shape[0], add_tile, 0, unroll=4)
    split = local_t_hbm.shape[0]
    turned_ref[...] = counts_ref[...].T
    local_copy = started(turned_ref.at[pl.ds(0, split), :], local_t_hbm, sems.at[replicas])
    halo_copy = started(
        turned_ref.at[pl.ds(split, turned_ref.shape[0] - split), :], halo_t_hbm, sems.at[replicas + 1]
    )
    halo_ref[...] = counts_ref[:, split:]
    for copy in feats_copies:
        copy.wait()
    rows_done = 256
    for at in range(0, counts_ref.shape[0], rows_done):
        rows = pl.ds(at, rows_done)
        sums_ref[rows, :] = dot(counts_ref[rows, :split], feats_ref[...], 1, 0)
    sums_copy = started(sums_ref, sums_hbm, sems.at[replicas + 2])
    local_copy.wait()
    halo_copy.wait()
    sums_copy.wait()


def quarter_copies(local_hbm, local_ref, sems, order):
    quarter = local_ref.shape[0] // len(order)
    rows = {k: pl.ds(k * quarter, quarter) for k in order}
    return rows, {
        k: started(local_hbm.at[rows[k], :], local_ref.at[rows[k], :], sems.at[k]) for k in order
    }


def gather_kernel(slots_hbm, feats_hbm, rows_hbm, slots_ref, feats_ref, rows_ref, sems):
    slots_copy = started(slots_hbm, slots_ref, sems.at[0])
    feats_copy = started(feats_hbm, feats_ref, sems.at[1])
    slots_copy.wait()
    slot_count, peers = slots_ref.shape
    node_rows = feats_ref.shape[0]
    lane = lax.broadcasted_iota(jnp.int32, (slot_count, node_rows), 1)
    slots = slots_ref[...]
    step = min(32, peers)
    copies = []
    for at in range(0, peers, step):
        pick = jnp.concatenate(
            [
                jnp.where(lane == slots[:, s : s + 1], 1.0, 0.0).astype(F32)
                for s in range(at, at + step)
            ],
            axis=0,
        ).astype(BF16)
        if at == 0:
            feats_copy.wait()
        rows = pl.ds(at * slot_count, step * slot_count)
        rows_ref[rows, :] = dot(pick, feats_ref[...], 1, 0).astype(BF16)
        copies.append(
            started(rows_ref.at[rows, :], rows_hbm.at[rows, :], sems.at[2 + at // step])
        )
    for copy in copies:
        copy.wait()


def sum_kernel(
    counts_ref, incoming_ref, local_hbm, own_ref, send1, send2, send3, local_ref, total_ref, sems
):
    order = (2, 1, 3, 0)
    quarters, copies = quarter_copies(local_hbm, local_ref, sems, order)
    for rows in quarters.values():
        total_ref[rows, :] = dot(counts_ref[rows, :], incoming_ref[...], 1, 0)
    for k, rows in quarters.items():
        copies[k].wait()
        total = total_ref[rows, :] + local_ref[rows, :]
        if k:
            (send1, send2, send3)[k - 1][...] = total.astype(BF16)
        else:
            own_ref[...] = total


def dense_quarter(agg, feats, grad_out, scale, w_self, w_neigh):
    pre = dot(agg, w_neigh, 1, 0) + dot(feats, w_self, 1, 0)
    sigmoid = jax.nn.sigmoid(pre)
    grad_pre = (grad_out.astype(F32) * sigmoid * (1.0 + pre * (1.0 - sigmoid))).astype(BF16)
    grad_agg = (dot(grad_pre, w_neigh, 1, 1) * scale).astype(BF16)
    return pre * sigmoid, grad_pre, grad_agg


def own_kernel(
    replicas, rep_ref, agg_ref, grad_ref, grad1, grad2, grad3, feats_hbm, w_self_ref, w_neigh_ref, scale_ref,
    out_ref, base_hbm, grad_agg_ref, weights_ref, feats_all_ref, grads_ref, feats_ref, base_ref, sems,
):
    quarter, feat_width = agg_ref.shape
    share = feat_width // replicas
    own_rows = pl.ds(pl.multiple_of(rep_ref[0] * quarter, quarter), quarter)
    feats_copy = started(feats_hbm.at[own_rows, :], feats_ref, sems.at[0])
    ahead = []
    for k, grad in ((2, grad2), (1, grad1), (3, grad3)):
        at = pl.multiple_of(((rep_ref[0] + k) % replicas) * quarter, quarter)
        to = pl.ds((k - 1) * quarter, quarter)
        ahead.append(started(feats_hbm.at[pl.ds(at, quarter), :], feats_all_ref.at[to, :], sems.at[2 * k]))
        ahead.append(started(grad, grads_ref.at[to, :], sems.at[2 * k + 1]))
    feats_copy.wait()
    out, grad_pre, grad_agg = dense_quarter(
        agg_ref[...], feats_ref[...], grad_ref[...], scale_ref[:quarter, :], w_self_ref[...],
        w_neigh_ref[...],
    )
    out_ref[...] = out.astype(BF16)
    grad_agg_ref[...] = grad_agg
    base_ref[...] = dot(grad_pre, w_self_ref[...], 1, 1)
    base_copy = started(base_ref, base_hbm, sems.at[1])
    share_cols = pl.ds(pl.multiple_of(rep_ref[0] * share, LANES), share)
    weights_ref[:share, :] = dot(feats_ref[:, share_cols], grad_pre, 0, 0)
    weights_ref[share:, :] = dot(agg_ref[:, share_cols], grad_pre, 0, 0)
    for copy in ahead:
        copy.wait()
    base_copy.wait()


def far_kernel(
    replicas, step, rep_ref, agg_ref, grads_ref, feats_ref, w_self_ref, w_neigh_ref, scale_ref, before_ref,
    grad_agg_ref, weights_ref,
):
    quarter, feat_width = agg_ref.shape
    share = feat_width // replicas
    at = pl.ds((step - 1) * quarter, quarter)
    _, grad_pre, grad_agg = dense_quarter(
        agg_ref[...], feats_ref[at, :], grads_ref[at, :], scale_ref[pl.ds(step * quarter, quarter), :],
        w_self_ref[...], w_neigh_ref[...],
    )
    grad_agg_ref[...] = grad_agg
    share_cols = pl.ds(pl.multiple_of(rep_ref[0] * share, LANES), share)
    weights_ref[:share, :] = before_ref[:share, :] + dot(feats_ref[at, share_cols], grad_pre, 0, 0)
    weights_ref[share:, :] = before_ref[share:, :] + dot(agg_ref[:, share_cols], grad_pre, 0, 0)


def dense_kernel(
    replicas, rep_ref, agg1, agg3, grads_ref, feats_ref, w_self_ref, w_neigh_ref, scale_ref,
    halo_t_hbm, grad_agg0_ref, grad_agg2_ref, weights_ref, grad_agg_hbm, joint_hbm,
    halo_t_ref, grad_agg_ref, joint_ref, sems,
):
    aggs = {1: agg1, 3: agg3}
    quarter, feat_width = agg1.shape
    share = feat_width // replicas
    halo_rows = halo_t_ref.shape[0]
    step = min(256, halo_rows)
    starts = range(0, halo_rows, step)
    at = 0
    halo_copies = [
        started(halo_t_hbm.at[pl.ds(i, step), :], halo_t_ref.at[pl.ds(i, step), :], sems.at[at + n])
        for n, i in enumerate(starts)
    ]
    at += len(starts)
    share_cols = pl.ds(pl.multiple_of(rep_ref[0] * share, LANES), share)
    grad_self = weights_ref[:share, :]
    grad_neigh = weights_ref[share:, :]
    grad_agg_ref[:quarter, :] = grad_agg0_ref[...]
    grad_agg_ref[pl.ds(2 * quarter, quarter), :] = grad_agg2_ref[...]
    for k, agg_ref in aggs.items():
        rows = pl.ds(k * quarter, quarter)
        past = pl.ds((k - 1) * quarter, quarter)
        _, grad_pre, grad_agg = dense_quarter(
            agg_ref[...], feats_ref[past, :], grads_ref[past, :], scale_ref[rows, :], w_self_ref[...],
            w_neigh_ref[...],
        )
        grad_agg_ref[rows, :] = grad_agg
        grad_self = grad_self + dot(feats_ref[past, share_cols], grad_pre, 0, 0)
        grad_neigh = grad_neigh + dot(agg_ref[:, share_cols], grad_pre, 0, 0)
    grad_agg_copy = started(grad_agg_ref, grad_agg_hbm, sems.at[at])
    tile = 0
    per_peer = (joint_ref.shape[1] - feat_width) // LANES
    for part in (grad_self, grad_neigh):
        for g in range(0, share, 8):
            for c in range(0, feat_width, LANES):
                peer, slot = tile // per_peer, tile % per_peer
                lane = feat_width + slot * LANES
                joint_ref[peer * 8 : peer * 8 + 8, lane : lane + LANES] = part[
                    g : g + 8, c : c + LANES
                ].astype(BF16)
                tile += 1
    joint_copies = []
    for n, i in enumerate(starts):
        rows = pl.ds(i, step)
        halo_copies[n].wait()
        joint_ref[rows, :feat_width] = dot(halo_t_ref[rows, :], grad_agg_ref[...], 1, 0).astype(BF16)
        joint_copies.append(started(joint_ref.at[rows, :], joint_hbm.at[rows, :], sems.at[at + 1 + n]))
    grad_agg_copy.wait()
    for copy in joint_copies:
        copy.wait()


def local_kernel(
    replicas, counts_hbm, grad_hbm, base_hbm, local_hbm, counts_ref, grad_ref, base_ref, local_ref, sems
):
    copies = [
        started(*pair, sems.at[n])
        for n, pair in enumerate(
            ((counts_hbm, counts_ref), (grad_hbm, grad_ref), (base_hbm, base_ref))
        )
    ]
    for copy in copies:
        copy.wait()
    quarter = base_ref.shape[0]
    for k in range(replicas):
        rows = pl.ds(k * quarter, quarter)
        total = dot(counts_ref[rows, :], grad_ref[...], 1, 0)
        local_ref[rows, :] = total if k else total + base_ref[...]
    copy = started(local_ref, local_hbm, sems.at[3])
    copy.wait()


def tile_kernel(joint_ref, copies_hbm, tiles_ref, sems):
    halo_rows, lanes = tiles_ref.shape
    feat_width = joint_ref.shape[1] - lanes
    tiles = joint_ref[:, feat_width:].astype(F32).reshape(halo_rows // 8, 8, lanes)
    tile = tiles.sum(axis=0, keepdims=True)
    tiles_ref[...] = jnp.broadcast_to(tile, tiles.shape).reshape(halo_rows, lanes).astype(BF16)
    copy = started(tiles_ref, copies_hbm, sems.at[0])
    copy.wait()


def return_kernel(
    replicas, rep_ref, slots_ref, joint_ref, local_hbm, own_ref, send1, send2, send3, local_ref,
    total_ref, sems,
):
    quarter, feat_width = own_ref.shape
    halo_rows = joint_ref.shape[0]
    order = (2, 1, 3, 0)
    quarters, copies = quarter_copies(local_hbm, local_ref, sems, order)
    slots = slots_ref[...]
    slot = lax.broadcasted_iota(jnp.int32, slots.shape, 0)
    lane = lax.broadcasted_iota(jnp.int32, slots.shape, 1)
    pieces = []
    for at in range(0, halo_rows, LANES):
        picked = jnp.take_along_axis(slots, at // 8 + lane // 8, axis=1)
        pieces.append(jnp.where(slot == lane % 8, picked, 0).sum(axis=0, keepdims=True))
    turned = jnp.concatenate(pieces, axis=1) - rep_ref[0] * quarter
    turned = jnp.where(turned < 0, turned + quarter * replicas, turned)
    turned = jnp.broadcast_to(turned, (quarter, halo_rows))
    row = lax.broadcasted_iota(jnp.int32, (quarter, halo_rows), 0)
    for k, rows in quarters.items():
        pick = jnp.where(row + k * quarter == turned, 1.0, 0.0).astype(BF16)
        total_ref[rows, :] = dot(pick, joint_ref[:, :feat_width], 1, 0)
    for k, rows in quarters.items():
        copies[k].wait()
        total = total_ref[rows, :] + local_ref[rows, :]
        if k:
            (send1, send2, send3)[k - 1][...] = total.astype(BF16)
        else:
            own_ref[...] = total


def place_kernel(rep_ref, part0, part1, part3, part2, self_ref, neigh_ref):
    parts = (part0, part1, part2, part3)
    share = part0.shape[0] // 2
    for k, part in enumerate(parts):
        at = pl.ds(pl.multiple_of(((rep_ref[0] + k) % len(parts)) * share, share), share)
        self_ref[at, :] = part[:share, :]
        neigh_ref[at, :] = part[share:, :]


def send_to(x, step, replicas):
    return lax.ppermute(x, "rep", [(i, (i + step) % replicas) for i in range(replicas)])


def from_ahead(x, replicas):
    ahead = {k: send_to(x, replicas - k, replicas) for k in reversed(FAR_FIRST)}
    return [ahead[k] for k in range(1, replicas)]


def on_device(
    node_feats, w_self, w_neigh, send_rows, tile_dst, tile_src, tile_bits, norm_count, grad_out
):
    node_rows, feat_width = node_feats.shape
    peer_count = lax.axis_size(WIDE)
    replicas = lax.axis_size("rep")
    slot_count = send_rows.shape[2]
    tile_total = tile_dst.shape[2]
    quarter = node_rows // replicas
    share = feat_width // replicas
    rep_index = lax.axis_index("rep")
    rep_ref = rep_index.reshape(1).astype(jnp.int32)
    dst_count = node_rows // BLOCK
    halo_rows = peer_count * slot_count
    first_row = rep_index * quarter
    first_block = rep_index * (quarter // BLOCK)
    send_outs = [shape(quarter, feat_width, BF16)] * (replicas - 1)

    slots = send_rows[0].T
    (outgoing,) = call(
        gather_kernel,
        "gather_rows",
        [shape(halo_rows, feat_width, BF16)],
        [HBM, HBM],
        (slots, node_feats),
        2 * node_rows * halo_rows * feat_width,
        out_specs=[HBM],
        scratch=[
            pltpu.VMEM((slot_count, peer_count), jnp.int32),
            pltpu.VMEM((node_rows, feat_width), BF16),
            pltpu.VMEM((halo_rows, feat_width), BF16),
            pltpu.SemaphoreType.DMA((2 + max(1, peer_count // 32),)),
        ],
    )
    incoming = lax.all_to_all(outgoing, WIDE, 0, 0, tiled=True)

    scale = lax.rsqrt(norm_count.astype(F32))
    scale = lax.dynamic_slice_in_dim(jnp.concatenate([scale, scale]), first_row, node_rows, 0)
    scale = scale[:, None]
    grad_outs = [grad_out] + from_ahead(grad_out, replicas)
    dst = (tile_dst[0, 0] - first_block) % dst_count
    src = tile_src[0, 0]
    src = jnp.where(src < dst_count, (src - first_block) % dst_count, src)
    block_flops = 2 * node_rows * halo_rows * feat_width
    local_t, counts_halo, halo_t, sums_local = call(
        functools.partial(count_kernel, replicas),
        "tile_counts",
        [
            shape(node_rows, node_rows, BF16),
            shape(node_rows, halo_rows, BF16),
            shape(halo_rows, node_rows, BF16),
            shape(node_rows, feat_width, F32),
        ],
        [SMEM, SMEM, VMEM, HBM],
        (rep_ref, dst * 64 + src, tile_bits.reshape(tile_total * 2, LANES), node_feats),
        tile_total * BLOCK * LANES * 20 + block_flops,
        out_specs=[HBM, VMEM, HBM, HBM],
        scratch=[
            pltpu.VMEM((node_rows, node_rows + halo_rows), BF16),
            pltpu.VMEM((node_rows + halo_rows, node_rows), BF16),
            pltpu.VMEM((node_rows, feat_width), BF16),
            pltpu.VMEM((node_rows, feat_width), F32),
            pltpu.SemaphoreType.DMA((replicas + 3,)),
        ],
    )
    incoming, counts_halo, sums_local, scale, *grad_outs = lax.optimization_barrier(
        (incoming, counts_halo, sums_local, scale, *grad_outs)
    )

    own_sums, *sends = call(
        sum_kernel,
        "neighbour_sums",
        [shape(quarter, feat_width, F32)] + send_outs,
        [VMEM, VMEM, HBM],
        (counts_halo, incoming, sums_local),
        block_flops,
        scratch=[pltpu.VMEM((node_rows, feat_width), F32)] * 2
        + [pltpu.SemaphoreType.DMA((replicas,))],
    )
    for k in FAR_FIRST:
        own_sums = own_sums + send_to(sends[k - 1], k, replicas).astype(F32)
    own_agg = (own_sums * scale[:quarter]).astype(BF16)
    aggs = from_ahead(own_agg, replicas)
    joint_width = feat_width + 2 * share * feat_width // halo_rows
    halo_steps = max(1, halo_rows // 256)
    out_feats, own_base, own_grad_agg, own_weights, feats_ahead, grads_ahead = call(
        functools.partial(own_kernel, replicas),
        "dense_own",
        [
            shape(quarter, feat_width, BF16),
            shape(quarter, feat_width, F32),
            shape(quarter, feat_width, BF16),
            shape(2 * share, feat_width, F32),
            shape(node_rows - quarter, feat_width, BF16),
            shape(node_rows - quarter, feat_width, BF16),
        ],
        [SMEM, VMEM, VMEM, HBM, HBM, HBM, HBM, VMEM, VMEM, VMEM],
        (rep_ref, own_agg, *grad_outs, node_feats, w_self, w_neigh, scale),
        block_flops // 2,
        out_specs=[VMEM, HBM, VMEM, VMEM, VMEM, VMEM],
        scratch=[
            pltpu.VMEM((quarter, feat_width), BF16),
            pltpu.VMEM((quarter, feat_width), F32),
            pltpu.SemaphoreType.DMA((2 * replicas,)),
        ],
    )
    far_grad_agg, far_weights = call(
        functools.partial(far_kernel, replicas, 2),
        "dense_far",
        [shape(quarter, feat_width, BF16), shape(2 * share, feat_width, F32)],
        [SMEM] + [VMEM] * 7,
        (rep_ref, aggs[1], grads_ahead, feats_ahead, w_self, w_neigh, scale, own_weights),
        block_flops // 2,
    )
    grad_agg, joint = call(
        functools.partial(dense_kernel, replicas),
        "dense_rest",
        [shape(node_rows, feat_width, BF16), shape(halo_rows, joint_width, BF16)],
        [SMEM] + [VMEM] * 7 + [HBM] + [VMEM] * 3,
        (
            rep_ref, aggs[0], aggs[2], grads_ahead, feats_ahead, w_self, w_neigh, scale, halo_t,
            own_grad_agg, far_grad_agg, far_weights,
        ),
        2 * block_flops,
        out_specs=[HBM, HBM],
        scratch=[
            pltpu.VMEM((halo_rows, node_rows), BF16),
            pltpu.VMEM((node_rows, feat_width), BF16),
            pltpu.VMEM((halo_rows, joint_width), BF16),
            pltpu.SemaphoreType.DMA((1 + 2 * halo_steps,)),
        ],
    )
    returned = lax.all_to_all(joint, WIDE, 0, 0, tiled=True)
    (local_grad,) = call(
        functools.partial(local_kernel, replicas),
        "local_rows",
        [shape(node_rows, feat_width, F32)],
        [HBM] * 3,
        (local_t, grad_agg, own_base),
        block_flops,
        out_specs=[HBM],
        scratch=[
            pltpu.VMEM((node_rows, node_rows), BF16),
            pltpu.VMEM((node_rows, feat_width), BF16),
            pltpu.VMEM((quarter, feat_width), F32),
            pltpu.VMEM((node_rows, feat_width), F32),
            pltpu.SemaphoreType.DMA((4,)),
        ],
    )

    returned, local_grad = lax.optimization_barrier((returned, local_grad))
    lanes = joint_width - feat_width
    (copies,) = call(
        tile_kernel,
        "weight_tile",
        [shape(halo_rows, lanes, BF16)],
        [VMEM],
        (returned,),
        halo_rows * lanes,
        out_specs=[HBM],
        scratch=[pltpu.VMEM((halo_rows, lanes), BF16), pltpu.SemaphoreType.DMA((1,))],
    )
    own_grad, *sends = call(
        functools.partial(return_kernel, replicas),
        "returned_rows",
        [shape(quarter, feat_width, F32)] + send_outs,
        [SMEM, VMEM, VMEM, HBM],
        (rep_ref, jnp.pad(slots, ((0, 0), (0, -peer_count % LANES))), returned, local_grad),
        block_flops,
        scratch=[pltpu.VMEM((node_rows, feat_width), F32)] * 2
        + [pltpu.SemaphoreType.DMA((replicas,))],
    )
    for k in FAR_FIRST:
        own_grad = own_grad + send_to(sends[k - 1], k, replicas).astype(F32)

    tiles = lax.all_to_all(copies, WIDE, 0, 0, tiled=True)
    lane_tiles = feat_width // LANES
    own_share = (
        tiles.reshape(peer_count, slot_count, -1, LANES)
        .transpose(0, 2, 1, 3)
        .reshape(-1, lane_tiles, slot_count, LANES)
        .transpose(0, 2, 1, 3)
        .reshape(2 * share, feat_width)
    )
    shares = from_ahead(own_share, replicas)
    grad_self, grad_neigh = call(
        place_kernel,
        "place",
        [shape(feat_width, feat_width, BF16)] * 2,
        [SMEM] + [VMEM] * replicas,
        (rep_ref, own_share, shares[0], shares[2], shares[1]),
        0,
    )
    return out_feats, own_grad.astype(BF16), grad_self, grad_neigh


def solution(mesh):
    fine = Mesh(
        mesh.devices.reshape(8, mesh.shape["wide"] // 16, 2, mesh.shape["rep"]), WIDE + ("rep",)
    )
    in_specs = (
        P(WIDE, None),
        P(),
        P(),
        P(WIDE, None, "rep"),
        P(WIDE, "rep", None),
        P(WIDE, "rep", None),
        P(WIDE, "rep", None),
        P(WIDE),
        P(WIDE + ("rep",), None),
    )
    out_specs = (P(WIDE + ("rep",), None), P(WIDE + ("rep",), None), P(), P())
    return jax.shard_map(
        on_device, mesh=fine, in_specs=in_specs, out_specs=out_specs, check_vma=False
    )
```

```python
import functools

import jax
import jax.numpy as jnp
from jax import lax
from jax.experimental import pallas as pl
from jax.experimental.pallas import tpu as pltpu
from jax.sharding import Mesh
from jax.sharding import PartitionSpec as P

BLOCK = 64
LANES = 128
WIDE = ("y", "z", "core")
FAR_FIRST = (2, 1, 3)
F32 = jnp.float32
BF16 = jnp.bfloat16
VMEM = pl.BlockSpec(memory_space=pltpu.VMEM)
HBM = pl.BlockSpec(memory_space=pltpu.HBM)
SMEM = pl.BlockSpec(memory_space=pltpu.SMEM)


def dot(left, right, left_dim, right_dim):
    dims = (((left_dim,), (right_dim,)), ((), ()))
    return lax.dot_general(left, right, dims, preferred_element_type=F32)


def call(kernel, name, outs, in_specs, args, flops, out_specs=None, scratch=(), vmem=24):
    moved = sum(a.size * a.dtype.itemsize for a in args) + sum(
        o.size * o.dtype.itemsize for o in outs
    )
    args = [
        pltpu.with_memory_space_constraint(a, pltpu.HBM) if spec is HBM else a
        for a, spec in zip(args, in_specs, strict=True)
    ]
    out_specs = out_specs or [VMEM] * len(outs)
    outs = [
        pltpu.HBM(o.shape, o.dtype) if spec is HBM else o
        for o, spec in zip(outs, out_specs, strict=True)
    ]
    return pl.pallas_call(
        kernel,
        out_shape=outs,
        in_specs=in_specs,
        out_specs=out_specs,
        scratch_shapes=scratch,
        compiler_params=pltpu.CompilerParams(vmem_limit_bytes=vmem << 20),
        cost_estimate=pl.CostEstimate(flops=flops, bytes_accessed=moved, transcendentals=0),
        name=name,
    )(*args)


def shape(rows, cols, dtype):
    return jax.ShapeDtypeStruct((rows, cols), dtype)


def started(source, target, sem):
    copy = pltpu.make_async_copy(source, target, sem)
    copy.start()
    return copy


def turned_quarters(rep_ref, feats_hbm, feats_ref, sems, replicas):
    quarter = feats_ref.shape[0] // replicas
    copies = []
    for k in range(replicas):
        at = pl.multiple_of(((rep_ref[0] + k) % replicas) * quarter, quarter)
        copies.append(
            started(
                feats_hbm.at[pl.ds(at, quarter), :],
                feats_ref.at[pl.ds(k * quarter, quarter), :],
                sems.at[k],
            )
        )
    return copies


def count_kernel(
    replicas, rep_ref, place_ref, words_ref, feats_hbm, local_t_hbm, halo_ref, halo_t_hbm, sums_hbm,
    counts_ref, turned_ref, feats_ref, sums_ref, sems,
):
    feats_copies = turned_quarters(rep_ref, feats_hbm, feats_ref, sems, replicas)
    counts_ref[...] = jnp.zeros_like(counts_ref)
    row = lax.broadcasted_iota(jnp.int32, (BLOCK, LANES), 0)
    lane = lax.broadcasted_iota(jnp.int32, (BLOCK, LANES), 1)
    word_lane = (row % 32) * 4 + (lane % BLOCK) // 16
    shift = lane % 16
    half = lane // BLOCK

    def add_tile(t, carry):
        place = place_ref[t]
        dst = pl.multiple_of((place // 64) * BLOCK, BLOCK)
        src = place % 64
        upper = jnp.broadcast_to(words_ref[pl.ds(2 * t, 1), :], (32, LANES))
        lower = jnp.broadcast_to(words_ref[pl.ds(2 * t + 1, 1), :], (32, LANES))
        words = jnp.concatenate([upper, lower], axis=0)
        picked = jnp.take_along_axis(words, word_lane, axis=1)
        bits = jnp.right_shift(picked, shift) & 1
        tile = jnp.where(half == src % 2, bits, 0).astype(F32).astype(BF16)
        rows = pl.ds(dst, BLOCK)
        cols = pl.ds(pl.multiple_of((src // 2) * LANES, LANES), LANES)
        counts_ref[rows, cols] = counts_ref[rows, cols] + tile
        return carry

    lax.fori_loop(0, place_ref.shape[0], add_tile, 0, unroll=4)
    split = local_t_hbm.shape[0]
    turned_ref[...] = counts_ref[...].T
    local_copy = started(turned_ref.at[pl.ds(0, split), :], local_t_hbm, sems.at[replicas])
    halo_copy = started(
        turned_ref.at[pl.ds(split, turned_ref.shape[0] - split), :], halo_t_hbm, sems.at[replicas + 1]
    )
    halo_ref[...] = counts_ref[:, split:]
    for copy in feats_copies:
        copy.wait()
    rows_done = 256
    for at in range(0, counts_ref.shape[0], rows_done):
        rows = pl.ds(at, rows_done)
        sums_ref[rows, :] = dot(counts_ref[rows, :split], feats_ref[...], 1, 0)
    sums_copy = started(sums_ref, sums_hbm, sems.at[replicas + 2])
    local_copy.wait()
    halo_copy.wait()
    sums_copy.wait()


def quarter_copies(local_hbm, local_ref, sems, order):
    quarter = local_ref.shape[0] // len(order)
    rows = {k: pl.ds(k * quarter, quarter) for k in order}
    return rows, {
        k: started(local_hbm.at[rows[k], :], local_ref.at[rows[k], :], sems.at[k]) for k in order
    }


def gather_kernel(slots_hbm, feats_hbm, rows_hbm, slots_ref, feats_ref, rows_ref, sems):
    slots_copy = started(slots_hbm, slots_ref, sems.at[0])
    feats_copy = started(feats_hbm, feats_ref, sems.at[1])
    slots_copy.wait()
    slot_count, peers = slots_ref.shape
    node_rows = feats_ref.shape[0]
    lane = lax.broadcasted_iota(jnp.int32, (slot_count, node_rows), 1)
    slots = slots_ref[...]
    step = min(32, peers)
    copies = []
    for at in range(0, peers, step):
        pick = jnp.concatenate(
            [
                jnp.where(lane == slots[:, s : s + 1], 1.0, 0.0).astype(F32)
                for s in range(at, at + step)
            ],
            axis=0,
        ).astype(BF16)
        if at == 0:
            feats_copy.wait()
        rows = pl.ds(at * slot_count, step * slot_count)
        rows_ref[rows, :] = dot(pick, feats_ref[...], 1, 0).astype(BF16)
        copies.append(
            started(rows_ref.at[rows, :], rows_hbm.at[rows, :], sems.at[2 + at // step])
        )
    for copy in copies:
        copy.wait()


def sum_kernel(
    counts_ref, incoming_ref, local_hbm, own_ref, send1, send2, send3, local_ref, total_ref, sems
):
    order = (2, 1, 3, 0)
    quarters, copies = quarter_copies(local_hbm, local_ref, sems, order)
    for rows in quarters.values():
        total_ref[rows, :] = dot(counts_ref[rows, :], incoming_ref[...], 1, 0)
    for k, rows in quarters.items():
        copies[k].wait()
        total = total_ref[rows, :] + local_ref[rows, :]
        if k:
            (send1, send2, send3)[k - 1][...] = total.astype(BF16)
        else:
            own_ref[...] = total


def dense_quarter(agg, feats, grad_out, scale, w_self, w_neigh):
    pre = dot(agg, w_neigh, 1, 0) + dot(feats, w_self, 1, 0)
    sigmoid = jax.nn.sigmoid(pre)
    grad_pre = (grad_out.astype(F32) * sigmoid * (1.0 + pre * (1.0 - sigmoid))).astype(BF16)
    grad_agg = (dot(grad_pre, w_neigh, 1, 1) * scale).astype(BF16)
    return pre * sigmoid, grad_pre, grad_agg


def own_kernel(
    replicas, rep_ref, agg_ref, grad_ref, grad1, grad2, grad3, feats_hbm, w_self_ref, w_neigh_ref, scale_ref,
    halo_t_hbm, out_ref, base_hbm, grad_agg_ref, weights_ref, feats_all_ref, grads_ref, halo_t_ref, feats_ref, base_ref, sems,
):
    quarter, feat_width = agg_ref.shape
    share = feat_width // replicas
    own_rows = pl.ds(pl.multiple_of(rep_ref[0] * quarter, quarter), quarter)
    feats_copy = started(feats_hbm.at[own_rows, :], feats_ref, sems.at[0])
    ahead = []
    for k, grad in ((2, grad2), (1, grad1), (3, grad3)):
        at = pl.multiple_of(((rep_ref[0] + k) % replicas) * quarter, quarter)
        to = pl.ds((k - 1) * quarter, quarter)
        ahead.append(started(feats_hbm.at[pl.ds(at, quarter), :], feats_all_ref.at[to, :], sems.at[2 * k]))
        ahead.append(started(grad, grads_ref.at[to, :], sems.at[2 * k + 1]))
    ahead.append(started(halo_t_hbm, halo_t_ref, sems.at[2 * replicas]))
    feats_copy.wait()
    out, grad_pre, grad_agg = dense_quarter(
        agg_ref[...], feats_ref[...], grad_ref[...], scale_ref[:quarter, :], w_self_ref[...],
        w_neigh_ref[...],
    )
    out_ref[...] = out.astype(BF16)
    grad_agg_ref[...] = grad_agg
    base_ref[...] = dot(grad_pre, w_self_ref[...], 1, 1)
    base_copy = started(base_ref, base_hbm, sems.at[1])
    share_cols = pl.ds(pl.multiple_of(rep_ref[0] * share, LANES), share)
    weights_ref[:share, :] = dot(feats_ref[:, share_cols], grad_pre, 0, 0)
    weights_ref[share:, :] = dot(agg_ref[:, share_cols], grad_pre, 0, 0)
    for copy in ahead:
        copy.wait()
    base_copy.wait()


def far_kernel(
    replicas, step, rep_ref, agg_ref, grads_ref, feats_ref, w_self_ref, w_neigh_ref, scale_ref, before_ref,
    grad_agg_ref, weights_ref,
):
    quarter, feat_width = agg_ref.shape
    share = feat_width // replicas
    at = pl.ds((step - 1) * quarter, quarter)
    _, grad_pre, grad_agg = dense_quarter(
        agg_ref[...], feats_ref[at, :], grads_ref[at, :], scale_ref[pl.ds(step * quarter, quarter), :],
        w_self_ref[...], w_neigh_ref[...],
    )
    grad_agg_ref[...] = grad_agg
    share_cols = pl.ds(pl.multiple_of(rep_ref[0] * share, LANES), share)
    weights_ref[:share, :] = before_ref[:share, :] + dot(feats_ref[at, share_cols], grad_pre, 0, 0)
    weights_ref[share:, :] = before_ref[share:, :] + dot(agg_ref[:, share_cols], grad_pre, 0, 0)


def dense_kernel(
    replicas, rep_ref, agg1, agg3, grads_ref, feats_ref, w_self_ref, w_neigh_ref, scale_ref,
    halo_t_ref, grad_agg0_ref, grad_agg2_ref, weights_ref, grad_agg_hbm, joint_hbm,
    grad_agg_ref, joint_ref, sems,
):
    aggs = {1: agg1, 3: agg3}
    quarter, feat_width = agg1.shape
    share = feat_width // replicas
    halo_rows = halo_t_ref.shape[0]
    step = min(256, halo_rows)
    starts = range(0, halo_rows, step)
    share_cols = pl.ds(pl.multiple_of(rep_ref[0] * share, LANES), share)
    grad_self = weights_ref[:share, :]
    grad_neigh = weights_ref[share:, :]
    grad_agg_ref[:quarter, :] = grad_agg0_ref[...]
    grad_agg_ref[pl.ds(2 * quarter, quarter), :] = grad_agg2_ref[...]
    for k, agg_ref in aggs.items():
        rows = pl.ds(k * quarter, quarter)
        past = pl.ds((k - 1) * quarter, quarter)
        _, grad_pre, grad_agg = dense_quarter(
            agg_ref[...], feats_ref[past, :], grads_ref[past, :], scale_ref[rows, :], w_self_ref[...],
            w_neigh_ref[...],
        )
        grad_agg_ref[rows, :] = grad_agg
        grad_self = grad_self + dot(feats_ref[past, share_cols], grad_pre, 0, 0)
        grad_neigh = grad_neigh + dot(agg_ref[:, share_cols], grad_pre, 0, 0)
    grad_agg_copy = started(grad_agg_ref, grad_agg_hbm, sems.at[0])
    tile = 0
    per_peer = (joint_ref.shape[1] - feat_width) // LANES
    for part in (grad_self, grad_neigh):
        for g in range(0, share, 8):
            for c in range(0, feat_width, LANES):
                peer, slot = tile // per_peer, tile % per_peer
                lane = feat_width + slot * LANES
                joint_ref[peer * 8 : peer * 8 + 8, lane : lane + LANES] = part[
                    g : g + 8, c : c + LANES
                ].astype(BF16)
                tile += 1
    joint_copies = []
    for n, i in enumerate(starts):
        rows = pl.ds(i, step)
        joint_ref[rows, :feat_width] = dot(halo_t_ref[rows, :], grad_agg_ref[...], 1, 0).astype(BF16)
        joint_copies.append(started(joint_ref.at[rows, :], joint_hbm.at[rows, :], sems.at[1 + n]))
    grad_agg_copy.wait()
    for copy in joint_copies:
        copy.wait()


def local_kernel(
    replicas, counts_hbm, grad_hbm, base_hbm, local_hbm, counts_ref, grad_ref, base_ref, local_ref, sems
):
    copies = [
        started(*pair, sems.at[n])
        for n, pair in enumerate(
            ((counts_hbm, counts_ref), (grad_hbm, grad_ref), (base_hbm, base_ref))
        )
    ]
    for copy in copies:
        copy.wait()
    quarter = base_ref.shape[0]
    for k in range(replicas):
        rows = pl.ds(k * quarter, quarter)
        total = dot(counts_ref[rows, :], grad_ref[...], 1, 0)
        local_ref[rows, :] = total if k else total + base_ref[...]
    copy = started(local_ref, local_hbm, sems.at[3])
    copy.wait()


def tile_kernel(joint_ref, copies_hbm, tiles_ref, sems):
    halo_rows, lanes = tiles_ref.shape
    feat_width = joint_ref.shape[1] - lanes
    tiles = joint_ref[:, feat_width:].astype(F32).reshape(halo_rows // 8, 8, lanes)
    tile = tiles.sum(axis=0, keepdims=True)
    tiles_ref[...] = jnp.broadcast_to(tile, tiles.shape).reshape(halo_rows, lanes).astype(BF16)
    copy = started(tiles_ref, copies_hbm, sems.at[0])
    copy.wait()


def return_kernel(
    replicas, rep_ref, slots_ref, joint_ref, local_hbm, own_ref, send1, send2, send3, local_ref,
    total_ref, sems,
):
    quarter, feat_width = own_ref.shape
    halo_rows = joint_ref.shape[0]
    order = (2, 1, 3, 0)
    quarters, copies = quarter_copies(local_hbm, local_ref, sems, order)
    slots = slots_ref[...]
    slot = lax.broadcasted_iota(jnp.int32, slots.shape, 0)
    lane = lax.broadcasted_iota(jnp.int32, slots.shape, 1)
    pieces = []
    for at in range(0, halo_rows, LANES):
        picked = jnp.take_along_axis(slots, at // 8 + lane // 8, axis=1)
        pieces.append(jnp.where(slot == lane % 8, picked, 0).sum(axis=0, keepdims=True))
    turned = jnp.concatenate(pieces, axis=1) - rep_ref[0] * quarter
    turned = jnp.where(turned < 0, turned + quarter * replicas, turned)
    turned = jnp.broadcast_to(turned, (quarter, halo_rows))
    row = lax.broadcasted_iota(jnp.int32, (quarter, halo_rows), 0)
    for k, rows in quarters.items():
        pick = jnp.where(row + k * quarter == turned, 1.0, 0.0).astype(BF16)
        total_ref[rows, :] = dot(pick, joint_ref[:, :feat_width], 1, 0)
    for k, rows in quarters.items():
        copies[k].wait()
        total = total_ref[rows, :] + local_ref[rows, :]
        if k:
            (send1, send2, send3)[k - 1][...] = total.astype(BF16)
        else:
            own_ref[...] = total


def place_kernel(rep_ref, part0, part1, part3, part2, self_ref, neigh_ref):
    parts = (part0, part1, part2, part3)
    share = part0.shape[0] // 2
    for k, part in enumerate(parts):
        at = pl.ds(pl.multiple_of(((rep_ref[0] + k) % len(parts)) * share, share), share)
        self_ref[at, :] = part[:share, :]
        neigh_ref[at, :] = part[share:, :]


def send_to(x, step, replicas):
    return lax.ppermute(x, "rep", [(i, (i + step) % replicas) for i in range(replicas)])


def from_ahead(x, replicas):
    ahead = {k: send_to(x, replicas - k, replicas) for k in reversed(FAR_FIRST)}
    return [ahead[k] for k in range(1, replicas)]


def on_device(
    node_feats, w_self, w_neigh, send_rows, tile_dst, tile_src, tile_bits, norm_count, grad_out
):
    node_rows, feat_width = node_feats.shape
    peer_count = lax.axis_size(WIDE)
    replicas = lax.axis_size("rep")
    slot_count = send_rows.shape[2]
    tile_total = tile_dst.shape[2]
    quarter = node_rows // replicas
    share = feat_width // replicas
    rep_index = lax.axis_index("rep")
    rep_ref = rep_index.reshape(1).astype(jnp.int32)
    dst_count = node_rows // BLOCK
    halo_rows = peer_count * slot_count
    first_row = rep_index * quarter
    first_block = rep_index * (quarter // BLOCK)
    send_outs = [shape(quarter, feat_width, BF16)] * (replicas - 1)

    slots = send_rows[0].T
    (outgoing,) = call(
        gather_kernel,
        "gather_rows",
        [shape(halo_rows, feat_width, BF16)],
        [HBM, HBM],
        (slots, node_feats),
        2 * node_rows * halo_rows * feat_width,
        out_specs=[HBM],
        scratch=[
            pltpu.VMEM((slot_count, peer_count), jnp.int32),
            pltpu.VMEM((node_rows, feat_width), BF16),
            pltpu.VMEM((halo_rows, feat_width), BF16),
            pltpu.SemaphoreType.DMA((2 + max(1, peer_count // 32),)),
        ],
    )
    incoming = lax.all_to_all(outgoing, WIDE, 0, 0, tiled=True)

    scale = lax.rsqrt(norm_count.astype(F32))
    scale = lax.dynamic_slice_in_dim(jnp.concatenate([scale, scale]), first_row, node_rows, 0)
    scale = scale[:, None]
    grad_outs = [grad_out] + from_ahead(grad_out, replicas)
    dst = (tile_dst[0, 0] - first_block) % dst_count
    src = tile_src[0, 0]
    src = jnp.where(src < dst_count, (src - first_block) % dst_count, src)
    block_flops = 2 * node_rows * halo_rows * feat_width
    local_t, counts_halo, halo_t, sums_local = call(
        functools.partial(count_kernel, replicas),
        "tile_counts",
        [
            shape(node_rows, node_rows, BF16),
            shape(node_rows, halo_rows, BF16),
            shape(halo_rows, node_rows, BF16),
            shape(node_rows, feat_width, F32),
        ],
        [SMEM, SMEM, VMEM, HBM],
        (rep_ref, dst * 64 + src, tile_bits.reshape(tile_total * 2, LANES), node_feats),
        tile_total * BLOCK * LANES * 20 + block_flops,
        out_specs=[HBM, VMEM, HBM, HBM],
        scratch=[
            pltpu.VMEM((node_rows, node_rows + halo_rows), BF16),
            pltpu.VMEM((node_rows + halo_rows, node_rows), BF16),
            pltpu.VMEM((node_rows, feat_width), BF16),
            pltpu.VMEM((node_rows, feat_width), F32),
            pltpu.SemaphoreType.DMA((replicas + 3,)),
        ],
    )
    incoming, counts_halo, sums_local, scale, *grad_outs = lax.optimization_barrier(
        (incoming, counts_halo, sums_local, scale, *grad_outs)
    )

    own_sums, *sends = call(
        sum_kernel,
        "neighbour_sums",
        [shape(quarter, feat_width, F32)] + send_outs,
        [VMEM, VMEM, HBM],
        (counts_halo, incoming, sums_local),
        block_flops,
        scratch=[pltpu.VMEM((node_rows, feat_width), F32)] * 2
        + [pltpu.SemaphoreType.DMA((replicas,))],
    )
    for k in FAR_FIRST:
        own_sums = own_sums + send_to(sends[k - 1], k, replicas).astype(F32)
    own_agg = (own_sums * scale[:quarter]).astype(BF16)
    aggs = from_ahead(own_agg, replicas)
    joint_width = feat_width + 2 * share * feat_width // halo_rows
    halo_steps = max(1, halo_rows // 256)
    out_feats, own_base, own_grad_agg, own_weights, feats_ahead, grads_ahead, halo_ahead = call(
        functools.partial(own_kernel, replicas),
        "dense_own",
        [
            shape(quarter, feat_width, BF16),
            shape(quarter, feat_width, F32),
            shape(quarter, feat_width, BF16),
            shape(2 * share, feat_width, F32),
            shape(node_rows - quarter, feat_width, BF16),
            shape(node_rows - quarter, feat_width, BF16),
            shape(halo_rows, node_rows, BF16),
        ],
        [SMEM, VMEM, VMEM, HBM, HBM, HBM, HBM, VMEM, VMEM, VMEM, HBM],
        (rep_ref, own_agg, *grad_outs, node_feats, w_self, w_neigh, scale, halo_t),
        block_flops // 2,
        out_specs=[VMEM, HBM, VMEM, VMEM, VMEM, VMEM, VMEM],
        scratch=[
            pltpu.VMEM((quarter, feat_width), BF16),
            pltpu.VMEM((quarter, feat_width), F32),
            pltpu.SemaphoreType.DMA((2 * replicas + 1,)),
        ],
    )
    far_grad_agg, far_weights = call(
        functools.partial(far_kernel, replicas, 2),
        "dense_far",
        [shape(quarter, feat_width, BF16), shape(2 * share, feat_width, F32)],
        [SMEM] + [VMEM] * 7,
        (rep_ref, aggs[1], grads_ahead, feats_ahead, w_self, w_neigh, scale, own_weights),
        block_flops // 2,
    )
    grad_agg, joint = call(
        functools.partial(dense_kernel, replicas),
        "dense_rest",
        [shape(node_rows, feat_width, BF16), shape(halo_rows, joint_width, BF16)],
        [SMEM] + [VMEM] * 11,
        (
            rep_ref, aggs[0], aggs[2], grads_ahead, feats_ahead, w_self, w_neigh, scale, halo_ahead,
            own_grad_agg, far_grad_agg, far_weights,
        ),
        2 * block_flops,
        out_specs=[HBM, HBM],
        scratch=[
            pltpu.VMEM((node_rows, feat_width), BF16),
            pltpu.VMEM((halo_rows, joint_width), BF16),
            pltpu.SemaphoreType.DMA((1 + halo_steps,)),
        ],
    )
    returned = lax.all_to_all(joint, WIDE, 0, 0, tiled=True)
    (local_grad,) = call(
        functools.partial(local_kernel, replicas),
        "local_rows",
        [shape(node_rows, feat_width, F32)],
        [HBM] * 3,
        (local_t, grad_agg, own_base),
        block_flops,
        out_specs=[HBM],
        scratch=[
            pltpu.VMEM((node_rows, node_rows), BF16),
            pltpu.VMEM((node_rows, feat_width), BF16),
            pltpu.VMEM((quarter, feat_width), F32),
            pltpu.VMEM((node_rows, feat_width), F32),
            pltpu.SemaphoreType.DMA((4,)),
        ],
    )

    returned, local_grad = lax.optimization_barrier((returned, local_grad))
    lanes = joint_width - feat_width
    (copies,) = call(
        tile_kernel,
        "weight_tile",
        [shape(halo_rows, lanes, BF16)],
        [VMEM],
        (returned,),
        halo_rows * lanes,
        out_specs=[HBM],
        scratch=[pltpu.VMEM((halo_rows, lanes), BF16), pltpu.SemaphoreType.DMA((1,))],
    )
    own_grad, *sends = call(
        functools.partial(return_kernel, replicas),
        "returned_rows",
        [shape(quarter, feat_width, F32)] + send_outs,
        [SMEM, VMEM, VMEM, HBM],
        (rep_ref, jnp.pad(slots, ((0, 0), (0, -peer_count % LANES))), returned, local_grad),
        block_flops,
        scratch=[pltpu.VMEM((node_rows, feat_width), F32)] * 2
        + [pltpu.SemaphoreType.DMA((replicas,))],
    )
    for k in FAR_FIRST:
        own_grad = own_grad + send_to(sends[k - 1], k, replicas).astype(F32)

    tiles = lax.all_to_all(copies, WIDE, 0, 0, tiled=True)
    lane_tiles = feat_width // LANES
    own_share = (
        tiles.reshape(peer_count, slot_count, -1, LANES)
        .transpose(0, 2, 1, 3)
        .reshape(-1, lane_tiles, slot_count, LANES)
        .transpose(0, 2, 1, 3)
        .reshape(2 * share, feat_width)
    )
    shares = from_ahead(own_share, replicas)
    grad_self, grad_neigh = call(
        place_kernel,
        "place",
        [shape(feat_width, feat_width, BF16)] * 2,
        [SMEM] + [VMEM] * replicas,
        (rep_ref, own_share, shares[0], shares[2], shares[1]),
        0,
    )
    return out_feats, own_grad.astype(BF16), grad_self, grad_neigh


def solution(mesh):
    fine = Mesh(
        mesh.devices.reshape(8, mesh.shape["wide"] // 16, 2, mesh.shape["rep"]), WIDE + ("rep",)
    )
    in_specs = (
        P(WIDE, None),
        P(),
        P(),
        P(WIDE, None, "rep"),
        P(WIDE, "rep", None),
        P(WIDE, "rep", None),
        P(WIDE, "rep", None),
        P(WIDE),
        P(WIDE + ("rep",), None),
    )
    out_specs = (P(WIDE + ("rep",), None), P(WIDE + ("rep",), None), P(), P())
    return jax.shard_map(
        on_device, mesh=fine, in_specs=in_specs, out_specs=out_specs, check_vma=False
    )
```
